128 devices in a mesh: grp: 32 (over z, y, core), tp: 4 (over x).
Axes of the slice: x: 4, y: 4, z: 4, core: 2. Of those that a mesh axis runs over, the one named last changes fastest.
Arguments:
- tokens: bfloat16 [8192, 2048], P('grp', 'tp'), may hold values from -6 to 6
- attn_gain: float32 [2048], replicated, may hold values from 0.6 to 6
- w_query: bfloat16 [2048, 2048], P(None, 'tp'), may hold values from -0.125 to 0.125
- w_key: bfloat16 [2048, 512], P(None, 'tp'), may hold values from -0.125 to 0.125
- w_value: bfloat16 [2048, 512], P(None, 'tp'), may hold values from -0.125 to 0.125
- w_out: bfloat16 [2048, 2048], P('tp'), may hold values from -0.125 to 0.125
- mlp_gain: float32 [2048], replicated, may hold values from 0.1 to 1.9
- w_gate: bfloat16 [2048, 4096], P('grp', 'tp'), may hold values from -0.125 to 0.125
- w_up: bfloat16 [2048, 4096], P('grp', 'tp'), may hold values from -0.125 to 0.125
- w_down: bfloat16 [4096, 2048], P('tp', 'grp'), may hold values from -0.09375 to 0.09375
- k_cache: bfloat16 [32, 16384, 512], P(None, 'grp', 'tp'), may hold values from -72 to 72
- v_cache: bfloat16 [32, 16384, 512], P(None, 'grp', 'tp'), may hold values from -6 to 6
- prefix_len: int32 [32], replicated, may hold values from 0 to 16128, as said below
Outputs:
- result: float32 [8192, 2048], P('grp', 'tp')
- k_cache_out: bfloat16 [32, 16384, 512], P(None, 'grp', 'tp')
- v_cache_out: bfloat16 [32, 16384, 512], P(None, 'grp', 'tp')
The draws below stay inside these ranges and needn't reach their ends.
Inputs may be any that keep to these rules, and one draw needn't show every extreme that they name: `prefix_len`: some request has none cached and some has 16128.
All inputs are finite; a program needn't handle non-finite values.
Results may differ from the reference program's by a relative error of at most 0.04.
Values may be sent and summed in bfloat16 or wider, within the bound.
A program may use at most 448 MiB of HBM per device.

```python
import jax
import jax.numpy as jnp
from jax import lax

D = 2048
HEADS = 32
KVH = 8
HD = 64
FF = 4096
NEW_TOK = 256
CTX = 16384
REQ = 32
TOKENS = 8192
N_GRP = 32


def draw_attn_gain(key, part):
    return jax.random.uniform(jax.random.fold_in(key, 12), (D,), jnp.float32, 0.6, 1.4)


def draw_k_cache(key, part):
    base = jnp.clip(jax.random.normal(jax.random.fold_in(key, 21), (REQ, CTX, KVH * HD), jnp.float32), -6.0, 6.0)
    return base.astype(jnp.bfloat16)


def draw_prefix_len(key, part):
    lengths = jax.random.randint(jax.random.fold_in(key, 31), (REQ,), 0, CTX - NEW_TOK + 1, dtype=jnp.int32)
    order = jax.random.permutation(jax.random.fold_in(key, 32), REQ)
    lengths = lengths.at[order[0]].set(CTX - NEW_TOK)
    lengths = lengths.at[order[1]].set(0)
    return lengths


def block_levels(stream_key, shape, split, low, high):
    factor_of = 1.0
    for dim, blocks in split:
        steps = jax.random.uniform(jax.random.fold_in(jax.random.fold_in(stream_key, 6), dim), (blocks,), jnp.float32, low / len(split), high / len(split))
        factor_of = factor_of * jnp.repeat(jnp.exp(steps), shape[dim] // blocks).reshape((-1,) + (1,) * (len(shape) - 1 - dim))
    return factor_of


def gaussian(stream_key, extent, spread, most, split=(), kind=jnp.bfloat16):
    array = spread * jax.random.normal(stream_key, extent, jnp.float32)
    if split:
        array = array * block_levels(stream_key, extent, split, -0.22, 0.18)
    return jnp.clip(array, -most, most).astype(kind)


def setup_inputs(seed: int = 0) -> dict:
    seeds = jax.random.split(jax.random.key(seed), 14)
    tokens = gaussian(seeds[0], (TOKENS, D), 1.0, 6.0, ((0, 32), (1, 4)))
    attn_gain = draw_attn_gain(jax.random.fold_in(seeds[13], 71), 0)
    w_query = gaussian(seeds[2], (D, HEADS * HD), D ** -0.5, 0.125, ((1, 4),))
    w_key = gaussian(seeds[3], (D, KVH * HD), D ** -0.5, 0.125, ((1, 4),))
    w_value = gaussian(seeds[4], (D, KVH * HD), D ** -0.5, 0.125, ((1, 4),))
    w_out = gaussian(seeds[5], (HEADS * HD, D), (HEADS * HD) ** -0.5, 0.125, ((0, 4),))
    mlp_gain = jnp.clip(1.0 + 0.18 * jax.random.normal(seeds[6], (D,), jnp.float32), 0.1, 1.9)
    w_gate = gaussian(seeds[7], (D, FF), D ** -0.5, 0.125, ((0, 32), (1, 4)))
    w_up = gaussian(seeds[8], (D, FF), D ** -0.5, 0.125, ((0, 32), (1, 4)))
    w_down = gaussian(seeds[9], (FF, D), FF ** -0.5, 0.09375, ((0, 4), (1, 32)))
    k_cache = draw_k_cache(jax.random.fold_in(seeds[13], 71), 0)
    v_cache = gaussian(seeds[11], (REQ, CTX, KVH * HD), 1.0, 6.0, ((1, 32), (2, 4)))
    prefix_len = draw_prefix_len(jax.random.fold_in(seeds[13], 71), 0)
    return dict(tokens=tokens, attn_gain=attn_gain, w_query=w_query, w_key=w_key, w_value=w_value, w_out=w_out, mlp_gain=mlp_gain, w_gate=w_gate, w_up=w_up, w_down=w_down, k_cache=k_cache, v_cache=v_cache, prefix_len=prefix_len)


eps_norm = 1e-05
rope_base = 500000.0
neg_fill = -1e+30

def rms_scale(rows, gain):
    rows = rows.astype(jnp.float32)
    return rows * lax.rsqrt(lax.optimization_barrier(jnp.mean(rows * rows, axis=-1, keepdims=True)) + eps_norm) * gain.astype(jnp.float32)

def rotate(heads, positions):
    width = heads.shape[-1]
    half = width // 2
    inverse = rope_base ** (-2.0 * jnp.arange(half, dtype=jnp.float32) / width)
    angles = positions.astype(jnp.float32)[:, None] * inverse[None, :]
    cosine = jnp.cos(angles)[:, None, :]
    sine = jnp.sin(angles)[:, None, :]
    first = heads[..., :half]
    second = heads[..., half:]
    return jnp.concatenate([first * cosine - second * sine, second * cosine + first * sine], axis=-1)

def shard_partial(query, keys, values, start, plen):
    scores = jnp.einsum('tkgd,skd->kgts', query.astype(jnp.float32), keys.astype(jnp.float32)) * 0.125
    live = start + jnp.arange(keys.shape[0], dtype=jnp.int32) < plen
    masked = jnp.where(live, scores, neg_fill)
    top = lax.optimization_barrier(jnp.max(masked, axis=-1))
    expo = jnp.where(live, jnp.exp(masked - top[..., None]), 0.0)
    total = lax.optimization_barrier(jnp.sum(expo, axis=-1))
    weights = expo.astype(jnp.bfloat16)
    summed = jnp.einsum('kgts,skd->tkgd', weights.astype(jnp.float32), values.astype(jnp.float32))
    total_t = jnp.transpose(total, (2, 0, 1))
    scaled = summed / jnp.maximum(total_t, 1.0)[..., None]
    return (scaled.astype(jnp.bfloat16), jnp.transpose(top, (2, 0, 1)), total_t)

def fresh_partial(query, keys, values):
    scores = jnp.einsum('tkgd,ukd->kgtu', query.astype(jnp.float32), keys.astype(jnp.float32)) * 0.125
    count = keys.shape[0]
    causal = jnp.arange(count, dtype=jnp.int32)[:, None] >= jnp.arange(count, dtype=jnp.int32)[None, :]
    masked = jnp.where(causal, scores, neg_fill)
    top = lax.optimization_barrier(jnp.max(masked, axis=-1))
    expo = jnp.where(causal, jnp.exp(masked - top[..., None]), 0.0)
    total = lax.optimization_barrier(jnp.sum(expo, axis=-1))
    weights = expo.astype(jnp.bfloat16)
    summed = jnp.einsum('kgtu,ukd->tkgd', weights.astype(jnp.float32), values.astype(jnp.float32))
    total_t = jnp.transpose(total, (2, 0, 1))
    return (summed / total_t[..., None], jnp.transpose(top, (2, 0, 1)), total_t)

def merge_parts(own_out, own_top, own_total, shard_out, shard_top, shard_total):
    peak = jnp.maximum(own_top, lax.optimization_barrier(jnp.max(shard_top, axis=0)))
    own_weight = jnp.exp(own_top - peak) * own_total
    shard_weight = jnp.exp(shard_top - peak[None]) * shard_total
    numer = own_weight[..., None] * own_out + lax.optimization_barrier(jnp.sum(shard_weight[..., None] * shard_out.astype(jnp.float32), axis=0))
    return numer / (own_weight + lax.optimization_barrier(jnp.sum(shard_weight, axis=0)))[..., None]

def request_attention(items):
    query, key_new, value_new, key_old, value_old, plen = items
    groups = HEADS // KVH
    query = query.reshape(NEW_TOK, KVH, groups, HD)
    key_new = key_new.reshape(NEW_TOK, KVH, HD)
    value_new = value_new.reshape(NEW_TOK, KVH, HD)
    span = CTX // N_GRP
    key_old = key_old.reshape(N_GRP, span, KVH, HD)
    value_old = value_old.reshape(N_GRP, span, KVH, HD)
    starts = jnp.arange(N_GRP, dtype=jnp.int32) * span
    shard_out, shard_top, shard_total = jax.vmap(shard_partial, in_axes=(None, 0, 0, 0, None))(query, key_old, value_old, starts, plen)
    own_out, own_top, own_total = fresh_partial(query, key_new, value_new)
    merged = merge_parts(own_out, own_top, own_total, shard_out, shard_top, shard_total)
    return merged.reshape(NEW_TOK, HEADS * HD).astype(jnp.bfloat16)

def append_rows(cache, rows, plen):
    return lax.dynamic_update_slice_in_dim(cache, rows, plen, 0)

def reference(tokens, attn_gain, w_query, w_key, w_value, w_out, mlp_gain, w_gate, w_up, w_down, k_cache, v_cache, prefix_len):
    normed = rms_scale(tokens, attn_gain).astype(jnp.bfloat16)
    positions = prefix_len[:, None] + jnp.arange(NEW_TOK, dtype=jnp.int32)[None, :]
    query = jnp.dot(normed, w_query, preferred_element_type=jnp.float32).reshape(REQ, NEW_TOK, HEADS, HD)
    query = jax.vmap(rotate)(query, positions).astype(jnp.bfloat16)
    key_new = jnp.dot(normed, w_key, preferred_element_type=jnp.float32).reshape(REQ, NEW_TOK, KVH, HD)
    key_new = jax.vmap(rotate)(key_new, positions).astype(jnp.bfloat16).reshape(REQ, NEW_TOK, KVH * HD)
    value_new = jnp.dot(normed, w_value, preferred_element_type=jnp.float32).astype(jnp.bfloat16).reshape(REQ, NEW_TOK, KVH * HD)
    attended = lax.map(request_attention, (query.reshape(REQ, NEW_TOK, HEADS * HD), key_new, value_new, k_cache, v_cache, prefix_len))
    attended = attended.reshape(TOKENS, HEADS * HD)
    first = (tokens.astype(jnp.float32) + jnp.dot(attended, w_out, preferred_element_type=jnp.float32)).astype(jnp.bfloat16)
    normed_two = rms_scale(first, mlp_gain).astype(jnp.bfloat16)
    gate = jnp.dot(normed_two, w_gate, preferred_element_type=jnp.float32)
    upward = jnp.dot(normed_two, w_up, preferred_element_type=jnp.float32)
    hidden = (jax.nn.silu(gate) * upward).astype(jnp.bfloat16)
    result = first.astype(jnp.float32) + jnp.dot(hidden, w_down, preferred_element_type=jnp.float32)
    k_cache_out = jax.vmap(append_rows)(k_cache, key_new, prefix_len)
    v_cache_out = jax.vmap(append_rows)(v_cache, value_new, prefix_len)
    return (result, k_cache_out, v_cache_out)
```

```python
import math

import jax
import jax.numpy as jnp
from jax import lax
from jax.experimental import pallas as pl
from jax.experimental.pallas import tpu as pltpu
from jax.sharding import PartitionSpec as P

HD = 64
NEW_TOK = 256
EPS = 1e-05
ROPE_BASE = 500000.0
NEG = -1e30
LOG2E = math.log2(math.e)


def rms_scale(rows, gain):
    rows = rows.astype(jnp.float32)
    return rows * lax.rsqrt(jnp.mean(rows * rows, axis=-1, keepdims=True) + EPS) * gain


def attend_columns(keys, qbd, vta, mask, o_store, ml_ref, kv, chunk, width):
    lanes = pl.ds(kv * 1024 + chunk * width, width)
    s = jnp.dot(keys, qbd[:, lanes], preferred_element_type=jnp.float32)
    if mask is not None:
        s = jnp.where(mask, s, NEG)
    top = jnp.max(s, axis=0, keepdims=True)
    p = jnp.exp2((s - top) * LOG2E).astype(jnp.bfloat16)
    o = jnp.dot(vta[kv], p, preferred_element_type=jnp.float32)
    out_lanes = pl.ds(chunk * width, width)
    o_store(kv, out_lanes, o[:HD])
    ml_ref[0, kv : kv + 1, out_lanes] = top
    ml_ref[0, 2 + kv : 3 + kv, out_lanes] = o[HD : HD + 1]


def fill_scratch(q, v, qbd, vta):
    zero = jnp.zeros((HD, 1024), jnp.bfloat16)
    qbd[0:HD, 0:1024] = q[0:HD]
    qbd[HD : 2 * HD, 0:1024] = zero
    qbd[0:HD, 1024:2048] = zero
    qbd[HD : 2 * HD, 1024:2048] = q[HD : 2 * HD]
    vt = jnp.transpose(v.astype(jnp.float32)).astype(jnp.bfloat16)
    ones = jnp.ones((16, v.shape[0]), jnp.bfloat16)
    for kv in range(2):
        vta[kv, 0:HD] = vt[kv * HD : (kv + 1) * HD]
        vta[kv, HD : HD + 16] = ones


def shard_kernel(
    start_ref, plen_ref, q_ref, k_ref, v_ref, nk_ref, nv_ref, o_ref, ml_ref, ko_ref, vo_ref, qbd, vta
):
    r = pl.program_id(0)
    off = plen_ref[r] - start_ref[0]
    span = k_ref.shape[1]
    hit = (off > -NEW_TOK) & (off < span)

    @pl.when(hit)
    def _():
        rows = lax.broadcasted_iota(jnp.int32, (span, NEW_TOK), 0)
        cols = lax.broadcasted_iota(jnp.int32, (span, NEW_TOK), 1)
        pick = (rows - off == cols).astype(jnp.float32).astype(jnp.bfloat16)
        rel = lax.broadcasted_iota(jnp.int32, (span, 128), 0) - off
        inside = (rel >= 0) & (rel < NEW_TOK)
        for new, old, out in ((nk_ref, k_ref, ko_ref), (nv_ref, v_ref, vo_ref)):
            placed = jnp.dot(pick, new[0], preferred_element_type=jnp.float32)
            out[0] = jnp.where(inside, placed, old[0].astype(jnp.float32)).astype(jnp.bfloat16)

    @pl.when(jnp.logical_not(hit))
    def _():
        ko_ref[0] = k_ref[0]
        vo_ref[0] = v_ref[0]

    def store(kv, lanes, o):
        o_ref[0, pl.ds(kv * HD, HD), lanes] = o.astype(jnp.bfloat16)

    def run(masked):
        fill_scratch(q_ref[0], v_ref[0], qbd, vta)
        mask = None
        if masked:
            mask = lax.broadcasted_iota(jnp.int32, (span, 256), 0) < off
        for kv in range(2):
            for chunk in range(4):
                attend_columns(k_ref[0], qbd, vta, mask, store, ml_ref, kv, chunk, 256)

    @pl.when(off >= span)
    def _():
        run(False)

    @pl.when((off > 0) & (off < span))
    def _():
        run(True)

    @pl.when(off <= 0)
    def _():
        o_ref[0] = jnp.zeros((2 * HD, 1024), jnp.bfloat16)
        ml_ref[0, 0:2] = jnp.full((2, 1024), NEG, jnp.float32)
        ml_ref[0, 2:4] = jnp.zeros((2, 1024), jnp.float32)


def shard_attention(start, prefix_len, all_q, k_cache, v_cache, all_k, all_v):
    reqs, span, width = k_cache.shape
    row = lambda r, *_: (r, 0, 0)
    spec = lambda *shape: pl.BlockSpec((1,) + shape, row)
    flops = reqs * 2048 * span * HD * 4
    return pl.pallas_call(
        shard_kernel,
        out_shape=(
            jax.ShapeDtypeStruct((reqs, 128, 1024), jnp.bfloat16),
            jax.ShapeDtypeStruct((reqs, 8, 1024), jnp.float32),
            jax.ShapeDtypeStruct(k_cache.shape, k_cache.dtype),
            jax.ShapeDtypeStruct(v_cache.shape, v_cache.dtype),
        ),
        grid_spec=pltpu.PrefetchScalarGridSpec(
            num_scalar_prefetch=2,
            grid=(reqs,),
            in_specs=[
                spec(128, 1024),
                spec(span, width),
                spec(span, width),
                spec(NEW_TOK, width),
                spec(NEW_TOK, width),
            ],
            out_specs=[spec(128, 1024), spec(8, 1024), spec(span, width), spec(span, width)],
            scratch_shapes=[
                pltpu.VMEM((128, 2048), jnp.bfloat16),
                pltpu.VMEM((2, HD + 16, span), jnp.bfloat16),
            ],
        ),
        compiler_params=pltpu.CompilerParams(
            dimension_semantics=("arbitrary",), vmem_limit_bytes=40 << 20
        ),
        cost_estimate=pl.CostEstimate(
            flops=flops * 3, bytes_accessed=40 << 20, transcendentals=reqs * 2048 * span
        ),
    )(start, prefix_len, all_q, k_cache, v_cache, all_k, all_v)


def own_kernel(q_ref, k_ref, v_ref, o_ref, ml_ref, qbd, vta):
    fill_scratch(q_ref[...], v_ref[...], qbd, vta)
    mask = lax.broadcasted_iota(jnp.int32, (NEW_TOK, NEW_TOK), 0) <= lax.broadcasted_iota(
        jnp.int32, (NEW_TOK, NEW_TOK), 1
    )

    def store(kv, lanes, o):
        o_ref[pl.ds(kv * HD, HD), lanes] = o

    for kv in range(2):
        for chunk in range(4):
            attend_columns(k_ref[...], qbd, vta, mask, store, ml_ref, kv, chunk, 256)


def own_attention(q, k, v):
    return pl.pallas_call(
        own_kernel,
        out_shape=(
            jax.ShapeDtypeStruct((128, 1024), jnp.float32),
            jax.ShapeDtypeStruct((1, 8, 1024), jnp.float32),
        ),
        scratch_shapes=[
            pltpu.VMEM((128, 2048), jnp.bfloat16),
            pltpu.VMEM((2, HD + 16, NEW_TOK), jnp.bfloat16),
        ],
        compiler_params=pltpu.CompilerParams(vmem_limit_bytes=24 << 20),
        cost_estimate=pl.CostEstimate(flops=1 << 28, bytes_accessed=2 << 20, transcendentals=1 << 19),
    )(q, k, v)


def shards(
    tokens,
    attn_gain,
    w_query,
    w_key,
    w_value,
    w_out,
    mlp_gain,
    w_gate,
    w_up,
    w_down,
    k_cache,
    v_cache,
    prefix_len,
):
    groups = lax.axis_size("grp")
    group = lax.axis_index("grp")
    slice_len = k_cache.shape[1]
    start = group * slice_len
    weights = lax.all_gather(
        jnp.concatenate([w_gate, w_up, w_down.T], axis=0), "grp", axis=0, tiled=False
    )
    whole = lax.all_gather(tokens, "tp", axis=1, tiled=True)
    normed = rms_scale(whole, attn_gain).astype(jnp.bfloat16)
    own_len = lax.dynamic_slice_in_dim(prefix_len, group, 1)[0]
    positions = (own_len + jnp.arange(NEW_TOK, dtype=jnp.int32)).astype(jnp.float32)
    inverse = ROPE_BASE ** (-2.0 * jnp.arange(HD // 2, dtype=jnp.float32) / HD)
    angles = positions[None, :] * inverse[:, None]
    cosine, sine = jnp.cos(angles), jnp.sin(angles)
    q = lax.dot_general(
        w_query, normed, (((0,), (1,)), ((), ())), preferred_element_type=jnp.float32
    ).reshape(2, 4, 2, 32, NEW_TOK)
    first, second = q[:, :, 0], q[:, :, 1]
    q = jnp.stack(
        [first * cosine - second * sine, second * cosine + first * sine], axis=2
    ).reshape(2, 4, HD, NEW_TOK)
    q = q.astype(jnp.bfloat16) * jnp.bfloat16(0.125)
    q = jnp.transpose(q, (0, 2, 1, 3)).reshape(128, 1024)
    k = jnp.dot(normed, w_key, preferred_element_type=jnp.float32).reshape(NEW_TOK, 2, 2, 32)
    kc, ks = cosine.T[:, None, :], sine.T[:, None, :]
    first, second = k[:, :, 0], k[:, :, 1]
    k = (
        jnp.stack([first * kc - second * ks, second * kc + first * ks], axis=2)
        .reshape(NEW_TOK, 128)
        .astype(jnp.bfloat16)
    )
    v = jnp.dot(normed, w_value, preferred_element_type=jnp.float32).astype(jnp.bfloat16)
    all_q = lax.all_gather(q, "grp", axis=0)
    all_k = lax.all_gather(k, "grp", axis=0)
    all_v = lax.all_gather(v, "grp", axis=0)
    part_o, part_ml, k_next, v_next = shard_attention(
        start[None], prefix_len, all_q, k_cache, v_cache, all_k, all_v
    )
    own_o, own_ml = own_attention(q, k, v)
    back_o = lax.all_to_all(part_o, "grp", split_axis=0, concat_axis=0, tiled=True)
    back_ml = lax.all_to_all(part_ml[:, :4], "grp", split_axis=0, concat_axis=0, tiled=True)
    tops, totals = back_ml[:, 0:2], back_ml[:, 2:4]
    peak = jnp.maximum(own_ml[0, 0:2], jnp.max(tops, axis=0))
    own_w = jnp.exp(own_ml[0, 0:2] - peak)
    shard_w = jnp.exp(tops - peak[None])
    numer = own_w[:, None, :] * own_o.reshape(2, HD, 1024) + jnp.sum(
        shard_w[:, :, None, :] * back_o.reshape(groups, 2, HD, 1024).astype(jnp.float32), axis=0
    )
    denom = own_w * own_ml[0, 2:4] + jnp.sum(shard_w * totals, axis=0)
    attended = (numer / denom[:, None, :]).astype(jnp.bfloat16)
    attended = (
        attended.reshape(2, HD, 4, NEW_TOK).transpose(3, 0, 2, 1).reshape(NEW_TOK, 512)
    )
    attn_terms = jnp.dot(attended, w_out, preferred_element_type=jnp.float32)
    mixed = lax.psum_scatter(attn_terms, "tp", scatter_dimension=1, tiled=True)
    first = (tokens.astype(jnp.float32) + mixed).astype(jnp.bfloat16)
    first_whole = lax.all_gather(first, "tp", axis=1, tiled=True)
    normed_two = rms_scale(first_whole, mlp_gain).astype(jnp.bfloat16)
    w_g = weights[:, 0:64].reshape(2048, -1)
    w_u = weights[:, 64:128].reshape(2048, -1)
    w_d = weights[:, 128:192].reshape(2048, -1)
    gate = jnp.dot(normed_two, w_g, preferred_element_type=jnp.float32)
    upward = jnp.dot(normed_two, w_u, preferred_element_type=jnp.float32)
    hidden = (jax.nn.silu(gate) * upward).astype(jnp.bfloat16)
    down_terms = lax.dot_general(
        hidden, w_d, (((1,), (1,)), ((), ())), preferred_element_type=jnp.float32
    )
    down = lax.psum_scatter(down_terms, "tp", scatter_dimension=1, tiled=True)
    result = first.astype(jnp.float32) + down
    return (result, k_next, v_next)


def solution(mesh):
    placed = (
        P("grp", "tp"),
        P(),
        P(None, "tp"),
        P(None, "tp"),
        P(None, "tp"),
        P("tp", None),
        P(),
        P("grp", "tp"),
        P("grp", "tp"),
        P("tp", "grp"),
        P(None, "grp", "tp"),
        P(None, "grp", "tp"),
        P(),
    )
    return jax.shard_map(
        shards,
        mesh=mesh,
        in_specs=placed,
        out_specs=(P("grp", "tp"), P(None, "grp", "tp"), P(None, "grp", "tp")),
        check_vma=False,
    )
```

```python
import math

import jax
import jax.numpy as jnp
from jax import lax
from jax.experimental import pallas as pl
from jax.experimental.pallas import tpu as pltpu
from jax.sharding import PartitionSpec as P

HD = 64
NEW_TOK = 256
EPS = 1e-05
ROPE_BASE = 500000.0
NEG = -1e30
LOG2E = math.log2(math.e)


def rms_scale(rows, gain):
    rows = rows.astype(jnp.float32)
    return rows * lax.rsqrt(jnp.mean(rows * rows, axis=-1, keepdims=True) + EPS) * gain


def attend_columns(keys, qbd, vta, mask, o_store, ml_ref, kv, chunk, width):
    lanes = pl.ds(kv * 1024 + chunk * width, width)
    s = jnp.dot(keys, qbd[:, lanes], preferred_element_type=jnp.float32)
    if mask is not None:
        s = jnp.where(mask, s, NEG)
    top = jnp.max(s, axis=0, keepdims=True)
    p = jnp.exp2((s - top) * LOG2E).astype(jnp.bfloat16)
    o = jnp.dot(vta[kv], p, preferred_element_type=jnp.float32)
    o_store(kv, pl.ds(chunk * width, width), o[:HD])
    ml_ref[kv, chunk : chunk + 1] = top
    ml_ref[kv, 4 + chunk : 5 + chunk] = o[HD : HD + 1]


def fill_scratch(q, vt, qbd, vta):
    zero = jnp.zeros((HD, 1024), jnp.bfloat16)
    qbd[0:HD, 0:1024] = q[0:HD]
    qbd[HD : 2 * HD, 0:1024] = zero
    qbd[0:HD, 1024:2048] = zero
    qbd[HD : 2 * HD, 1024:2048] = q[HD : 2 * HD]
    ones = jnp.ones((16, vt.shape[1]), jnp.bfloat16)
    for kv in range(2):
        vta[kv, 0:HD] = vt[kv * HD : (kv + 1) * HD]
        vta[kv, HD : HD + 16] = ones


def flip(x):
    return jnp.transpose(x.astype(jnp.float32)).astype(jnp.bfloat16)


def shard_kernel(
    start_ref, plen_ref, q_ref, k_ref, v_ref, o_ref, ml_ref, ko_ref, vo_ref, qbd, vta
):
    r = pl.program_id(0)
    off = plen_ref[r] - start_ref[0]
    span = k_ref.shape[1]
    hit = (off > -NEW_TOK) & (off < span)

    @pl.when(hit)
    def _():
        rows = lax.broadcasted_iota(jnp.int32, (span, NEW_TOK), 0)
        cols = lax.broadcasted_iota(jnp.int32, (span, NEW_TOK), 1)
        pick = (rows - off == cols).astype(jnp.float32).astype(jnp.bfloat16)
        rel = lax.broadcasted_iota(jnp.int32, (span, 128), 0) - off
        inside = (rel >= 0) & (rel < NEW_TOK)
        for first, old, out in ((0, k_ref, ko_ref), (512, v_ref, vo_ref)):
            new = jnp.concatenate(
                [q_ref[0, 128:192, first : first + 256], q_ref[0, 128:192, first + 256 : first + 512]],
                axis=0,
            )
            placed = jnp.dot(pick, flip(new), preferred_element_type=jnp.float32)
            out[0] = jnp.where(inside, placed, old[0].astype(jnp.float32)).astype(jnp.bfloat16)

    @pl.when(jnp.logical_not(hit))
    def _():
        ko_ref[0] = k_ref[0]
        vo_ref[0] = v_ref[0]

    def store(kv, lanes, o):
        o_ref[0, pl.ds(kv * HD, HD), lanes] = o.astype(jnp.bfloat16)

    def run(masked):
        fill_scratch(q_ref[0, 0:128], flip(v_ref[0]), qbd, vta)
        mask = None
        if masked:
            mask = lax.broadcasted_iota(jnp.int32, (span, 256), 0) < off
        for kv in range(2):
            for chunk in range(4):
                attend_columns(k_ref[0], qbd, vta, mask, store, ml_ref.at[0], kv, chunk, 256)

    @pl.when(off >= span)
    def _():
        run(False)

    @pl.when((off > 0) & (off < span))
    def _():
        run(True)

    @pl.when(off <= 0)
    def _():
        o_ref[0] = jnp.zeros((2 * HD, 1024), jnp.bfloat16)
        for kv in range(2):
            ml_ref[0, kv, 0:4] = jnp.full((4, 256), NEG, jnp.float32)
            ml_ref[0, kv, 4:8] = jnp.zeros((4, 256), jnp.float32)


def shard_attention(start, prefix_len, packed, k_cache, v_cache):
    reqs, span, width = k_cache.shape
    spec = lambda *shape: pl.BlockSpec((1,) + shape, lambda r, *_: (r,) + (0,) * len(shape))
    flops = reqs * 2048 * span * HD * 4
    return pl.pallas_call(
        shard_kernel,
        out_shape=(
            jax.ShapeDtypeStruct((reqs, 128, 1024), jnp.bfloat16),
            jax.ShapeDtypeStruct((reqs, 2, 8, 256), jnp.float32),
            jax.ShapeDtypeStruct(k_cache.shape, k_cache.dtype),
            jax.ShapeDtypeStruct(v_cache.shape, v_cache.dtype),
        ),
        grid_spec=pltpu.PrefetchScalarGridSpec(
            num_scalar_prefetch=2,
            grid=(reqs,),
            in_specs=[
                spec(192, 1024),
                spec(span, width),
                spec(span, width),
            ],
            out_specs=[spec(128, 1024), spec(2, 8, 256), spec(span, width), spec(span, width)],
            scratch_shapes=[
                pltpu.VMEM((128, 2048), jnp.bfloat16),
                pltpu.VMEM((2, HD + 16, span), jnp.bfloat16),
            ],
        ),
        compiler_params=pltpu.CompilerParams(
            dimension_semantics=("arbitrary",), vmem_limit_bytes=40 << 20
        ),
        cost_estimate=pl.CostEstimate(
            flops=flops * 3, bytes_accessed=40 << 20, transcendentals=reqs * 2048 * span
        ),
    )(start, prefix_len, packed, k_cache, v_cache)


def own_kernel(q_ref, o_ref, ml_ref, qbd, vta):
    part = lambda i: q_ref[128:192, i * 256 : (i + 1) * 256]
    fill_scratch(q_ref[0:128], jnp.concatenate([part(2), part(3)], axis=0), qbd, vta)
    keys = flip(jnp.concatenate([part(0), part(1)], axis=0))
    mask = lax.broadcasted_iota(jnp.int32, (NEW_TOK, NEW_TOK), 0) <= lax.broadcasted_iota(
        jnp.int32, (NEW_TOK, NEW_TOK), 1
    )

    def store(kv, lanes, o):
        o_ref[pl.ds(kv * HD, HD), lanes] = o

    for kv in range(2):
        for chunk in range(4):
            attend_columns(keys, qbd, vta, mask, store, ml_ref, kv, chunk, 256)


def own_attention(packed):
    return pl.pallas_call(
        own_kernel,
        out_shape=(
            jax.ShapeDtypeStruct((128, 1024), jnp.float32),
            jax.ShapeDtypeStruct((2, 8, 256), jnp.float32),
        ),
        scratch_shapes=[
            pltpu.VMEM((128, 2048), jnp.bfloat16),
            pltpu.VMEM((2, HD + 16, NEW_TOK), jnp.bfloat16),
        ],
        compiler_params=pltpu.CompilerParams(vmem_limit_bytes=24 << 20),
        cost_estimate=pl.CostEstimate(flops=1 << 28, bytes_accessed=2 << 20, transcendentals=1 << 19),
    )(packed)


MESH = pl.DeviceIdType.MESH


def grid_place():
    me = lax.axis_index("grp")
    z, y, core = me // 8, (me // 2) % 4, me % 2
    return me, z, y, core


class Sender:
    def __init__(self, axis, send_sems, recv_sems):
        self.axis, self.send_sems, self.recv_sems, self.started = axis, send_sems, recv_sems, []

    def __call__(self, src, dst, device):
        i = len(self.started)
        copy = pltpu.make_async_remote_copy(
            src_ref=src,
            dst_ref=dst,
            send_sem=self.send_sems.at[i],
            recv_sem=self.recv_sems.at[i],
            device_id={self.axis: device},
            device_id_type=MESH,
        )
        copy.start()
        self.started.append(copy)
        return copy

    def finish(self):
        for copy in self.started:
            copy.wait_send()


def greet(axis, devices):
    barrier = pltpu.get_barrier_semaphore()
    for device in devices:
        pl.semaphore_signal(barrier, inc=1, device_id={axis: device}, device_id_type=MESH)
    pl.semaphore_wait(barrier, len(devices))


def grp_gather_kernel(x_ref, out_ref, local_sem, send_sems, recv_sems):
    me, z, y, c = grid_place()
    sib = me + 1 - 2 * c
    yp, ym, yo = (y + 1) % 4, (y + 3) % 4, (y + 2) % 4
    zp, zm, zo = (z + 1) % 4, (z + 3) % 4, (z + 2) % 4
    dev = lambda zz, yy: zz * 8 + yy * 2 + c
    rows = x_ref.shape[0]
    half, quarter = rows // 2, rows // 4
    a, b = pl.ds(0, half), pl.ds(half, half)
    a0, a1 = pl.ds(0, quarter), pl.ds(quarter, quarter)
    b0, b1 = pl.ds(half, quarter), pl.ds(half + quarter, quarter)
    lo, hi, every = pl.ds(0, 2), pl.ds(2, 2), pl.ds(0, 4)
    east, west, north, south = dev(z, yp), dev(z, ym), dev(zp, y), dev(zm, y)
    send = Sender("grp", send_sems, recv_sems)
    own = pltpu.make_async_copy(x_ref, out_ref.at[z, y, c], local_sem)
    own.start()
    greet("grp", (east, west, north, south, sib))

    def same(device, *index):
        ref = out_ref.at[index]
        return send(ref, ref, device)

    ap = send(x_ref.at[a], out_ref.at[z, y, c, a], east)
    bp = send(x_ref.at[b], out_ref.at[z, y, c, b], north)
    am = send(x_ref.at[a], out_ref.at[z, y, c, a], west)
    bm = send(x_ref.at[b], out_ref.at[z, y, c, b], south)
    ap.wait_recv()
    afp = same(east, z, ym, c, a0)
    bp.wait_recv()
    bfp = same(north, zm, y, c, b0)
    am.wait_recv()
    afm = same(west, z, yp, c, a1)
    bm.wait_recv()
    bfm = same(south, zp, y, c, b1)
    own.wait()
    afp.wait_recv()
    afm.wait_recv()
    gap = same(north, z, every, c, a)
    gam = same(south, z, every, c, a)
    bfp.wait_recv()
    bfm.wait_recv()
    gbp = same(east, every, y, c, b)
    gbm = same(west, every, y, c, b)
    over = [same(sib, z, every, c, a), same(sib, every, y, c, b)]
    gap.wait_recv()
    gafp = same(north, zm, lo, c, a)
    over.append(same(sib, zm, every, c, a))
    gbp.wait_recv()
    gbfp = same(east, lo, ym, c, b)
    over.append(same(sib, every, ym, c, b))
    gam.wait_recv()
    gafm = same(south, zp, hi, c, a)
    over.append(same(sib, zp, every, c, a))
    gbm.wait_recv()
    gbfm = same(west, hi, yp, c, b)
    over.append(same(sib, every, yp, c, b))
    gafp.wait_recv()
    gafm.wait_recv()
    over.append(same(sib, zo, every, c, a))
    gbfp.wait_recv()
    gbfm.wait_recv()
    over.append(same(sib, every, yo, c, b))
    send.finish()
    for copy in over:
        copy.wait_recv()


def grp_gather(x, collective_id):
    rows, width = x.shape
    out = pl.pallas_call(
        grp_gather_kernel,
        out_shape=jax.ShapeDtypeStruct((4, 4, 2, rows, width), x.dtype),
        in_specs=[pl.BlockSpec(memory_space=pl.ANY)],
        out_specs=pl.BlockSpec(memory_space=pl.ANY),
        scratch_shapes=[
            pltpu.SemaphoreType.DMA,
            pltpu.SemaphoreType.DMA((24,)),
            pltpu.SemaphoreType.DMA((24,)),
        ],
        compiler_params=pltpu.CompilerParams(collective_id=collective_id, has_side_effects=True),
        cost_estimate=pl.CostEstimate(flops=0, bytes_accessed=100 << 20, transcendentals=0),
    )(x)
    return out.reshape(32, rows, width)


def tp_gather_kernel(x_ref, out_ref, local_sem, send_sems, recv_sems):
    me = lax.axis_index("tp")
    right, left = (me + 1) % 4, (me + 3) % 4
    rows, width = x_ref.shape
    send = Sender("tp", send_sems, recv_sems)
    cols = lambda i: pl.ds(pl.multiple_of(i * width, width), width)
    top, low = pl.ds(0, rows // 2), pl.ds(rows // 2, rows // 2)
    own = pltpu.make_async_copy(x_ref, out_ref.at[:, cols(me)], local_sem)
    own.start()
    greet("tp", (right, left))
    p = send(x_ref, out_ref.at[:, cols(me)], right)
    m = send(x_ref, out_ref.at[:, cols(me)], left)
    p.wait_recv()
    ref = out_ref.at[top, cols(left)]
    fp = send(ref, ref, right)
    m.wait_recv()
    ref = out_ref.at[low, cols(right)]
    fm = send(ref, ref, left)
    fp.wait_recv()
    fm.wait_recv()
    own.wait()
    send.finish()


def tp_gather(x, collective_id):
    rows, width = x.shape
    return pl.pallas_call(
        tp_gather_kernel,
        out_shape=jax.ShapeDtypeStruct((rows, 4 * width), x.dtype),
        in_specs=[pl.BlockSpec(memory_space=pl.ANY)],
        out_specs=pl.BlockSpec(memory_space=pl.ANY),
        scratch_shapes=[
            pltpu.SemaphoreType.DMA,
            pltpu.SemaphoreType.DMA((4,)),
            pltpu.SemaphoreType.DMA((4,)),
        ],
        compiler_params=pltpu.CompilerParams(collective_id=collective_id, has_side_effects=True),
        cost_estimate=pl.CostEstimate(flops=0, bytes_accessed=30 << 20, transcendentals=0),
    )(x)


def merge_stats(parts):
    top = parts[0][0]
    for m, _ in parts[1:]:
        top = jnp.maximum(top, m)
    weights = [jnp.exp2((m - top) * LOG2E) for m, _ in parts]
    total = weights[0] * parts[0][1]
    for w, (_, l) in zip(weights[1:], parts[1:]):
        total = total + w * l
    return weights, top, total


def blend(outs, weights, g):
    acc = outs[0].astype(jnp.float32) * weights[0][g : g + 1]
    for o, w in zip(outs[1:], weights[1:]):
        acc = acc + o.astype(jnp.float32) * w[g : g + 1]
    return acc


def merge_into(acc, accm, others, index, kv, picks):
    stat = lambda ref, i: (ref[i + (pl.ds(0, 4),)], ref[i + (pl.ds(4, 4),)])
    mine = index + (kv,)
    weights, top, total = merge_stats(
        [stat(accm, mine)] + [stat(m, pick) for (_, m), pick in zip(others, picks)]
    )
    accm[mine + (pl.ds(0, 4),)] = top
    accm[mine + (pl.ds(4, 4),)] = total
    for g in range(4):
        lanes = pl.ds(g * 256, 256)
        here = index + (pl.ds(kv * HD, HD), lanes)
        outs = [acc[here]] + [o[pick + (pl.ds(0, HD), lanes)] for (o, _), pick in zip(others, picks)]
        acc[here] = blend(outs, weights, g).astype(jnp.bfloat16)


def grp_merge_kernel(
    o_ref, ml_ref, own_o_ref, own_ml_ref, out_ref,
    acc, accm, r1, r1m, ra, ram, rb, rbm, r3, r3m, local_sems, send_sems, recv_sems,
):
    me, z, y, c = grid_place()
    sib = me + 1 - 2 * c
    yp, ym, yo = (y + 1) % 4, (y + 3) % 4, (y + 2) % 4
    zp, zm, zo = (z + 1) % 4, (z + 3) % 4, (z + 2) % 4
    dev = lambda zz, yy: zz * 8 + yy * 2 + c
    east, west, north, south = dev(z, yp), dev(z, ym), dev(zp, y), dev(zm, y)
    far_y, far_z = dev(z, yo), dev(zo, y)
    send = Sender("grp", send_sems, recv_sems)
    loads = []
    for q in range(4):
        copy = pltpu.make_async_copy(o_ref.at[q, :, c], acc.at[q], local_sems.at[q])
        copy.start()
        loads.append(copy)
    copy = pltpu.make_async_copy(ml_ref.at[:, :, c], accm, local_sems.at[4])
    copy.start()
    loads.append(copy)
    greet("grp", (east, west, north, south, far_y, far_z, sib))
    stats = send(ml_ref.at[:, :, 1 - c], r1m, sib)
    pieces = [send(o_ref.at[q, :, 1 - c], r1.at[q], sib) for q in range(4)]
    for load in loads:
        load.wait()
    stats.wait_recv()
    for q in range(4):
        pieces[q].wait_recv()

        def core_merge(yy, carry, q=q):
            for kv in range(2):
                stat = lambda ref: (ref[q, yy, kv, 0:4], ref[q, yy, kv, 4:8])
                weights, top, total = merge_stats([stat(accm), stat(r1m)])
                accm[q, yy, kv, 0:4] = top
                accm[q, yy, kv, 4:8] = total
                for g in range(4):
                    here = (q, yy, pl.ds(kv * HD, HD), pl.ds(g * 256, 256))
                    acc[here] = blend([acc[here], r1[here]], weights, g).astype(jnp.bfloat16)
            return carry

        lax.fori_loop(0, 4, core_merge, 0)

    lo, hi = pl.ds(0, 2), pl.ds(2, 2)
    ka, kb = pl.ds(0, HD), pl.ds(HD, HD)

    def ship_a(zs, yy, slot, device):
        return (
            send(acc.at[zs, yy, ka], ra.at[slot], device),
            send(accm.at[zs, yy, 0], ram.at[slot], device),
        )

    def ship_b(zz, ys, slot, device):
        return (
            send(acc.at[zz, ys, kb], rb.at[slot], device),
            send(accm.at[zz, ys, 1], rbm.at[slot], device),
        )

    def arrived(pair):
        pair[0].wait_recv()
        pair[1].wait_recv()

    axp = ship_a(lo, yo, 0, east)
    bxp = ship_b(zo, lo, 0, north)
    axm = ship_a(hi, yo, 1, west)
    bxm = ship_b(zo, hi, 1, south)
    app = ship_a(hi, yp, 2, east)
    bpp = ship_b(zp, hi, 2, north)
    apm = ship_a(lo, ym, 3, west)
    bpm = ship_b(zm, lo, 3, south)

    def fold_a(base, yy, slots):
        def body(i, carry):
            merge_into(acc, accm, [(ra, ram)] * len(slots), (base + i, yy), 0, [(s, i) for s in slots])
            return carry

        lax.fori_loop(0, 2, body, 0)

    def fold_b(zz, base, slots):
        def body(i, carry):
            merge_into(acc, accm, [(rb, rbm)] * len(slots), (zz, base + i), 1, [(s, i) for s in slots])
            return carry

        lax.fori_loop(0, 2, body, 0)

    arrived(axp)
    fold_a(0, yp, [0])
    amp = ship_a(lo, yp, 4, east)
    arrived(bxp)
    fold_b(zp, 0, [0])
    bmp = ship_b(zp, lo, 4, north)
    arrived(axm)
    fold_a(2, ym, [1])
    amm = ship_a(hi, ym, 5, west)
    arrived(bxm)
    fold_b(zm, 2, [1])
    bmm = ship_b(zm, hi, 5, south)
    arrived(app)
    arrived(apm)
    arrived(bpp)
    arrived(bpm)
    arrived(amp)
    fold_a(0, y, [3, 4])
    arrived(amm)
    fold_a(2, y, [2, 5])
    arrived(bmp)
    fold_b(z, 0, [3, 4])
    arrived(bmm)
    fold_b(z, 2, [2, 5])

    last = []
    for slot, (zz, device) in enumerate(((zo, far_z), (zp, north), (zm, south))):
        last.append(send(acc.at[zz, y, ka], r3.at[0, slot], device))
        last.append(send(accm.at[zz, y, 0], r3m.at[0, slot], device))
    for slot, (yy, device) in enumerate(((yo, far_y), (yp, east), (ym, west))):
        last.append(send(acc.at[z, yy, kb], r3.at[1, slot], device))
        last.append(send(accm.at[z, yy, 1], r3m.at[1, slot], device))
    for copy in last:
        copy.wait_recv()
    for kv in range(2):
        stat = lambda ref, i: (ref[i + (pl.ds(0, 4),)], ref[i + (pl.ds(4, 4),)])
        parts = [stat(own_ml_ref, (kv,)), stat(accm, (z, y, kv))]
        parts += [stat(r3m, (kv, s)) for s in range(3)]
        weights, _, total = merge_stats(parts)
        scale = 1.0 / total
        weights = [w * scale for w in weights]
        for g in range(4):
            lanes = pl.ds(g * 256, 256)
            rows = pl.ds(kv * HD, HD)
            outs = [own_o_ref[rows, lanes], acc[z, y, rows, lanes]]
            outs += [r3[kv, s, :, lanes] for s in range(3)]
            out_ref[rows, lanes] = blend(outs, weights, g).astype(jnp.bfloat16)
    send.finish()


def grp_merge(part_o, part_ml, own_o, own_ml, collective_id):
    bf, f32 = jnp.bfloat16, jnp.float32
    any_spec = pl.BlockSpec(memory_space=pl.ANY)
    vmem = pl.BlockSpec(memory_space=pltpu.VMEM)
    copies = 5 + 24 + 12
    return pl.pallas_call(
        grp_merge_kernel,
        out_shape=jax.ShapeDtypeStruct((128, 1024), bf),
        in_specs=[any_spec, any_spec, vmem, vmem],
        out_specs=vmem,
        scratch_shapes=[
            pltpu.VMEM((4, 4, 128, 1024), bf),
            pltpu.VMEM((4, 4, 2, 8, 256), f32),
            pltpu.VMEM((4, 4, 128, 1024), bf),
            pltpu.VMEM((4, 4, 2, 8, 256), f32),
            pltpu.VMEM((6, 2, HD, 1024), bf),
            pltpu.VMEM((6, 2, 8, 256), f32),
            pltpu.VMEM((6, 2, HD, 1024), bf),
            pltpu.VMEM((6, 2, 8, 256), f32),
            pltpu.VMEM((2, 3, HD, 1024), bf),
            pltpu.VMEM((2, 3, 8, 256), f32),
            pltpu.SemaphoreType.DMA((5,)),
            pltpu.SemaphoreType.DMA((copies,)),
            pltpu.SemaphoreType.DMA((copies,)),
        ],
        compiler_params=pltpu.CompilerParams(
            collective_id=collective_id, has_side_effects=True, vmem_limit_bytes=32 << 20
        ),
        cost_estimate=pl.CostEstimate(flops=0, bytes_accessed=130 << 20, transcendentals=0),
    )(
        part_o.reshape(4, 4, 2, 128, 1024),
        part_ml.reshape(4, 4, 2, 2, 8, 256),
        own_o,
        own_ml,
    )


def shards(
    tokens,
    attn_gain,
    w_query,
    w_key,
    w_value,
    w_out,
    mlp_gain,
    w_gate,
    w_up,
    w_down,
    k_cache,
    v_cache,
    prefix_len,
):
    group = lax.axis_index("grp")
    slice_len = k_cache.shape[1]
    start = group * slice_len
    weights = lax.all_gather(
        jnp.concatenate([w_gate, w_up, w_down.T], axis=0), "grp", axis=0, tiled=False
    )
    whole = tp_gather(tokens, 0)
    normed = rms_scale(whole, attn_gain).astype(jnp.bfloat16)
    own_len = lax.dynamic_slice_in_dim(prefix_len, group, 1)[0]
    positions = (own_len + jnp.arange(NEW_TOK, dtype=jnp.int32)).astype(jnp.float32)
    inverse = ROPE_BASE ** (-2.0 * jnp.arange(HD // 2, dtype=jnp.float32) / HD)
    angles = positions[None, :] * inverse[:, None]
    cosine, sine = jnp.cos(angles), jnp.sin(angles)
    flat = lambda w: lax.dot_general(
        w, normed, (((0,), (1,)), ((), ())), preferred_element_type=jnp.float32
    )

    def rope(heads):
        heads = heads.reshape(-1, 2, 32, NEW_TOK)
        first, second = heads[:, 0], heads[:, 1]
        turned = [first * cosine - second * sine, second * cosine + first * sine]
        return jnp.stack(turned, axis=1).reshape(-1, HD, NEW_TOK).astype(jnp.bfloat16)

    q = rope(flat(w_query)) * jnp.bfloat16(0.125)
    q = jnp.transpose(q.reshape(2, 4, HD, NEW_TOK), (0, 2, 1, 3)).reshape(128, 1024)
    new = jnp.concatenate(
        [rope(flat(w_key)), flat(w_value).astype(jnp.bfloat16).reshape(2, HD, NEW_TOK)], axis=0
    )
    packed = jnp.concatenate([q, jnp.transpose(new, (1, 0, 2)).reshape(HD, 1024)], axis=0)
    part_o, part_ml, k_next, v_next = shard_attention(
        start[None], prefix_len, grp_gather(packed, 1), k_cache, v_cache
    )
    own_o, own_ml = own_attention(packed)
    attended = grp_merge(part_o, part_ml, own_o, own_ml, 2)
    attended = (
        attended.reshape(2, HD, 4, NEW_TOK).transpose(3, 0, 2, 1).reshape(NEW_TOK, 512)
    )
    attn_terms = jnp.dot(attended, w_out, preferred_element_type=jnp.float32)
    mixed = lax.psum_scatter(attn_terms, "tp", scatter_dimension=1, tiled=True)
    first = (tokens.astype(jnp.float32) + mixed).astype(jnp.bfloat16)
    first_whole = lax.all_gather(first, "tp", axis=1, tiled=True)
    normed_two = rms_scale(first_whole, mlp_gain).astype(jnp.bfloat16)
    w_g = weights[:, 0:64].reshape(2048, -1)
    w_u = weights[:, 64:128].reshape(2048, -1)
    w_d = weights[:, 128:192].reshape(2048, -1)
    gate = jnp.dot(normed_two, w_g, preferred_element_type=jnp.float32)
    upward = jnp.dot(normed_two, w_u, preferred_element_type=jnp.float32)
    hidden = (jax.nn.silu(gate) * upward).astype(jnp.bfloat16)
    down_terms = lax.dot_general(
        hidden, w_d, (((1,), (1,)), ((), ())), preferred_element_type=jnp.float32
    )
    down = lax.psum_scatter(down_terms, "tp", scatter_dimension=1, tiled=True)
    result = first.astype(jnp.float32) + down
    return (result, k_next, v_next)


def solution(mesh):
    placed = (
        P("grp", "tp"),
        P(),
        P(None, "tp"),
        P(None, "tp"),
        P(None, "tp"),
        P("tp", None),
        P(),
        P("grp", "tp"),
        P("grp", "tp"),
        P("tp", "grp"),
        P(None, "grp", "tp"),
        P(None, "grp", "tp"),
        P(),
    )
    return jax.shard_map(
        shards,
        mesh=mesh,
        in_specs=placed,
        out_specs=(P("grp", "tp"), P(None, "grp", "tp"), P(None, "grp", "tp")),
        check_vma=False,
    )
```

```python
import math

import jax
import jax.numpy as jnp
from jax import lax
from jax.experimental import pallas as pl
from jax.experimental.pallas import tpu as pltpu
from jax.sharding import PartitionSpec as P

HD = 64
NEW_TOK = 256
EPS = 1e-05
ROPE_BASE = 500000.0
NEG = -1e30
LOG2E = math.log2(math.e)


def rms_scale(rows, gain):
    rows = rows.astype(jnp.float32)
    return rows * lax.rsqrt(jnp.mean(rows * rows, axis=-1, keepdims=True) + EPS) * gain


def attend(keys, qbd, vta, mask, o_store, ml_ref, width=512):
    blocks = 2048 // width

    def scores(i):
        return jnp.dot(
            keys, qbd[:, i * width : (i + 1) * width], preferred_element_type=jnp.float32
        )

    def soften(s):
        s = jnp.where(mask, s, NEG)
        top = jnp.max(s, axis=0, keepdims=True)
        return top, jnp.exp2((s - top) * LOG2E).astype(jnp.bfloat16)

    def finish(i, top, p):
        kv, first = divmod(i * width, 1024)
        o = jnp.dot(vta[kv], p, preferred_element_type=jnp.float32)
        o_store(kv, pl.ds(first, width), o[:HD])
        for j in range(0, width, 256):
            g = (first + j) // 256
            ml_ref[kv, g : g + 1] = top[:, j : j + 256]
            ml_ref[kv, 4 + g : 5 + g] = o[HD : HD + 1, j : j + 256]

    s, before = scores(0), None
    for i in range(blocks):
        ahead = scores(i + 1) if i + 1 < blocks else None
        now = soften(s)
        if before is not None:
            finish(i - 1, *before)
        before, s = now, ahead
    finish(blocks - 1, *before)


def fill_scratch(q, vt, qbd, vta):
    zero = jnp.zeros((HD, 1024), jnp.bfloat16)
    qbd[0:HD, 0:1024] = q[0:HD]
    qbd[HD : 2 * HD, 0:1024] = zero
    qbd[0:HD, 1024:2048] = zero
    qbd[HD : 2 * HD, 1024:2048] = q[HD : 2 * HD]
    ones = jnp.ones((16, vt.shape[1]), jnp.bfloat16)
    for kv in range(2):
        vta[kv, 0:HD] = vt[kv * HD : (kv + 1) * HD]
        vta[kv, HD : HD + 16] = ones


def flip(x):
    return jnp.transpose(x.astype(jnp.float32)).astype(jnp.bfloat16)


def shard_kernel(
    start_ref, plen_ref, q_ref, k_ref, v_ref, o_ref, ml_ref, ko_ref, vo_ref, qbd, vta
):
    r = pl.program_id(0)
    off = plen_ref[r] - start_ref[0]
    span = k_ref.shape[1]
    hit = (off > -NEW_TOK) & (off < span)

    @pl.when(hit)
    def _():
        rows = lax.broadcasted_iota(jnp.int32, (span, NEW_TOK), 0)
        cols = lax.broadcasted_iota(jnp.int32, (span, NEW_TOK), 1)
        pick = (rows - off == cols).astype(jnp.float32).astype(jnp.bfloat16)
        rel = lax.broadcasted_iota(jnp.int32, (span, 128), 0) - off
        inside = (rel >= 0) & (rel < NEW_TOK)
        for first, old, out in ((0, k_ref, ko_ref), (512, v_ref, vo_ref)):
            new = jnp.concatenate(
                [q_ref[0, 128:192, first : first + 256], q_ref[0, 128:192, first + 256 : first + 512]],
                axis=0,
            )
            placed = jnp.dot(pick, flip(new), preferred_element_type=jnp.float32)
            out[0] = jnp.where(inside, placed, old[0].astype(jnp.float32)).astype(jnp.bfloat16)

    @pl.when(jnp.logical_not(hit))
    def _():
        ko_ref[0] = k_ref[0]
        vo_ref[0] = v_ref[0]

    def store(kv, lanes, o):
        o_ref[0, pl.ds(kv * HD, HD), lanes] = o.astype(jnp.bfloat16)

    @pl.when(off > 0)
    def _():
        fill_scratch(q_ref[0, 0:128], flip(v_ref[0]), qbd, vta)
        mask = lax.broadcasted_iota(jnp.int32, (span, 512), 0) < off
        attend(k_ref[0], qbd, vta, mask, store, ml_ref.at[0])

    @pl.when(off <= 0)
    def _():
        o_ref[0] = jnp.zeros((2 * HD, 1024), jnp.bfloat16)
        for kv in range(2):
            ml_ref[0, kv, 0:4] = jnp.full((4, 256), NEG, jnp.float32)
            ml_ref[0, kv, 4:8] = jnp.zeros((4, 256), jnp.float32)


def shard_attention(start, prefix_len, packed, k_cache, v_cache):
    reqs, span, width = k_cache.shape
    spec = lambda *shape: pl.BlockSpec((1,) + shape, lambda r, *_: (r,) + (0,) * len(shape))
    flops = reqs * 2048 * span * HD * 4
    return pl.pallas_call(
        shard_kernel,
        out_shape=(
            jax.ShapeDtypeStruct((reqs, 128, 1024), jnp.bfloat16),
            jax.ShapeDtypeStruct((reqs, 2, 8, 256), jnp.float32),
            jax.ShapeDtypeStruct(k_cache.shape, k_cache.dtype),
            jax.ShapeDtypeStruct(v_cache.shape, v_cache.dtype),
        ),
        grid_spec=pltpu.PrefetchScalarGridSpec(
            num_scalar_prefetch=2,
            grid=(reqs,),
            in_specs=[
                spec(192, 1024),
                spec(span, width),
                spec(span, width),
            ],
            out_specs=[spec(128, 1024), spec(2, 8, 256), spec(span, width), spec(span, width)],
            scratch_shapes=[
                pltpu.VMEM((128, 2048), jnp.bfloat16),
                pltpu.VMEM((2, HD + 16, span), jnp.bfloat16),
            ],
        ),
        compiler_params=pltpu.CompilerParams(
            dimension_semantics=("arbitrary",), vmem_limit_bytes=58 << 20
        ),
        cost_estimate=pl.CostEstimate(
            flops=flops * 3, bytes_accessed=40 << 20, transcendentals=reqs * 2048 * span
        ),
    )(start, prefix_len, packed, k_cache, v_cache)


def own_kernel(q_ref, o_ref, ml_ref, qbd, vta):
    part = lambda i: q_ref[128:192, i * 256 : (i + 1) * 256]
    fill_scratch(q_ref[0:128], jnp.concatenate([part(2), part(3)], axis=0), qbd, vta)
    keys = flip(jnp.concatenate([part(0), part(1)], axis=0))
    mask = (
        lax.broadcasted_iota(jnp.int32, (NEW_TOK, 512), 0)
        <= lax.broadcasted_iota(jnp.int32, (NEW_TOK, 512), 1) % NEW_TOK
    )

    def store(kv, lanes, o):
        o_ref[pl.ds(kv * HD, HD), lanes] = o

    attend(keys, qbd, vta, mask, store, ml_ref)


def own_attention(packed):
    return pl.pallas_call(
        own_kernel,
        out_shape=(
            jax.ShapeDtypeStruct((128, 1024), jnp.float32),
            jax.ShapeDtypeStruct((2, 8, 256), jnp.float32),
        ),
        scratch_shapes=[
            pltpu.VMEM((128, 2048), jnp.bfloat16),
            pltpu.VMEM((2, HD + 16, NEW_TOK), jnp.bfloat16),
        ],
        compiler_params=pltpu.CompilerParams(vmem_limit_bytes=24 << 20),
        cost_estimate=pl.CostEstimate(flops=1 << 28, bytes_accessed=2 << 20, transcendentals=1 << 19),
    )(packed)


MESH = pl.DeviceIdType.MESH


def grid_place():
    me = lax.axis_index("grp")
    z, y, core = me // 8, (me // 2) % 4, me % 2
    return me, z, y, core


class Sender:
    def __init__(self, axis, send_sems, recv_sems):
        self.axis, self.send_sems, self.recv_sems, self.started = axis, send_sems, recv_sems, []

    def __call__(self, src, dst, device, axis=None):
        i = len(self.started)
        copy = pltpu.make_async_remote_copy(
            src_ref=src,
            dst_ref=dst,
            send_sem=self.send_sems.at[i],
            recv_sem=self.recv_sems.at[i],
            device_id={axis or self.axis: device},
            device_id_type=MESH,
        )
        copy.start()
        self.started.append(copy)
        return copy

    def finish(self):
        for copy in self.started:
            copy.wait_send()


def greet(devices):
    barrier = pltpu.get_barrier_semaphore()
    for axis, device in devices:
        pl.semaphore_signal(barrier, inc=1, device_id={axis: device}, device_id_type=MESH)
    pl.semaphore_wait(barrier, len(devices))


def grp_gather_kernel(x_ref, w_ref, out_ref, w_out_ref, local_sems, send_sems, recv_sems):
    me, z, y, c = grid_place()
    sib = me + 1 - 2 * c
    yp, ym, yo = (y + 1) % 4, (y + 3) % 4, (y + 2) % 4
    zp, zm, zo = (z + 1) % 4, (z + 3) % 4, (z + 2) % 4
    dev = lambda zz, yy: zz * 8 + yy * 2 + c
    rows = x_ref.shape[0]
    half, quarter = rows // 2, rows // 4
    a, b = pl.ds(0, half), pl.ds(half, half)
    a0, a1 = pl.ds(0, quarter), pl.ds(quarter, quarter)
    b0, b1 = pl.ds(half, quarter), pl.ds(half + quarter, quarter)
    lo, hi, every = pl.ds(0, 2), pl.ds(2, 2), pl.ds(0, 4)
    east, west, north, south = dev(z, yp), dev(z, ym), dev(zp, y), dev(zm, y)
    send = Sender("grp", send_sems, recv_sems)
    x = lax.axis_index("tp")
    right, left, facing = (x + 1) % 4, (x + 3) % 4, (x + 2) % 4
    own = pltpu.make_async_copy(x_ref, out_ref.at[z, y, c], local_sems.at[0])
    own.start()
    own_w = pltpu.make_async_copy(w_ref, w_out_ref.at[x], local_sems.at[1])
    own_w.start()
    greet(
        [("grp", i) for i in (east, west, north, south, sib)] + [("tp", right), ("tp", left)]
    )

    def same(device, *index):
        ref = out_ref.at[index]
        return send(ref, ref, device)

    ap = send(x_ref.at[a], out_ref.at[z, y, c, a], east)
    bp = send(x_ref.at[b], out_ref.at[z, y, c, b], north)
    am = send(x_ref.at[a], out_ref.at[z, y, c, a], west)
    bm = send(x_ref.at[b], out_ref.at[z, y, c, b], south)
    share = w_ref.shape[0] // 2
    mine = pl.ds(pl.multiple_of(c * share, share), share)
    mine0 = pl.ds(pl.multiple_of(c * share, share // 2), share // 2)
    mine1 = pl.ds(pl.multiple_of(c * share + share // 2, share // 2), share // 2)

    def same_w(device, axis, *index):
        ref = w_out_ref.at[index]
        return send(ref, ref, device, axis)

    wp = send(w_ref.at[mine], w_out_ref.at[x, mine], right, "tp")
    wm = send(w_ref.at[mine], w_out_ref.at[x, mine], left, "tp")
    ap.wait_recv()
    afp = same(east, z, ym, c, a0)
    bp.wait_recv()
    bfp = same(north, zm, y, c, b0)
    am.wait_recv()
    afm = same(west, z, yp, c, a1)
    bm.wait_recv()
    bfm = same(south, zp, y, c, b1)
    own.wait()
    afp.wait_recv()
    afm.wait_recv()
    gap = same(north, z, every, c, a)
    gam = same(south, z, every, c, a)
    bfp.wait_recv()
    bfm.wait_recv()
    gbp = same(east, every, y, c, b)
    gbm = same(west, every, y, c, b)
    over = [same(sib, z, every, c, a), same(sib, every, y, c, b)]
    gap.wait_recv()
    gafp = same(north, zm, lo, c, a)
    over.append(same(sib, zm, every, c, a))
    gbp.wait_recv()
    gbfp = same(east, lo, ym, c, b)
    over.append(same(sib, every, ym, c, b))
    gam.wait_recv()
    gafm = same(south, zp, hi, c, a)
    over.append(same(sib, zp, every, c, a))
    gbm.wait_recv()
    gbfm = same(west, hi, yp, c, b)
    over.append(same(sib, every, yp, c, b))
    wp.wait_recv()
    wfp = same_w(right, "tp", left, mine0)
    over.append(same_w(sib, "grp", left, mine))
    wm.wait_recv()
    wfm = same_w(left, "tp", right, mine1)
    over.append(same_w(sib, "grp", right, mine))
    gafp.wait_recv()
    gafm.wait_recv()
    over.append(same(sib, zo, every, c, a))
    gbfp.wait_recv()
    gbfm.wait_recv()
    over.append(same(sib, every, yo, c, b))
    wfp.wait_recv()
    wfm.wait_recv()
    over.append(same_w(sib, "grp", facing, mine))
    own_w.wait()
    send.finish()
    for copy in over:
        copy.wait_recv()


def grp_gather(x, w, collective_id):
    rows, width = x.shape
    hbm = pl.BlockSpec(memory_space=pl.ANY)
    out, whole_w = pl.pallas_call(
        grp_gather_kernel,
        out_shape=(
            jax.ShapeDtypeStruct((4, 4, 2, rows, width), x.dtype),
            jax.ShapeDtypeStruct((4,) + w.shape, w.dtype),
        ),
        in_specs=[hbm, hbm],
        out_specs=(hbm, hbm),
        scratch_shapes=[
            pltpu.SemaphoreType.DMA((2,)),
            pltpu.SemaphoreType.DMA((32,)),
            pltpu.SemaphoreType.DMA((32,)),
        ],
        compiler_params=pltpu.CompilerParams(collective_id=collective_id, has_side_effects=True),
        cost_estimate=pl.CostEstimate(flops=0, bytes_accessed=100 << 20, transcendentals=0),
    )(x, w)
    return out.reshape(32, rows, width), whole_w.reshape(-1, w.shape[1])


def tp_gather_kernel(x_ref, out_ref, local_sem, send_sems, recv_sems):
    me = lax.axis_index("tp")
    right, left = (me + 1) % 4, (me + 3) % 4
    rows, width = x_ref.shape
    send = Sender("tp", send_sems, recv_sems)
    cols = lambda i: pl.ds(pl.multiple_of(i * width, width), width)
    top, low = pl.ds(0, rows // 2), pl.ds(rows // 2, rows // 2)
    own = pltpu.make_async_copy(x_ref, out_ref.at[:, cols(me)], local_sem)
    own.start()
    greet((("tp", right), ("tp", left)))
    p = send(x_ref, out_ref.at[:, cols(me)], right)
    m = send(x_ref, out_ref.at[:, cols(me)], left)
    p.wait_recv()
    ref = out_ref.at[top, cols(left)]
    fp = send(ref, ref, right)
    m.wait_recv()
    ref = out_ref.at[low, cols(right)]
    fm = send(ref, ref, left)
    fp.wait_recv()
    fm.wait_recv()
    own.wait()
    send.finish()


def tp_gather(x, collective_id):
    rows, width = x.shape
    return pl.pallas_call(
        tp_gather_kernel,
        out_shape=jax.ShapeDtypeStruct((rows, 4 * width), x.dtype),
        in_specs=[pl.BlockSpec(memory_space=pl.ANY)],
        out_specs=pl.BlockSpec(memory_space=pl.ANY),
        scratch_shapes=[
            pltpu.SemaphoreType.DMA,
            pltpu.SemaphoreType.DMA((4,)),
            pltpu.SemaphoreType.DMA((4,)),
        ],
        compiler_params=pltpu.CompilerParams(collective_id=collective_id, has_side_effects=True),
        cost_estimate=pl.CostEstimate(flops=0, bytes_accessed=30 << 20, transcendentals=0),
    )(x)


def merge_stats(parts):
    top = parts[0][0]
    for m, _ in parts[1:]:
        top = jnp.maximum(top, m)
    weights = [jnp.exp2((m - top) * LOG2E) for m, _ in parts]
    total = weights[0] * parts[0][1]
    for w, (_, l) in zip(weights[1:], parts[1:]):
        total = total + w * l
    return weights, top, total


def blend(outs, weights, g):
    acc = outs[0].astype(jnp.float32) * weights[0][g : g + 1]
    for o, w in zip(outs[1:], weights[1:]):
        acc = acc + o.astype(jnp.float32) * w[g : g + 1]
    return acc


def merge_into(acc, accm, others, index, kv, picks):
    stat = lambda ref, i: (ref[i + (pl.ds(0, 4),)], ref[i + (pl.ds(4, 4),)])
    mine = index + (kv,)
    weights, top, total = merge_stats(
        [stat(accm, mine)] + [stat(m, pick) for (_, m), pick in zip(others, picks)]
    )
    accm[mine + (pl.ds(0, 4),)] = top
    accm[mine + (pl.ds(4, 4),)] = total
    for g in range(4):
        lanes = pl.ds(g * 256, 256)
        here = index + (pl.ds(kv * HD, HD), lanes)
        outs = [acc[here]] + [o[pick + (pl.ds(0, HD), lanes)] for (o, _), pick in zip(others, picks)]
        acc[here] = blend(outs, weights, g).astype(jnp.bfloat16)


def grp_merge_kernel(
    o_ref, ml_ref, own_o_ref, own_ml_ref, out_ref,
    acc, accm, r1, r1m, ra, ram, rb, rbm, r3, r3m, att, local_sems, send_sems, recv_sems,
):
    me, z, y, c = grid_place()
    sib = me + 1 - 2 * c
    yp, ym, yo = (y + 1) % 4, (y + 3) % 4, (y + 2) % 4
    zp, zm, zo = (z + 1) % 4, (z + 3) % 4, (z + 2) % 4
    dev = lambda zz, yy: zz * 8 + yy * 2 + c
    east, west, north, south = dev(z, yp), dev(z, ym), dev(zp, y), dev(zm, y)
    far_y, far_z = dev(z, yo), dev(zo, y)
    send = Sender("grp", send_sems, recv_sems)
    loads = []
    for q in range(4):
        copy = pltpu.make_async_copy(o_ref.at[q, :, c], acc.at[q], local_sems.at[q])
        copy.start()
        loads.append(copy)
    copy = pltpu.make_async_copy(ml_ref.at[:, :, c], accm, local_sems.at[4])
    copy.start()
    loads.append(copy)
    x = lax.axis_index("tp")
    right, left = (x + 1) % 4, (x + 3) % 4
    greet(
        [("grp", i) for i in (east, west, north, south, far_y, far_z, sib)]
        + [("tp", right), ("tp", left)]
    )
    stats = send(ml_ref.at[:, :, 1 - c], r1m, sib)
    pieces = [send(o_ref.at[q, :, 1 - c], r1.at[q], sib) for q in range(4)]
    for load in loads:
        load.wait()
    stats.wait_recv()
    for q in range(4):
        pieces[q].wait_recv()

        def core_merge(yy, carry, q=q):
            for kv in range(2):
                stat = lambda ref: (ref[q, yy, kv, 0:4], ref[q, yy, kv, 4:8])
                weights, top, total = merge_stats([stat(accm), stat(r1m)])
                accm[q, yy, kv, 0:4] = top
                accm[q, yy, kv, 4:8] = total
                for g in range(4):
                    here = (q, yy, pl.ds(kv * HD, HD), pl.ds(g * 256, 256))
                    acc[here] = blend([acc[here], r1[here]], weights, g).astype(jnp.bfloat16)
            return carry

        lax.fori_loop(0, 4, core_merge, 0)

    lo, hi = pl.ds(0, 2), pl.ds(2, 2)
    ka, kb = pl.ds(0, HD), pl.ds(HD, HD)

    def ship_a(zs, yy, slot, device):
        return (
            send(acc.at[zs, yy, ka], ra.at[slot], device),
            send(accm.at[zs, yy, 0], ram.at[slot], device),
        )

    def ship_b(zz, ys, slot, device):
        return (
            send(acc.at[zz, ys, kb], rb.at[slot], device),
            send(accm.at[zz, ys, 1], rbm.at[slot], device),
        )

    def arrived(pair):
        pair[0].wait_recv()
        pair[1].wait_recv()

    axp = ship_a(lo, yo, 0, east)
    bxp = ship_b(zo, lo, 0, north)
    axm = ship_a(hi, yo, 1, west)
    bxm = ship_b(zo, hi, 1, south)
    app = ship_a(hi, yp, 2, east)
    bpp = ship_b(zp, hi, 2, north)
    apm = ship_a(lo, ym, 3, west)
    bpm = ship_b(zm, lo, 3, south)

    def fold_a(base, yy, slots):
        def body(i, carry):
            merge_into(acc, accm, [(ra, ram)] * len(slots), (base + i, yy), 0, [(s, i) for s in slots])
            return carry

        lax.fori_loop(0, 2, body, 0)

    def fold_b(zz, base, slots):
        def body(i, carry):
            merge_into(acc, accm, [(rb, rbm)] * len(slots), (zz, base + i), 1, [(s, i) for s in slots])
            return carry

        lax.fori_loop(0, 2, body, 0)

    arrived(axp)
    fold_a(0, yp, [0])
    amp = ship_a(lo, yp, 4, east)
    arrived(bxp)
    fold_b(zp, 0, [0])
    bmp = ship_b(zp, lo, 4, north)
    arrived(axm)
    fold_a(2, ym, [1])
    amm = ship_a(hi, ym, 5, west)
    arrived(bxm)
    fold_b(zm, 2, [1])
    bmm = ship_b(zm, hi, 5, south)
    arrived(app)
    arrived(apm)
    arrived(bpp)
    arrived(bpm)
    arrived(amp)
    fold_a(0, y, [3, 4])
    arrived(amm)
    fold_a(2, y, [2, 5])
    arrived(bmp)
    fold_b(z, 0, [3, 4])
    arrived(bmm)
    fold_b(z, 2, [2, 5])

    last = []
    for slot, (zz, device) in enumerate(((zo, far_z), (zp, north), (zm, south))):
        last.append(send(acc.at[zz, y, ka], r3.at[0, slot], device))
        last.append(send(accm.at[zz, y, 0], r3m.at[0, slot], device))
    for slot, (yy, device) in enumerate(((yo, far_y), (yp, east), (ym, west))):
        last.append(send(acc.at[z, yy, kb], r3.at[1, slot], device))
        last.append(send(accm.at[z, yy, 1], r3m.at[1, slot], device))
    for copy in last:
        copy.wait_recv()
    for kv in range(2):
        stat = lambda ref, i: (ref[i + (pl.ds(0, 4),)], ref[i + (pl.ds(4, 4),)])
        parts = [stat(own_ml_ref, (kv,)), stat(accm, (z, y, kv))]
        parts += [stat(r3m, (kv, s)) for s in range(3)]
        weights, _, total = merge_stats(parts)
        scale = 1.0 / total
        weights = [w * scale for w in weights]
        rows = pl.ds(kv * HD, HD)
        for pair in range(2):
            heads = []
            for g in (2 * pair, 2 * pair + 1):
                lanes = pl.ds(g * 256, 256)
                outs = [own_o_ref[rows, lanes], acc[z, y, rows, lanes]]
                outs += [r3[kv, s, :, lanes] for s in range(3)]
                heads.append(blend(outs, weights, g))
            block = jnp.transpose(jnp.concatenate(heads, axis=0)).astype(jnp.bfloat16)
            att[:, pl.ds((kv * 2 + pair) * 128, 128)] = block
    rows, width = att.shape
    cols = lambda i: pl.ds(pl.multiple_of(i * width, width), width)
    upper, lower = pl.ds(0, rows // 2), pl.ds(rows // 2, rows // 2)
    own = pltpu.make_async_copy(att, out_ref.at[:, cols(x)], local_sems.at[5])
    own.start()
    p = send(att, out_ref.at[:, cols(x)], right, "tp")
    m = send(att, out_ref.at[:, cols(x)], left, "tp")
    p.wait_recv()
    ref = out_ref.at[upper, cols(left)]
    fp = send(ref, ref, right, "tp")
    m.wait_recv()
    ref = out_ref.at[lower, cols(right)]
    fm = send(ref, ref, left, "tp")
    fp.wait_recv()
    fm.wait_recv()
    own.wait()
    send.finish()


def grp_merge(part_o, part_ml, own_o, own_ml, collective_id):
    bf, f32 = jnp.bfloat16, jnp.float32
    any_spec = pl.BlockSpec(memory_space=pl.ANY)
    vmem = pl.BlockSpec(memory_space=pltpu.VMEM)
    copies = 5 + 24 + 12 + 4
    return pl.pallas_call(
        grp_merge_kernel,
        out_shape=jax.ShapeDtypeStruct((NEW_TOK, 2048), bf),
        in_specs=[any_spec, any_spec, vmem, vmem],
        out_specs=any_spec,
        scratch_shapes=[
            pltpu.VMEM((4, 4, 128, 1024), bf),
            pltpu.VMEM((4, 4, 2, 8, 256), f32),
            pltpu.VMEM((4, 4, 128, 1024), bf),
            pltpu.VMEM((4, 4, 2, 8, 256), f32),
            pltpu.VMEM((6, 2, HD, 1024), bf),
            pltpu.VMEM((6, 2, 8, 256), f32),
            pltpu.VMEM((6, 2, HD, 1024), bf),
            pltpu.VMEM((6, 2, 8, 256), f32),
            pltpu.VMEM((2, 3, HD, 1024), bf),
            pltpu.VMEM((2, 3, 8, 256), f32),
            pltpu.VMEM((NEW_TOK, 512), bf),
            pltpu.SemaphoreType.DMA((6,)),
            pltpu.SemaphoreType.DMA((copies,)),
            pltpu.SemaphoreType.DMA((copies,)),
        ],
        compiler_params=pltpu.CompilerParams(
            collective_id=collective_id, has_side_effects=True, vmem_limit_bytes=58 << 20
        ),
        cost_estimate=pl.CostEstimate(flops=0, bytes_accessed=130 << 20, transcendentals=0),
    )(
        part_o.reshape(4, 4, 2, 128, 1024),
        part_ml.reshape(4, 4, 2, 2, 8, 256),
        own_o,
        own_ml,
    )


def tail_kernel(
    att_ref, tok_ref, gain_ref, wo_ref, w_ref, out_ref,
    wo, wb, acc, firsts, n2, gate, up, hid, mine, outbox, inbox, load_sems, send_sems, recv_sems,
):
    me = lax.axis_index("tp")
    right, left, facing = (me + 1) % 4, (me + 3) % 4, (me + 2) % 4
    send = Sender("tp", send_sems, recv_sems)
    wo_part = lambda i: pltpu.make_async_copy(
        wo_ref.at[pl.ds(i * 512, 512)], wo.at[pl.ds(i * 512, 512)], load_sems.at[i]
    )
    w_part = lambda i: pltpu.make_async_copy(
        w_ref.at[pl.ds(i * 4, 4)], wb.at[pl.ds(i * 4, 4)], load_sems.at[4 + i]
    )
    for i in range(4):
        wo_part(i).start()
    for i in range(8):
        w_part(i).start()
    greet((("tp", right), ("tp", left), ("tp", facing)))
    f32, bf = jnp.float32, jnp.bfloat16
    acc[...] = tok_ref[...].astype(f32)
    for i in range(4):
        wo_part(i).wait()

        def project(n, carry, i=i):
            lanes = pl.ds(pl.multiple_of(n * 512, 512), 512)
            acc[:, lanes] += jnp.dot(
                att_ref[:, i * 512 : (i + 1) * 512],
                wo[i * 512 : (i + 1) * 512, lanes],
                preferred_element_type=f32,
            )
            return carry

        lax.fori_loop(0, 4, project, 0)

    def norm(i, carry):
        rows = pl.ds(pl.multiple_of(i * 32, 32), 32)
        first = acc[rows].astype(bf)
        firsts[rows] = first
        n2[rows] = rms_scale(first, gain_ref[...]).astype(bf)
        return carry

    lax.fori_loop(0, NEW_TOK // 32, norm, 0)
    gate[...] = jnp.zeros_like(gate)
    up[...] = jnp.zeros_like(up)
    for i in range(8):
        w_part(i).wait()

        def widen(n, carry, i=i):
            lanes = pl.ds(pl.multiple_of(n * 512, 512), 512)
            x = n2[:, i * 256 : (i + 1) * 256]
            for total, at in ((gate, 0), (up, 64)):
                w = wb[4 * i : 4 * i + 4, at : at + 64, lanes].reshape(256, 512)
                total[:, lanes] += jnp.dot(x, w, preferred_element_type=f32)
            return carry

        lax.fori_loop(0, 2, widen, 0)

    def squash(i, carry):
        rows = pl.ds(pl.multiple_of(i * 32, 32), 32)
        v = gate[rows]
        hid[rows] = (v / (1.0 + jnp.exp(-v)) * up[rows]).astype(bf)
        return carry

    lax.fori_loop(0, NEW_TOK // 32, squash, 0)

    def terms(target):
        w = wb[pl.ds(target * 8, 8), 128:192].reshape(512, 1024)
        return lax.dot_general(
            hid[...], w, (((1,), (1,)), ((), ())), preferred_element_type=f32
        )

    for slot, target in enumerate((facing, right, left)):
        outbox[slot] = terms(target).astype(bf)
        send(outbox.at[slot], inbox.at[slot], target)
    cols = pl.ds(pl.multiple_of(me * 512, 512), 512)
    mine[...] = firsts[:, cols].astype(f32) + terms(me)
    for copy in send.started:
        copy.wait_recv()
    for slot in range(3):
        mine[...] += inbox[slot].astype(f32)
    out_ref[...] = mine[...]
    send.finish()


def tail(attended, whole, gain, w_out, weights, collective_id):
    bf, f32 = jnp.bfloat16, jnp.float32
    vmem = pl.BlockSpec(memory_space=pltpu.VMEM)
    hbm = pl.BlockSpec(memory_space=pl.ANY)
    rows, width = whole.shape
    return pl.pallas_call(
        tail_kernel,
        out_shape=jax.ShapeDtypeStruct((rows, width // 4), f32),
        in_specs=[vmem, vmem, vmem, hbm, hbm],
        out_specs=vmem,
        scratch_shapes=[
            pltpu.VMEM(w_out.shape, bf),
            pltpu.VMEM(weights.shape, bf),
            pltpu.VMEM((rows, width), f32),
            pltpu.VMEM((rows, width), bf),
            pltpu.VMEM((rows, width), bf),
            pltpu.VMEM((rows, 1024), f32),
            pltpu.VMEM((rows, 1024), f32),
            pltpu.VMEM((rows, 1024), bf),
            pltpu.VMEM((rows, 512), f32),
            pltpu.VMEM((3, rows, 512), bf),
            pltpu.VMEM((3, rows, 512), bf),
            pltpu.SemaphoreType.DMA((12,)),
            pltpu.SemaphoreType.DMA((3,)),
            pltpu.SemaphoreType.DMA((3,)),
        ],
        compiler_params=pltpu.CompilerParams(
            collective_id=collective_id, has_side_effects=True, vmem_limit_bytes=48 << 20
        ),
        cost_estimate=pl.CostEstimate(
            flops=5 << 30, bytes_accessed=40 << 20, transcendentals=1 << 18
        ),
    )(attended, whole, gain[None], w_out, weights)


def shards(
    tokens,
    attn_gain,
    w_query,
    w_key,
    w_value,
    w_out,
    mlp_gain,
    w_gate,
    w_up,
    w_down,
    k_cache,
    v_cache,
    prefix_len,
):
    group = lax.axis_index("grp")
    slice_len = k_cache.shape[1]
    start = group * slice_len
    whole = tp_gather(tokens, 0)
    normed = rms_scale(whole, attn_gain).astype(jnp.bfloat16)
    own_len = lax.dynamic_slice_in_dim(prefix_len, group, 1)[0]
    positions = (own_len + jnp.arange(NEW_TOK, dtype=jnp.int32)).astype(jnp.float32)
    inverse = ROPE_BASE ** (-2.0 * jnp.arange(HD // 2, dtype=jnp.float32) / HD)
    angles = positions[None, :] * inverse[:, None]
    cosine, sine = jnp.cos(angles), jnp.sin(angles)
    flat = lambda w: lax.dot_general(
        w, normed, (((0,), (1,)), ((), ())), preferred_element_type=jnp.float32
    )

    def rope(heads):
        heads = heads.reshape(-1, 2, 32, NEW_TOK)
        first, second = heads[:, 0], heads[:, 1]
        turned = [first * cosine - second * sine, second * cosine + first * sine]
        return jnp.stack(turned, axis=1).reshape(-1, HD, NEW_TOK).astype(jnp.bfloat16)

    q = rope(flat(w_query)) * jnp.bfloat16(0.125)
    q = jnp.transpose(q.reshape(2, 4, HD, NEW_TOK), (0, 2, 1, 3)).reshape(128, 1024)
    new = jnp.concatenate(
        [rope(flat(w_key)), flat(w_value).astype(jnp.bfloat16).reshape(2, HD, NEW_TOK)], axis=0
    )
    packed = jnp.concatenate([q, jnp.transpose(new, (1, 0, 2)).reshape(HD, 1024)], axis=0)
    gathered, whole_out = grp_gather(packed, w_out, 1)
    mlp_rows = jnp.concatenate([w_gate, w_up, w_down.T], axis=0)
    mlp_rows, gathered = lax.optimization_barrier((mlp_rows, gathered))
    weights = lax.all_gather(mlp_rows, "grp", axis=0, tiled=False)
    part_o, part_ml, k_next, v_next = shard_attention(
        start[None], prefix_len, gathered, k_cache, v_cache
    )
    own_o, own_ml = own_attention(packed)
    weights, part_o = lax.optimization_barrier((weights, part_o))
    attended = grp_merge(part_o, part_ml, own_o, own_ml, 2)
    result = tail(attended, whole, mlp_gain, whole_out, weights, 3)
    return (result, k_next, v_next)


def solution(mesh):
    placed = (
        P("grp", "tp"),
        P(),
        P(None, "tp"),
        P(None, "tp"),
        P(None, "tp"),
        P("tp", None),
        P(),
        P("grp", "tp"),
        P("grp", "tp"),
        P("tp", "grp"),
        P(None, "grp", "tp"),
        P(None, "grp", "tp"),
        P(),
    )
    return jax.shard_map(
        shards,
        mesh=mesh,
        in_specs=placed,
        out_specs=(P("grp", "tp"), P(None, "grp", "tp"), P(None, "grp", "tp")),
        check_vma=False,
    )
```

```python
import math

import jax
import jax.numpy as jnp
from jax import lax
from jax.experimental import pallas as pl
from jax.experimental.pallas import tpu as pltpu
from jax.sharding import PartitionSpec as P

HD = 64
NEW_TOK = 256
EPS = 1e-05
ROPE_BASE = 500000.0
NEG = -1e30
LOG2E = math.log2(math.e)


def rms_scale(rows, gain):
    rows = rows.astype(jnp.float32)
    return rows * lax.rsqrt(jnp.mean(rows * rows, axis=-1, keepdims=True) + EPS) * gain


def attend(keys, qbd, vta, mask, o_store, ml_ref, width=512):
    blocks = 2048 // width

    def scores(i):
        return jnp.dot(
            keys, qbd[:, i * width : (i + 1) * width], preferred_element_type=jnp.float32
        )

    def soften(s):
        s = jnp.where(mask, s, NEG)
        top = jnp.max(s, axis=0, keepdims=True)
        return top, jnp.exp2((s - top) * LOG2E).astype(jnp.bfloat16)

    def finish(i, top, p):
        kv, first = divmod(i * width, 1024)
        o = jnp.dot(vta[kv], p, preferred_element_type=jnp.float32)
        o_store(kv, pl.ds(first, width), o[:HD])
        for j in range(0, width, 256):
            g = (first + j) // 256
            ml_ref[kv, g : g + 1] = top[:, j : j + 256]
            ml_ref[kv, 4 + g : 5 + g] = o[HD : HD + 1, j : j + 256]

    s, before = scores(0), None
    for i in range(blocks):
        ahead = scores(i + 1) if i + 1 < blocks else None
        now = soften(s)
        if before is not None:
            finish(i - 1, *before)
        before, s = now, ahead
    finish(blocks - 1, *before)


def fill_scratch(q, vt, qbd, vta):
    zero = jnp.zeros((HD, 1024), jnp.bfloat16)
    qbd[0:HD, 0:1024] = q[0:HD]
    qbd[HD : 2 * HD, 0:1024] = zero
    qbd[0:HD, 1024:2048] = zero
    qbd[HD : 2 * HD, 1024:2048] = q[HD : 2 * HD]
    ones = jnp.ones((16, vt.shape[1]), jnp.bfloat16)
    for kv in range(2):
        vta[kv, 0:HD] = vt[kv * HD : (kv + 1) * HD]
        vta[kv, HD : HD + 16] = ones


def flip(x):
    return jnp.transpose(x.astype(jnp.float32)).astype(jnp.bfloat16)


def place_kernel(start_ref, plen_ref, new_ref, k_ref, v_ref, ko_ref, vo_ref):
    r = pl.program_id(0)
    off = plen_ref[r] - start_ref[0]
    span = k_ref.shape[1]
    hit = (off > -NEW_TOK) & (off < span)

    @pl.when(hit)
    def _():
        rows = lax.broadcasted_iota(jnp.int32, (span, NEW_TOK), 0)
        cols = lax.broadcasted_iota(jnp.int32, (span, NEW_TOK), 1)
        pick = (rows - off == cols).astype(jnp.float32).astype(jnp.bfloat16)
        rel = lax.broadcasted_iota(jnp.int32, (span, 128), 0) - off
        inside = (rel >= 0) & (rel < NEW_TOK)
        for first, old, out in ((0, k_ref, ko_ref), (512, v_ref, vo_ref)):
            new = jnp.concatenate(
                [new_ref[0, :, first : first + 256], new_ref[0, :, first + 256 : first + 512]], axis=0
            )
            placed = jnp.dot(pick, flip(new), preferred_element_type=jnp.float32)
            out[0] = jnp.where(inside, placed, old[0].astype(jnp.float32)).astype(jnp.bfloat16)

    @pl.when(jnp.logical_not(hit))
    def _():
        ko_ref[0] = k_ref[0]
        vo_ref[0] = v_ref[0]


def place_new(start, prefix_len, new, k_cache, v_cache):
    reqs, span, width = k_cache.shape
    spec = lambda *shape: pl.BlockSpec((1,) + shape, lambda r, *_: (r,) + (0,) * len(shape))
    return pl.pallas_call(
        place_kernel,
        out_shape=(
            jax.ShapeDtypeStruct(k_cache.shape, k_cache.dtype),
            jax.ShapeDtypeStruct(v_cache.shape, v_cache.dtype),
        ),
        grid_spec=pltpu.PrefetchScalarGridSpec(
            num_scalar_prefetch=2,
            grid=(reqs,),
            in_specs=[spec(64, 1024), spec(span, width), spec(span, width)],
            out_specs=[spec(span, width), spec(span, width)],
        ),
        compiler_params=pltpu.CompilerParams(
            dimension_semantics=("arbitrary",), vmem_limit_bytes=58 << 20
        ),
        cost_estimate=pl.CostEstimate(flops=1 << 28, bytes_accessed=20 << 20, transcendentals=0),
    )(start, prefix_len, new, k_cache, v_cache)


def own_kernel(q_ref, o_ref, ml_ref, qbd, vta):
    new = jnp.concatenate([q_ref[64:96], q_ref[160:192]], axis=0)
    part = lambda i: new[:, i * 256 : (i + 1) * 256]
    heads = jnp.concatenate([q_ref[0:64], q_ref[96:160]], axis=0)
    fill_scratch(heads, jnp.concatenate([part(2), part(3)], axis=0), qbd, vta)
    keys = flip(jnp.concatenate([part(0), part(1)], axis=0))
    mask = (
        lax.broadcasted_iota(jnp.int32, (NEW_TOK, 512), 0)
        <= lax.broadcasted_iota(jnp.int32, (NEW_TOK, 512), 1) % NEW_TOK
    )

    def store(kv, lanes, o):
        o_ref[pl.ds(kv * HD, HD), lanes] = o

    attend(keys, qbd, vta, mask, store, ml_ref)


def own_attention(packed):
    return pl.pallas_call(
        own_kernel,
        out_shape=(
            jax.ShapeDtypeStruct((128, 1024), jnp.float32),
            jax.ShapeDtypeStruct((2, 8, 256), jnp.float32),
        ),
        scratch_shapes=[
            pltpu.VMEM((128, 2048), jnp.bfloat16),
            pltpu.VMEM((2, HD + 16, NEW_TOK), jnp.bfloat16),
        ],
        compiler_params=pltpu.CompilerParams(vmem_limit_bytes=24 << 20),
        cost_estimate=pl.CostEstimate(flops=1 << 28, bytes_accessed=2 << 20, transcendentals=1 << 19),
    )(packed)


MESH = pl.DeviceIdType.MESH


def grid_place():
    me = lax.axis_index("grp")
    z, y, core = me // 8, (me // 2) % 4, me % 2
    return me, z, y, core


class Sender:
    def __init__(self, axis, send_sems, recv_sems):
        self.axis, self.send_sems, self.recv_sems, self.started = axis, send_sems, recv_sems, []

    def __call__(self, src, dst, device, axis=None):
        i = len(self.started)
        copy = pltpu.make_async_remote_copy(
            src_ref=src,
            dst_ref=dst,
            send_sem=self.send_sems.at[i],
            recv_sem=self.recv_sems.at[i],
            device_id={axis or self.axis: device},
            device_id_type=MESH,
        )
        copy.start()
        self.started.append(copy)
        return copy

    def finish(self):
        for copy in self.started:
            copy.wait_send()


def greet(devices):
    barrier = pltpu.get_barrier_semaphore()
    for axis, device in devices:
        pl.semaphore_signal(barrier, inc=1, device_id={axis: device}, device_id_type=MESH)
    pl.semaphore_wait(barrier, len(devices))


def attend_pair(keys, limits, q, vts, stores):
    masks = [lax.broadcasted_iota(jnp.int32, (keys[0].shape[0], 512), 0) < n for n in limits]

    def scores(i):
        return jnp.dot(
            keys[i // 2], q[:, i * 512 : (i + 1) * 512], preferred_element_type=jnp.float32
        )

    def soften(i, s):
        s = jnp.where(masks[i // 2], s, NEG)
        top = jnp.max(s, axis=0, keepdims=True)
        return top, jnp.exp2((s - top) * LOG2E).astype(jnp.bfloat16)

    def finish(i, top, p):
        o = jnp.dot(vts[i // 2], p, preferred_element_type=jnp.float32)
        stores[i // 2](i % 2, o, top)

    s, before = scores(0), None
    for i in range(4):
        ahead = scores(i + 1) if i < 3 else None
        now = soften(i, s)
        if before is not None:
            finish(i - 1, *before)
        before, s = now, ahead
    finish(3, *before)


def front_kernel(
    plen_ref, x_ref, wo_ref, mw_ref, k_ref, v_ref,
    acc_out, accm_out, new_out, wo_all, mw_all,
    qg, kbuf, vbuf, vta, acc, accm, box, boxm, r1, r1m, qbd,
    local_sems, send_sems, recv_sems, box_send, box_recv, boxm_send, boxm_recv,
):
    me, z, y, c = grid_place()
    x = lax.axis_index("tp")
    sib = me + 1 - 2 * c
    yp, ym, yo = (y + 1) % 4, (y + 3) % 4, (y + 2) % 4
    zp, zm, zo = (z + 1) % 4, (z + 3) % 4, (z + 2) % 4
    right, left, facing = (x + 1) % 4, (x + 3) % 4, (x + 2) % 4
    dev = lambda zz, yy: zz * 8 + yy * 2 + c
    east, west, north, south = dev(z, yp), dev(z, ym), dev(zp, y), dev(zm, y)
    span = k_ref.shape[1]
    start = me * span
    used = []

    def plan(src, dst, device, axis="grp"):
        used.append(
            pltpu.make_async_remote_copy(
                src_ref=src,
                dst_ref=dst,
                send_sem=send_sems.at[len(used)],
                recv_sem=recv_sems.at[len(used)],
                device_id={axis: device},
                device_id_type=MESH,
            )
        )
        return used[-1]

    def run(*copies):
        for copy in copies:
            copy.start()

    def arrive(*copies):
        for copy in copies:
            copy.wait_recv()

    a, b = pl.ds(0, 96), pl.ds(96, 96)
    a0, a1, b0, b1 = pl.ds(0, 48), pl.ds(48, 48), pl.ds(96, 48), pl.ds(144, 48)
    lo, hi, every = pl.ds(0, 2), pl.ds(2, 2), pl.ds(0, 4)

    def ring(src, whole):
        same = lambda device, *index: plan(whole.at[index], whole.at[index], device)
        own = lambda rows, device: plan(src.at[rows], whole.at[z, y, c, rows], device)
        return dict(
            first=[own(a, east), own(b, north), own(a, west), own(b, south)],
            first_on=[
                same(east, z, ym, c, a0),
                same(north, zm, y, c, b0),
                same(west, z, yp, c, a1),
                same(south, zp, y, c, b1),
            ],
            second=[
                same(north, z, every, c, a),
                same(east, every, y, c, b),
                same(south, z, every, c, a),
                same(west, every, y, c, b),
            ],
            second_on=[
                same(north, zm, lo, c, a),
                same(east, lo, ym, c, b),
                same(south, zp, hi, c, a),
                same(west, hi, yp, c, b),
            ],
            over=[
                same(sib, zm, every, c, a),
                same(sib, every, ym, c, b),
                same(sib, zp, every, c, a),
                same(sib, every, yp, c, b),
                same(sib, zo, every, c, a),
                same(sib, every, yo, c, b),
            ],
        )

    q = ring(x_ref, qg)
    same_q = lambda *index: plan(qg.at[index], qg.at[index], sib)
    over_own = plan(x_ref, qg.at[z, y, c], sib)
    over_first = [
        same_q(z, ym, c, a),
        same_q(zm, y, c, b),
        same_q(z, yp, c, a),
        same_q(zp, y, c, b),
        same_q(z, yo, c, a),
        same_q(zo, y, c, b),
    ]
    m = ring(mw_ref, mw_all)
    same_m = lambda *index: plan(mw_all.at[index], mw_all.at[index], sib)
    over_m = [same_m(z, every, c, a), same_m(every, y, c, b)]
    share = wo_ref.shape[0] // 2
    mine = pl.ds(pl.multiple_of(c * share, share), share)
    mine0 = pl.ds(pl.multiple_of(c * share, share // 2), share // 2)
    mine1 = pl.ds(pl.multiple_of(c * share + share // 2, share // 2), share // 2)
    same_w = lambda device, axis, *index: plan(wo_all.at[index], wo_all.at[index], device, axis)
    w_first = [
        plan(wo_ref.at[mine], wo_all.at[x, mine], right, "tp"),
        plan(wo_ref.at[mine], wo_all.at[x, mine], left, "tp"),
    ]
    w_on = [same_w(right, "tp", left, mine0), same_w(left, "tp", right, mine1)]
    w_over = [
        same_w(sib, "grp", left, mine),
        same_w(sib, "grp", right, mine),
        same_w(sib, "grp", facing, mine),
    ]
    locals_ = [
        pltpu.make_async_copy(src, dst, local_sems.at[i])
        for i, (src, dst) in enumerate(
            (
                (k_ref, kbuf),
                (v_ref, vbuf),
                (x_ref, qg.at[z, y, c]),
                (mw_ref, mw_all.at[z, y, c]),
                (wo_ref, wo_all.at[x]),
                (qg.at[:, :, :, pl.ds(64, 32)], new_out.at[:, :, :, pl.ds(0, 32)]),
                (qg.at[:, :, :, pl.ds(160, 32)], new_out.at[:, :, :, pl.ds(32, 32)]),
                (acc, acc_out),
                (accm, accm_out),
            )
        )
    ]
    run(*locals_[:5])
    greet(
        [("grp", i) for i in (east, west, north, south, sib)] + [("tp", right), ("tp", left)]
    )
    run(*q["first"], over_own, *w_first)
    locals_[1].wait()

    def prepare(r, carry):
        vt = flip(vbuf[r])
        ones = jnp.ones((16, span), jnp.bfloat16)
        for kv in range(2):
            vta[r, kv, 0:HD] = vt[kv * HD : (kv + 1) * HD]
            vta[r, kv, HD : HD + 16] = ones
        return carry

    lax.fori_loop(0, 32, prepare, 0)
    qbd[...] = jnp.zeros_like(qbd)
    locals_[0].wait()
    locals_[2].wait()
    over_own.wait_recv()

    def unit(step, kv, zz, yy):
        cores = (c, 1 - c)
        reqs = [(zz * 4 + yy) * 2 + cc for cc in cores]
        half = pl.ds(pl.multiple_of(kv * HD, HD), HD)
        q_rows = pl.ds(pl.multiple_of(kv * 96, 96), HD)
        for role in range(2):
            qbd[kv, half, role * 1024 : (role + 1) * 1024] = qg[zz, yy, cores[role], q_rows]

        def keep(o_ref, m_ref):
            def store(block, o, top):
                o_ref[zz, yy, half, pl.ds(block * 512, 512)] = o[:HD].astype(jnp.bfloat16)
                for j in range(2):
                    g = block * 2 + j
                    m_ref[zz, yy, kv, g : g + 1] = top[:, j * 256 : (j + 1) * 256]
                    m_ref[zz, yy, kv, 4 + g : 5 + g] = o[HD : HD + 1, j * 256 : (j + 1) * 256]

            return store

        attend_pair(
            [kbuf[r] for r in reqs],
            [plen_ref[r] - start for r in reqs],
            qbd.at[kv],
            [vta[r, kv] for r in reqs],
            [keep(acc, accm), keep(box, boxm)],
        )
        run(*ship(step, kv, zz, yy))

    def ship(step, kv, zz, yy):
        half = pl.ds(pl.multiple_of(kv * HD, HD), HD)
        to = dict(device_id={"grp": sib}, device_id_type=MESH)
        return (
            pltpu.make_async_remote_copy(
                src_ref=box.at[zz, yy, half],
                dst_ref=r1.at[zz, yy, half],
                send_sem=box_send.at[step],
                recv_sem=box_recv.at[step],
                **to,
            ),
            pltpu.make_async_remote_copy(
                src_ref=boxm.at[zz, yy, kv],
                dst_ref=r1m.at[zz, yy, kv],
                send_sem=boxm_send.at[step],
                recv_sem=boxm_recv.at[step],
                **to,
            ),
        )

    turn = lambda i: 3 * i - 5 * (i // 2) - 2 * (i // 3)

    def near_place(s):
        kv, d = s % 2, turn(s // 2)
        return kv, (z + kv * d) % 4, (y + (1 - kv) * d) % 4

    def far_place(s):
        d, kv, j = turn(1 + s // 8), (s // 4) % 2, s % 4
        zz = (1 - kv) * ((z + d) % 4) + kv * ((z + j) % 4)
        yy = (1 - kv) * ((y + j) % 4) + kv * ((y + d) % 4)
        return kv, zz, yy

    def near(s, carry):
        @pl.when(s == 1)
        def _():
            for i in range(4):
                q["first"][i].wait_recv()
                run(q["first_on"][i], over_first[i])

        @pl.when(s == 2)
        def _():
            arrive(*over_first[:4])

        @pl.when(s == 4)
        def _():
            arrive(q["first_on"][0], q["first_on"][2])
            run(q["second"][0], q["second"][2], over_first[4])
            arrive(q["first_on"][1], q["first_on"][3])
            run(q["second"][1], q["second"][3], over_first[5])

        @pl.when(s == 6)
        def _():
            arrive(*over_first[4:])

        unit(s, *near_place(s))
        return carry

    lax.fori_loop(0, 8, near, 0)

    def far(s, carry):
        @pl.when(s == 0)
        def _():
            for i in range(4):
                q["second"][i].wait_recv()
                run(q["second_on"][i], q["over"][i])
            locals_[3].wait()
            locals_[4].wait()
            run(*m["first"])
            for i in range(2):
                w_first[i].wait_recv()
                run(w_on[i], w_over[i])
            arrive(q["over"][0])

        @pl.when(s == 4)
        def _():
            arrive(q["over"][1])
            for i in range(4):
                m["first"][i].wait_recv()
                run(m["first_on"][i])

        @pl.when(s == 8)
        def _():
            arrive(q["over"][2])
            arrive(*q["second_on"])
            run(q["over"][4], q["over"][5])
            arrive(*m["first_on"])
            run(*m["second"], *over_m)

        @pl.when(s == 12)
        def _():
            arrive(q["over"][3])

        @pl.when(s == 16)
        def _():
            arrive(q["over"][4])

        @pl.when(s == 20)
        def _():
            arrive(q["over"][5])
            arrive(*w_on)
            run(w_over[2])
            for i in range(4):
                m["second"][i].wait_recv()
                run(m["second_on"][i], m["over"][i])

        unit(8 + s, *far_place(s))
        return carry

    lax.fori_loop(0, 24, far, 0)
    run(locals_[5], locals_[6])

    def near_arrived(s, carry):
        for copy in ship(s, *near_place(s)):
            copy.wait_recv()
        return carry

    def far_arrived(s, carry):
        for copy in ship(8 + s, *far_place(s)):
            copy.wait_recv()
        return carry

    lax.fori_loop(0, 8, near_arrived, 0)
    lax.fori_loop(0, 24, far_arrived, 0)

    def core_merge(i, carry):
        zz, yy = i // 4, i % 4
        for kv in range(2):
            stat = lambda ref: (ref[zz, yy, kv, 0:4], ref[zz, yy, kv, 4:8])
            weights, top, total = merge_stats([stat(accm), stat(r1m)])
            accm[zz, yy, kv, 0:4] = top
            accm[zz, yy, kv, 4:8] = total
            for g in range(4):
                here = (zz, yy, pl.ds(kv * HD, HD), pl.ds(g * 256, 256))
                acc[here] = blend([acc[here], r1[here]], weights, g).astype(jnp.bfloat16)
        return carry

    lax.fori_loop(0, 16, core_merge, 0)
    run(locals_[7], locals_[8])
    arrive(*m["second_on"])
    run(m["over"][4], m["over"][5])
    arrive(*over_m, *m["over"], *w_over)
    for copy in used:
        copy.wait_send()

    def near_sent(s, carry):
        for copy in ship(s, *near_place(s)):
            copy.wait_send()
        return carry

    def far_sent(s, carry):
        for copy in ship(8 + s, *far_place(s)):
            copy.wait_send()
        return carry

    lax.fori_loop(0, 8, near_sent, 0)
    lax.fori_loop(0, 24, far_sent, 0)
    for copy in locals_[5:]:
        copy.wait()


def front(prefix_len, packed, w_out, mlp_rows, k_cache, v_cache, collective_id):
    bf, f32 = jnp.bfloat16, jnp.float32
    hbm = pl.BlockSpec(memory_space=pl.ANY)
    vmem = pl.BlockSpec(memory_space=pltpu.VMEM)
    reqs, span, width = k_cache.shape
    acc, new, wo_all, mw_all, accm = pl.pallas_call(
        lambda p, x, wo, mw, k, v, o0, o1, o2, o3, o4, *rest: front_kernel(
            p, x, wo, mw, k, v, o0, o4, o1, o2, o3, *rest
        ),
        out_shape=(
            jax.ShapeDtypeStruct((4, 4, 128, 1024), bf),
            jax.ShapeDtypeStruct((4, 4, 2, 64, 1024), bf),
            jax.ShapeDtypeStruct((4,) + w_out.shape, bf),
            jax.ShapeDtypeStruct((4, 4, 2) + mlp_rows.shape, bf),
            jax.ShapeDtypeStruct((4, 4, 2, 8, 256), f32),
        ),
        in_specs=[pl.BlockSpec(memory_space=pltpu.SMEM), vmem, vmem, vmem, hbm, hbm],
        out_specs=(hbm,) * 5,
        scratch_shapes=[
            pltpu.VMEM((4, 4, 2, 192, 1024), bf),
            pltpu.VMEM(k_cache.shape, bf),
            pltpu.VMEM(k_cache.shape, bf),
            pltpu.VMEM((reqs, 2, HD + 16, span), bf),
            pltpu.VMEM((4, 4, 128, 1024), bf),
            pltpu.VMEM((4, 4, 2, 8, 256), f32),
            pltpu.VMEM((4, 4, 128, 1024), bf),
            pltpu.VMEM((4, 4, 2, 8, 256), f32),
            pltpu.VMEM((4, 4, 128, 1024), bf),
            pltpu.VMEM((4, 4, 2, 8, 256), f32),
            pltpu.VMEM((2, 128, 2048), bf),
            pltpu.SemaphoreType.DMA((9,)),
            pltpu.SemaphoreType.DMA((64,)),
            pltpu.SemaphoreType.DMA((64,)),
            pltpu.SemaphoreType.DMA((32,)),
            pltpu.SemaphoreType.DMA((32,)),
            pltpu.SemaphoreType.DMA((32,)),
            pltpu.SemaphoreType.DMA((32,)),
        ],
        compiler_params=pltpu.CompilerParams(
            collective_id=collective_id, has_side_effects=True, vmem_limit_bytes=60 << 20
        ),
        cost_estimate=pl.CostEstimate(
            flops=20 << 30, bytes_accessed=60 << 20, transcendentals=reqs * 2048 * span
        ),
    )(prefix_len, packed, w_out, mlp_rows, k_cache, v_cache)
    return acc, accm, new.reshape(reqs, 64, 1024), wo_all.reshape(-1, w_out.shape[1]), mw_all.reshape(
        (reqs,) + mlp_rows.shape
    )


def tp_gather_kernel(x_ref, out_ref, local_sem, send_sems, recv_sems):
    me = lax.axis_index("tp")
    right, left = (me + 1) % 4, (me + 3) % 4
    rows, width = x_ref.shape
    send = Sender("tp", send_sems, recv_sems)
    cols = lambda i: pl.ds(pl.multiple_of(i * width, width), width)
    top, low = pl.ds(0, rows // 2), pl.ds(rows // 2, rows // 2)
    own = pltpu.make_async_copy(x_ref, out_ref.at[:, cols(me)], local_sem)
    own.start()
    greet((("tp", right), ("tp", left)))
    p = send(x_ref, out_ref.at[:, cols(me)], right)
    m = send(x_ref, out_ref.at[:, cols(me)], left)
    p.wait_recv()
    ref = out_ref.at[top, cols(left)]
    fp = send(ref, ref, right)
    m.wait_recv()
    ref = out_ref.at[low, cols(right)]
    fm = send(ref, ref, left)
    fp.wait_recv()
    fm.wait_recv()
    own.wait()
    send.finish()


def tp_gather(x, collective_id):
    rows, width = x.shape
    return pl.pallas_call(
        tp_gather_kernel,
        out_shape=jax.ShapeDtypeStruct((rows, 4 * width), x.dtype),
        in_specs=[pl.BlockSpec(memory_space=pltpu.VMEM)],
        out_specs=pl.BlockSpec(memory_space=pl.ANY),
        scratch_shapes=[
            pltpu.SemaphoreType.DMA,
            pltpu.SemaphoreType.DMA((4,)),
            pltpu.SemaphoreType.DMA((4,)),
        ],
        compiler_params=pltpu.CompilerParams(collective_id=collective_id, has_side_effects=True),
        cost_estimate=pl.CostEstimate(flops=0, bytes_accessed=30 << 20, transcendentals=0),
    )(x)


def merge_stats(parts):
    top = parts[0][0]
    for m, _ in parts[1:]:
        top = jnp.maximum(top, m)
    weights = [jnp.exp2((m - top) * LOG2E) for m, _ in parts]
    total = weights[0] * parts[0][1]
    for w, (_, l) in zip(weights[1:], parts[1:]):
        total = total + w * l
    return weights, top, total


def blend(outs, weights, g):
    acc = outs[0].astype(jnp.float32) * weights[0][g : g + 1]
    for o, w in zip(outs[1:], weights[1:]):
        acc = acc + o.astype(jnp.float32) * w[g : g + 1]
    return acc


def merge_into(acc, accm, others, index, kv, picks):
    stat = lambda ref, i: (ref[i + (pl.ds(0, 4),)], ref[i + (pl.ds(4, 4),)])
    mine = index + (kv,)
    weights, top, total = merge_stats(
        [stat(accm, mine)] + [stat(m, pick) for (_, m), pick in zip(others, picks)]
    )
    accm[mine + (pl.ds(0, 4),)] = top
    accm[mine + (pl.ds(4, 4),)] = total
    for g in range(4):
        lanes = pl.ds(g * 256, 256)
        here = index + (pl.ds(kv * HD, HD), lanes)
        outs = [acc[here]] + [o[pick + (pl.ds(0, HD), lanes)] for (o, _), pick in zip(others, picks)]
        acc[here] = blend(outs, weights, g).astype(jnp.bfloat16)


def grp_merge_kernel(
    o_ref, ml_ref, own_o_ref, own_ml_ref, out_ref,
    acc, accm, ra, ram, rb, rbm, r3, r3m, att, local_sems, send_sems, recv_sems,
):
    me, z, y, c = grid_place()
    yp, ym, yo = (y + 1) % 4, (y + 3) % 4, (y + 2) % 4
    zp, zm, zo = (z + 1) % 4, (z + 3) % 4, (z + 2) % 4
    dev = lambda zz, yy: zz * 8 + yy * 2 + c
    east, west, north, south = dev(z, yp), dev(z, ym), dev(zp, y), dev(zm, y)
    far_y, far_z = dev(z, yo), dev(zo, y)
    send = Sender("grp", send_sems, recv_sems)
    loads = [
        pltpu.make_async_copy(o_ref, acc, local_sems.at[0]),
        pltpu.make_async_copy(ml_ref, accm, local_sems.at[1]),
    ]
    for load in loads:
        load.start()
    x = lax.axis_index("tp")
    right, left = (x + 1) % 4, (x + 3) % 4
    greet(
        [("grp", i) for i in (east, west, north, south, far_y, far_z)]
        + [("tp", right), ("tp", left)]
    )
    for load in loads:
        load.wait()
    lo, hi = pl.ds(0, 2), pl.ds(2, 2)
    ka, kb = pl.ds(0, HD), pl.ds(HD, HD)

    def ship_a(zs, yy, slot, device):
        return (
            send(acc.at[zs, yy, ka], ra.at[slot], device),
            send(accm.at[zs, yy, 0], ram.at[slot], device),
        )

    def ship_b(zz, ys, slot, device):
        return (
            send(acc.at[zz, ys, kb], rb.at[slot], device),
            send(accm.at[zz, ys, 1], rbm.at[slot], device),
        )

    def arrived(pair):
        pair[0].wait_recv()
        pair[1].wait_recv()

    axp = ship_a(lo, yo, 0, east)
    bxp = ship_b(zo, lo, 0, north)
    axm = ship_a(hi, yo, 1, west)
    bxm = ship_b(zo, hi, 1, south)
    app = ship_a(hi, yp, 2, east)
    bpp = ship_b(zp, hi, 2, north)
    apm = ship_a(lo, ym, 3, west)
    bpm = ship_b(zm, lo, 3, south)

    def fold_a(base, yy, slots):
        def body(i, carry):
            merge_into(acc, accm, [(ra, ram)] * len(slots), (base + i, yy), 0, [(s, i) for s in slots])
            return carry

        lax.fori_loop(0, 2, body, 0)

    def fold_b(zz, base, slots):
        def body(i, carry):
            merge_into(acc, accm, [(rb, rbm)] * len(slots), (zz, base + i), 1, [(s, i) for s in slots])
            return carry

        lax.fori_loop(0, 2, body, 0)

    arrived(axp)
    fold_a(0, yp, [0])
    amp = ship_a(lo, yp, 4, east)
    arrived(bxp)
    fold_b(zp, 0, [0])
    bmp = ship_b(zp, lo, 4, north)
    arrived(axm)
    fold_a(2, ym, [1])
    amm = ship_a(hi, ym, 5, west)
    arrived(bxm)
    fold_b(zm, 2, [1])
    bmm = ship_b(zm, hi, 5, south)
    arrived(app)
    arrived(apm)
    arrived(bpp)
    arrived(bpm)
    arrived(amp)
    fold_a(0, y, [3, 4])
    arrived(amm)
    fold_a(2, y, [2, 5])
    arrived(bmp)
    fold_b(z, 0, [3, 4])
    arrived(bmm)
    fold_b(z, 2, [2, 5])

    last = []
    for slot, (zz, device) in enumerate(((zo, far_z), (zp, north), (zm, south))):
        last.append(send(acc.at[zz, y, ka], r3.at[0, slot], device))
        last.append(send(accm.at[zz, y, 0], r3m.at[0, slot], device))
    for slot, (yy, device) in enumerate(((yo, far_y), (yp, east), (ym, west))):
        last.append(send(acc.at[z, yy, kb], r3.at[1, slot], device))
        last.append(send(accm.at[z, yy, 1], r3m.at[1, slot], device))
    for copy in last:
        copy.wait_recv()
    for kv in range(2):
        stat = lambda ref, i: (ref[i + (pl.ds(0, 4),)], ref[i + (pl.ds(4, 4),)])
        parts = [stat(own_ml_ref, (kv,)), stat(accm, (z, y, kv))]
        parts += [stat(r3m, (kv, s)) for s in range(3)]
        weights, _, total = merge_stats(parts)
        scale = 1.0 / total
        weights = [w * scale for w in weights]
        rows = pl.ds(kv * HD, HD)
        for pair in range(2):
            heads = []
            for g in (2 * pair, 2 * pair + 1):
                lanes = pl.ds(g * 256, 256)
                outs = [own_o_ref[rows, lanes], acc[z, y, rows, lanes]]
                outs += [r3[kv, s, :, lanes] for s in range(3)]
                heads.append(blend(outs, weights, g))
            block = jnp.transpose(jnp.concatenate(heads, axis=0)).astype(jnp.bfloat16)
            att[:, pl.ds((kv * 2 + pair) * 128, 128)] = block
    rows, width = att.shape
    cols = lambda i: pl.ds(pl.multiple_of(i * width, width), width)
    upper, lower = pl.ds(0, rows // 2), pl.ds(rows // 2, rows // 2)
    own = pltpu.make_async_copy(att, out_ref.at[:, cols(x)], local_sems.at[5])
    own.start()
    p = send(att, out_ref.at[:, cols(x)], right, "tp")
    m = send(att, out_ref.at[:, cols(x)], left, "tp")
    p.wait_recv()
    ref = out_ref.at[upper, cols(left)]
    fp = send(ref, ref, right, "tp")
    m.wait_recv()
    ref = out_ref.at[lower, cols(right)]
    fm = send(ref, ref, left, "tp")
    fp.wait_recv()
    fm.wait_recv()
    own.wait()
    send.finish()


def grp_merge(part_o, part_ml, own_o, own_ml, collective_id):
    bf, f32 = jnp.bfloat16, jnp.float32
    any_spec = pl.BlockSpec(memory_space=pl.ANY)
    vmem = pl.BlockSpec(memory_space=pltpu.VMEM)
    copies = 24 + 12 + 4
    return pl.pallas_call(
        grp_merge_kernel,
        out_shape=jax.ShapeDtypeStruct((NEW_TOK, 2048), bf),
        in_specs=[any_spec, any_spec, vmem, vmem],
        out_specs=any_spec,
        scratch_shapes=[
            pltpu.VMEM((4, 4, 128, 1024), bf),
            pltpu.VMEM((4, 4, 2, 8, 256), f32),
            pltpu.VMEM((6, 2, HD, 1024), bf),
            pltpu.VMEM((6, 2, 8, 256), f32),
            pltpu.VMEM((6, 2, HD, 1024), bf),
            pltpu.VMEM((6, 2, 8, 256), f32),
            pltpu.VMEM((2, 3, HD, 1024), bf),
            pltpu.VMEM((2, 3, 8, 256), f32),
            pltpu.VMEM((NEW_TOK, 512), bf),
            pltpu.SemaphoreType.DMA((6,)),
            pltpu.SemaphoreType.DMA((copies,)),
            pltpu.SemaphoreType.DMA((copies,)),
        ],
        compiler_params=pltpu.CompilerParams(
            collective_id=collective_id, has_side_effects=True, vmem_limit_bytes=58 << 20
        ),
        cost_estimate=pl.CostEstimate(flops=0, bytes_accessed=130 << 20, transcendentals=0),
    )(
        part_o,
        part_ml,
        own_o,
        own_ml,
    )


def tail_kernel(
    att_ref, tok_ref, gain_ref, wo_ref, w_ref, out_ref,
    wo, wb, acc, firsts, n2, gate, up, hid, mine, outbox, inbox, load_sems, send_sems, recv_sems,
):
    me = lax.axis_index("tp")
    right, left, facing = (me + 1) % 4, (me + 3) % 4, (me + 2) % 4
    send = Sender("tp", send_sems, recv_sems)
    wo_part = lambda i: pltpu.make_async_copy(
        wo_ref.at[pl.ds(i * 512, 512)], wo.at[pl.ds(i * 512, 512)], load_sems.at[i]
    )
    w_part = lambda i: pltpu.make_async_copy(
        w_ref.at[pl.ds(i * 4, 4)], wb.at[pl.ds(i * 4, 4)], load_sems.at[4 + i]
    )
    for i in range(4):
        wo_part(i).start()
    for i in range(8):
        w_part(i).start()
    greet((("tp", right), ("tp", left), ("tp", facing)))
    f32, bf = jnp.float32, jnp.bfloat16
    acc[...] = tok_ref[...].astype(f32)
    for i in range(4):
        wo_part(i).wait()

        def project(n, carry, i=i):
            lanes = pl.ds(pl.multiple_of(n * 512, 512), 512)
            acc[:, lanes] += jnp.dot(
                att_ref[:, i * 512 : (i + 1) * 512],
                wo[i * 512 : (i + 1) * 512, lanes],
                preferred_element_type=f32,
            )
            return carry

        lax.fori_loop(0, 4, project, 0)

    def norm(i, carry):
        rows = pl.ds(pl.multiple_of(i * 32, 32), 32)
        first = acc[rows].astype(bf)
        firsts[rows] = first
        n2[rows] = rms_scale(first, gain_ref[...]).astype(bf)
        return carry

    lax.fori_loop(0, NEW_TOK // 32, norm, 0)
    gate[...] = jnp.zeros_like(gate)
    up[...] = jnp.zeros_like(up)
    for i in range(8):
        w_part(i).wait()

        def widen(n, carry, i=i):
            lanes = pl.ds(pl.multiple_of(n * 512, 512), 512)
            x = n2[:, i * 256 : (i + 1) * 256]
            for total, at in ((gate, 0), (up, 64)):
                w = wb[4 * i : 4 * i + 4, at : at + 64, lanes].reshape(256, 512)
                total[:, lanes] += jnp.dot(x, w, preferred_element_type=f32)
            return carry

        lax.fori_loop(0, 2, widen, 0)

    def squash(i, carry):
        rows = pl.ds(pl.multiple_of(i * 32, 32), 32)
        v = gate[rows]
        hid[rows] = (v / (1.0 + jnp.exp(-v)) * up[rows]).astype(bf)
        return carry

    lax.fori_loop(0, NEW_TOK // 32, squash, 0)

    def terms(target):
        w = wb[pl.ds(target * 8, 8), 128:192].reshape(512, 1024)
        return lax.dot_general(
            hid[...], w, (((1,), (1,)), ((), ())), preferred_element_type=f32
        )

    for slot, target in enumerate((facing, right, left)):
        outbox[slot] = terms(target).astype(bf)
        send(outbox.at[slot], inbox.at[slot], target)
    cols = pl.ds(pl.multiple_of(me * 512, 512), 512)
    mine[...] = firsts[:, cols].astype(f32) + terms(me)
    for copy in send.started:
        copy.wait_recv()
    for slot in range(3):
        mine[...] += inbox[slot].astype(f32)
    out_ref[...] = mine[...]
    send.finish()


def tail(attended, whole, gain, w_out, weights, collective_id):
    bf, f32 = jnp.bfloat16, jnp.float32
    vmem = pl.BlockSpec(memory_space=pltpu.VMEM)
    hbm = pl.BlockSpec(memory_space=pl.ANY)
    rows, width = whole.shape
    return pl.pallas_call(
        tail_kernel,
        out_shape=jax.ShapeDtypeStruct((rows, width // 4), f32),
        in_specs=[vmem, vmem, vmem, hbm, hbm],
        out_specs=vmem,
        scratch_shapes=[
            pltpu.VMEM(w_out.shape, bf),
            pltpu.VMEM(weights.shape, bf),
            pltpu.VMEM((rows, width), f32),
            pltpu.VMEM((rows, width), bf),
            pltpu.VMEM((rows, width), bf),
            pltpu.VMEM((rows, 1024), f32),
            pltpu.VMEM((rows, 1024), f32),
            pltpu.VMEM((rows, 1024), bf),
            pltpu.VMEM((rows, 512), f32),
            pltpu.VMEM((3, rows, 512), bf),
            pltpu.VMEM((3, rows, 512), bf),
            pltpu.SemaphoreType.DMA((12,)),
            pltpu.SemaphoreType.DMA((3,)),
            pltpu.SemaphoreType.DMA((3,)),
        ],
        compiler_params=pltpu.CompilerParams(
            collective_id=collective_id, has_side_effects=True, vmem_limit_bytes=48 << 20
        ),
        cost_estimate=pl.CostEstimate(
            flops=5 << 30, bytes_accessed=40 << 20, transcendentals=1 << 18
        ),
    )(attended, whole, gain[None], w_out, weights)


def shards(
    tokens,
    attn_gain,
    w_query,
    w_key,
    w_value,
    w_out,
    mlp_gain,
    w_gate,
    w_up,
    w_down,
    k_cache,
    v_cache,
    prefix_len,
):
    group = lax.axis_index("grp")
    slice_len = k_cache.shape[1]
    start = group * slice_len
    whole = tp_gather(tokens, 0)
    normed = rms_scale(whole, attn_gain).astype(jnp.bfloat16)
    own_len = lax.dynamic_slice_in_dim(prefix_len, group, 1)[0]
    positions = (own_len + jnp.arange(NEW_TOK, dtype=jnp.int32)).astype(jnp.float32)
    inverse = ROPE_BASE ** (-2.0 * jnp.arange(HD // 2, dtype=jnp.float32) / HD)
    angles = positions[None, :] * inverse[:, None]
    cosine, sine = jnp.cos(angles), jnp.sin(angles)
    flat = lambda w: lax.dot_general(
        w, normed, (((0,), (1,)), ((), ())), preferred_element_type=jnp.float32
    )

    def rope(heads):
        heads = heads.reshape(-1, 2, 32, NEW_TOK)
        first, second = heads[:, 0], heads[:, 1]
        turned = [first * cosine - second * sine, second * cosine + first * sine]
        return jnp.stack(turned, axis=1).reshape(-1, HD, NEW_TOK).astype(jnp.bfloat16)

    q = rope(flat(w_query)) * jnp.bfloat16(0.125)
    q = jnp.transpose(q.reshape(2, 4, HD, NEW_TOK), (0, 2, 1, 3)).reshape(128, 1024)
    new = jnp.concatenate(
        [rope(flat(w_key)), flat(w_value).astype(jnp.bfloat16).reshape(2, HD, NEW_TOK)], axis=0
    )
    new = jnp.transpose(new, (1, 0, 2)).reshape(HD, 1024)
    packed = jnp.concatenate([q[:64], new[:32], q[64:], new[32:]], axis=0)
    mlp_rows = jnp.concatenate([w_gate, w_up, w_down.T], axis=0)
    part_o, part_ml, new_rows, whole_out, weights = front(
        prefix_len, packed, w_out, mlp_rows, k_cache, v_cache, 1
    )
    k_next, v_next = place_new(start[None], prefix_len, new_rows, k_cache, v_cache)
    own_o, own_ml = own_attention(packed)
    attended = grp_merge(part_o, part_ml, own_o, own_ml, 2)
    result = tail(attended, whole, mlp_gain, whole_out, weights, 3)
    return (result, k_next, v_next)


def solution(mesh):
    placed = (
        P("grp", "tp"),
        P(),
        P(None, "tp"),
        P(None, "tp"),
        P(None, "tp"),
        P("tp", None),
        P(),
        P("grp", "tp"),
        P("grp", "tp"),
        P("tp", "grp"),
        P(None, "grp", "tp"),
        P(None, "grp", "tp"),
        P(),
    )
    return jax.shard_map(
        shards,
        mesh=mesh,
        in_specs=placed,
        out_specs=(P("grp", "tp"), P(None, "grp", "tp"), P(None, "grp", "tp")),
        check_vma=False,
    )
```

```python
import math

import jax
import jax.numpy as jnp
from jax import lax
from jax.experimental import pallas as pl
from jax.experimental.pallas import tpu as pltpu
from jax.sharding import PartitionSpec as P

HD = 64
NEW_TOK = 256
EPS = 1e-05
ROPE_BASE = 500000.0
NEG = -1e30
LOG2E = math.log2(math.e)


def rms_scale(rows, gain):
    rows = rows.astype(jnp.float32)
    return rows * lax.rsqrt(jnp.mean(rows * rows, axis=-1, keepdims=True) + EPS) * gain


def attend(keys, qbd, vta, mask, o_store, ml_ref, width=512):
    blocks = 2048 // width

    def scores(i):
        return jnp.dot(
            keys, qbd[:, i * width : (i + 1) * width], preferred_element_type=jnp.float32
        )

    def soften(s):
        s = jnp.where(mask, s, NEG)
        top = jnp.max(s, axis=0, keepdims=True)
        return top, jnp.exp2((s - top) * LOG2E).astype(jnp.bfloat16)

    def finish(i, top, p):
        kv, first = divmod(i * width, 1024)
        o = jnp.dot(vta[kv], p, preferred_element_type=jnp.float32)
        o_store(kv, pl.ds(first, width), o[:HD])
        for j in range(0, width, 256):
            g = (first + j) // 256
            ml_ref[kv, g : g + 1] = top[:, j : j + 256]
            ml_ref[kv, 4 + g : 5 + g] = o[HD : HD + 1, j : j + 256]

    s, before = scores(0), None
    for i in range(blocks):
        ahead = scores(i + 1) if i + 1 < blocks else None
        now = soften(s)
        if before is not None:
            finish(i - 1, *before)
        before, s = now, ahead
    finish(blocks - 1, *before)


def fill_scratch(q, vt, qbd, vta):
    zero = jnp.zeros((HD, 1024), jnp.bfloat16)
    qbd[0:HD, 0:1024] = q[0:HD]
    qbd[HD : 2 * HD, 0:1024] = zero
    qbd[0:HD, 1024:2048] = zero
    qbd[HD : 2 * HD, 1024:2048] = q[HD : 2 * HD]
    ones = jnp.ones((16, vt.shape[1]), jnp.bfloat16)
    for kv in range(2):
        vta[kv, 0:HD] = vt[kv * HD : (kv + 1) * HD]
        vta[kv, HD : HD + 16] = ones


def flip(x):
    return jnp.transpose(x.astype(jnp.float32)).astype(jnp.bfloat16)


def place_kernel(start_ref, plen_ref, new_ref, k_ref, v_ref, ko_ref, vo_ref, kbuf, vbuf, nbuf, sems):
    reqs, span, _ = k_ref.shape
    each = 4
    pieces = reqs // each
    at = lambda i: pl.ds(i * each, each)
    news = pltpu.make_async_copy(new_ref, nbuf, sems.at[4, 0])
    sets = []
    for row, (src, dst) in enumerate(((k_ref, kbuf), (v_ref, vbuf), (kbuf, ko_ref), (vbuf, vo_ref))):
        sets.append(
            [
                pltpu.make_async_copy(src.at[at(i)], dst.at[at(i)], sems.at[row, i])
                for i in range(pieces)
            ]
        )
    news.start()
    for i in range(pieces):
        sets[0][i].start()
        sets[1][i].start()
    news.wait()

    for i in range(pieces):
        sets[0][i].wait()
        sets[1][i].wait()

        def patch(r, carry):
            off = plen_ref[r] - start_ref[0]

            @pl.when((off > -NEW_TOK) & (off < span))
            def _():
                rows = lax.broadcasted_iota(jnp.int32, (span, NEW_TOK), 0)
                cols = lax.broadcasted_iota(jnp.int32, (span, NEW_TOK), 1)
                pick = (rows - off == cols).astype(jnp.float32).astype(jnp.bfloat16)
                rel = lax.broadcasted_iota(jnp.int32, (span, 128), 0) - off
                inside = (rel >= 0) & (rel < NEW_TOK)
                for first, buf in ((0, kbuf), (512, vbuf)):
                    new = jnp.concatenate(
                        [nbuf[r, :, first : first + 256], nbuf[r, :, first + 256 : first + 512]],
                        axis=0,
                    )
                    placed = jnp.dot(pick, flip(new), preferred_element_type=jnp.float32)
                    old = buf[r].astype(jnp.float32)
                    buf[r] = jnp.where(inside, placed, old).astype(jnp.bfloat16)

            return carry

        lax.fori_loop(i * each, (i + 1) * each, patch, 0)
        sets[2][i].start()
        sets[3][i].start()
    for i in range(pieces):
        sets[2][i].wait()
        sets[3][i].wait()


def place_new(start, prefix_len, new, k_cache, v_cache):
    smem = pl.BlockSpec(memory_space=pltpu.SMEM)
    hbm = pl.BlockSpec(memory_space=pl.ANY)
    return pl.pallas_call(
        place_kernel,
        out_shape=(
            jax.ShapeDtypeStruct(k_cache.shape, k_cache.dtype),
            jax.ShapeDtypeStruct(v_cache.shape, v_cache.dtype),
        ),
        in_specs=[smem, smem, hbm, hbm, hbm],
        out_specs=(hbm, hbm),
        scratch_shapes=[
            pltpu.VMEM(k_cache.shape, k_cache.dtype),
            pltpu.VMEM(v_cache.shape, v_cache.dtype),
            pltpu.VMEM(new.shape, new.dtype),
            pltpu.SemaphoreType.DMA((5, 8)),
        ],
        compiler_params=pltpu.CompilerParams(vmem_limit_bytes=58 << 20),
        cost_estimate=pl.CostEstimate(flops=1 << 28, bytes_accessed=20 << 20, transcendentals=0),
    )(start, prefix_len, new, k_cache, v_cache)


def own_kernel(q_ref, o_ref, ml_ref, qbd, vta):
    new = jnp.concatenate([q_ref[64:96], q_ref[160:192]], axis=0)
    part = lambda i: new[:, i * 256 : (i + 1) * 256]
    heads = jnp.concatenate([q_ref[0:64], q_ref[96:160]], axis=0)
    fill_scratch(heads, jnp.concatenate([part(2), part(3)], axis=0), qbd, vta)
    keys = flip(jnp.concatenate([part(0), part(1)], axis=0))
    mask = (
        lax.broadcasted_iota(jnp.int32, (NEW_TOK, 512), 0)
        <= lax.broadcasted_iota(jnp.int32, (NEW_TOK, 512), 1) % NEW_TOK
    )

    def store(kv, lanes, o):
        o_ref[pl.ds(kv * HD, HD), lanes] = o

    attend(keys, qbd, vta, mask, store, ml_ref)


MESH = pl.DeviceIdType.MESH


def grid_place():
    me = lax.axis_index("grp")
    z, y, core = me // 8, (me // 2) % 4, me % 2
    return me, z, y, core


class Sender:
    def __init__(self, axis, send_sems, recv_sems):
        self.axis, self.send_sems, self.recv_sems, self.started = axis, send_sems, recv_sems, []

    def __call__(self, src, dst, device, axis=None):
        i = len(self.started)
        copy = pltpu.make_async_remote_copy(
            src_ref=src,
            dst_ref=dst,
            send_sem=self.send_sems.at[i],
            recv_sem=self.recv_sems.at[i],
            device_id={axis or self.axis: device},
            device_id_type=MESH,
        )
        copy.start()
        self.started.append(copy)
        return copy

    def finish(self):
        for copy in self.started:
            copy.wait_send()


def greet(devices):
    barrier = pltpu.get_barrier_semaphore()
    for axis, device in devices:
        pl.semaphore_signal(barrier, inc=1, device_id={axis: device}, device_id_type=MESH)
    pl.semaphore_wait(barrier, len(devices))


class Planner:
    def __init__(self, send_sems, recv_sems):
        self.send_sems, self.recv_sems, self.made = send_sems, recv_sems, []

    def __call__(self, src, dst, device, axis="grp"):
        i = len(self.made)
        self.made.append(
            pltpu.make_async_remote_copy(
                src_ref=src,
                dst_ref=dst,
                send_sem=self.send_sems.at[i],
                recv_sem=self.recv_sems.at[i],
                device_id={axis: device},
                device_id_type=MESH,
            )
        )
        return self.made[-1]


def run(*copies):
    for copy in copies:
        copy.start()


def arrive(*copies):
    for copy in copies:
        copy.wait_recv()


def ring(plan, src, whole, full=True):
    me, z, y, c = grid_place()
    sib = me + 1 - 2 * c
    yp, ym, yo = (y + 1) % 4, (y + 3) % 4, (y + 2) % 4
    zp, zm, zo = (z + 1) % 4, (z + 3) % 4, (z + 2) % 4
    dev = lambda zz, yy: zz * 8 + yy * 2 + c
    east, west, north, south = dev(z, yp), dev(z, ym), dev(zp, y), dev(zm, y)
    n = src.shape[0] // 4
    a, b = pl.ds(0, 2 * n), pl.ds(2 * n, 2 * n)
    a0, a1, b0, b1 = (pl.ds(i * n, n) for i in range(4))
    lo, hi, every = pl.ds(0, 2), pl.ds(2, 2), pl.ds(0, 4)
    same = lambda device, *index: plan(whole.at[index], whole.at[index], device)
    own = lambda rows, device: plan(src.at[rows], whole.at[z, y, c, rows], device)
    out = dict(
        first=[own(a, east), own(b, north), own(a, west), own(b, south)],
        first_on=[
            same(east, z, ym, c, a0),
            same(north, zm, y, c, b0),
            same(west, z, yp, c, a1),
            same(south, zp, y, c, b1),
        ],
        second=[
            same(north, z, lo, c, a),
            same(east, lo, y, c, b),
            same(south, z, hi, c, a),
            same(west, hi, y, c, b),
        ],
        second_more=[
            same(north, z, hi, c, a),
            same(east, hi, y, c, b),
            same(south, z, lo, c, a),
            same(west, lo, y, c, b),
        ],
        second_on=[
            same(north, zm, lo, c, a),
            same(east, lo, ym, c, b),
            same(south, zp, hi, c, a),
            same(west, hi, yp, c, b),
        ],
        over=[
            same(sib, zm, lo, c, a),
            same(sib, lo, ym, c, b),
            same(sib, zp, hi, c, a),
            same(sib, hi, yp, c, b),
        ],
        over_more=[
            same(sib, zm, hi, c, a),
            same(sib, hi, ym, c, b),
            same(sib, zp, lo, c, a),
            same(sib, lo, yp, c, b),
        ],
        over_last=[same(sib, zo, every, c, a), same(sib, every, yo, c, b)],
    )
    if full:
        out["over_line"] = [same(sib, z, every, c, a), same(sib, every, y, c, b)]
    return out


def attend_pair(keys, limits, q, vts, stores):
    masks = [lax.broadcasted_iota(jnp.int32, (keys[0].shape[0], 512), 0) < n for n in limits]

    def scores(i):
        return jnp.dot(
            keys[i // 2], q[:, i * 512 : (i + 1) * 512], preferred_element_type=jnp.float32
        )

    def soften(i, s):
        s = jnp.where(masks[i // 2], s, NEG)
        top = jnp.max(s, axis=0, keepdims=True)
        return top, jnp.exp2((s - top) * LOG2E).astype(jnp.bfloat16)

    def finish(i, top, p):
        o = jnp.dot(vts[i // 2], p, preferred_element_type=jnp.float32)
        stores[i // 2](i % 2, o, top)

    s, before = scores(0), None
    for i in range(4):
        ahead = scores(i + 1) if i < 3 else None
        now = soften(i, s)
        if before is not None:
            finish(i - 1, *before)
        before, s = now, ahead
    finish(3, *before)


def front_kernel(
    plen_ref, x_ref, wo_hbm, mw_ref, k_ref, v_ref,
    acc_out, accm_out, new_out, wo_all, mw_all, own_o, own_ml,
    own_q, own_v, wo_ref, qg, kbuf, vbuf, vta, acc, accm, box, boxm, r1, r1m, qbd,
    local_sems, send_sems, recv_sems, box_send, box_recv, boxm_send, boxm_recv,
):
    me, z, y, c = grid_place()
    x = lax.axis_index("tp")
    sib = me + 1 - 2 * c
    yp, ym, yo = (y + 1) % 4, (y + 3) % 4, (y + 2) % 4
    zp, zm, zo = (z + 1) % 4, (z + 3) % 4, (z + 2) % 4
    right, left, facing = (x + 1) % 4, (x + 3) % 4, (x + 2) % 4
    dev = lambda zz, yy: zz * 8 + yy * 2 + c
    east, west, north, south = dev(z, yp), dev(z, ym), dev(zp, y), dev(zm, y)
    span = k_ref.shape[1]
    start = me * span
    plan = Planner(send_sems, recv_sems)
    a, b = pl.ds(0, 96), pl.ds(96, 96)
    q = ring(plan, x_ref, qg, full=False)
    same_q = lambda *index: plan(qg.at[index], qg.at[index], sib)
    over_own = plan(x_ref, qg.at[z, y, c], sib)
    over_first = [
        same_q(z, ym, c, a),
        same_q(zm, y, c, b),
        same_q(z, yp, c, a),
        same_q(zp, y, c, b),
        same_q(z, yo, c, a),
        same_q(zo, y, c, b),
    ]
    m = ring(plan, mw_ref, mw_all)
    share = wo_ref.shape[0] // 2
    mine = pl.ds(pl.multiple_of(c * share, share), share)
    mine0 = pl.ds(pl.multiple_of(c * share, share // 2), share // 2)
    mine1 = pl.ds(pl.multiple_of(c * share + share // 2, share // 2), share // 2)
    same_w = lambda device, axis, *index: plan(wo_all.at[index], wo_all.at[index], device, axis)
    w_first = [
        plan(wo_ref.at[mine], wo_all.at[x, mine], right, "tp"),
        plan(wo_ref.at[mine], wo_all.at[x, mine], left, "tp"),
    ]
    w_on = [same_w(right, "tp", left, mine0), same_w(left, "tp", right, mine1)]
    w_over = [
        same_w(sib, "grp", left, mine),
        same_w(sib, "grp", right, mine),
        same_w(sib, "grp", facing, mine),
    ]
    locals_ = [
        pltpu.make_async_copy(src, dst, local_sems.at[i])
        for i, (src, dst) in enumerate(
            (
                (k_ref, kbuf),
                (v_ref, vbuf),
                (x_ref, qg.at[z, y, c]),
                (mw_ref, mw_all.at[z, y, c]),
                (wo_ref, wo_all.at[x]),
                (qg.at[:, :, :, pl.ds(64, 32)], new_out.at[:, :, :, pl.ds(0, 32)]),
                (qg.at[:, :, :, pl.ds(160, 32)], new_out.at[:, :, :, pl.ds(32, 32)]),
                (acc, acc_out),
                (accm, accm_out),
            )
        )
    ]
    wo_load = pltpu.make_async_copy(wo_hbm, wo_ref, local_sems.at[9])
    run(locals_[1], locals_[2])
    greet(
        [("grp", i) for i in (east, west, north, south, sib)] + [("tp", right), ("tp", left)]
    )
    run(*q["first"], over_own)
    wo_load.start()
    run(locals_[0], locals_[3])
    wo_load.wait()
    run(*w_first, locals_[4])
    own_kernel(x_ref, own_o, own_ml, own_q, own_v)
    locals_[1].wait()
    qbd[...] = jnp.zeros_like(qbd)

    def prepare(r, carry):
        vt = flip(vbuf[r])
        ones = jnp.ones((16, span), jnp.bfloat16)
        for kv in range(2):
            vta[r, kv, 0:HD] = vt[kv * HD : (kv + 1) * HD]
            vta[r, kv, HD : HD + 16] = ones
        return carry

    lax.fori_loop(0, 16, prepare, 0)
    for i in range(4):
        q["first"][i].wait_recv()
        run(q["first_on"][i], over_first[i])
    lax.fori_loop(16, 32, prepare, 0)
    locals_[2].wait()
    arrive(*q["first_on"])
    run(*q["second"], over_first[4], over_first[5], *q["second_more"])
    locals_[0].wait()
    over_own.wait_recv()

    def unit(step, kv, zz, yy):
        cores = (c, 1 - c)
        reqs = [(zz * 4 + yy) * 2 + cc for cc in cores]
        half = pl.ds(pl.multiple_of(kv * HD, HD), HD)
        q_rows = pl.ds(pl.multiple_of(kv * 96, 96), HD)
        for role in range(2):
            qbd[kv, half, role * 1024 : (role + 1) * 1024] = qg[zz, yy, cores[role], q_rows]

        def keep(o_ref, m_ref):
            def store(block, o, top):
                o_ref[zz, yy, half, pl.ds(block * 512, 512)] = o[:HD].astype(jnp.bfloat16)
                for j in range(2):
                    g = block * 2 + j
                    m_ref[zz, yy, kv, g : g + 1] = top[:, j * 256 : (j + 1) * 256]
                    m_ref[zz, yy, kv, 4 + g : 5 + g] = o[HD : HD + 1, j * 256 : (j + 1) * 256]

            return store

        attend_pair(
            [kbuf[r] for r in reqs],
            [plen_ref[r] - start for r in reqs],
            qbd.at[kv],
            [vta[r, kv] for r in reqs],
            [keep(acc, accm), keep(box, boxm)],
        )
        run(*ship(step, kv, zz, yy))

    def ship(step, kv, zz, yy):
        half = pl.ds(pl.multiple_of(kv * HD, HD), HD)
        to = dict(device_id={"grp": sib}, device_id_type=MESH)
        return (
            pltpu.make_async_remote_copy(
                src_ref=box.at[zz, yy, half],
                dst_ref=r1.at[zz, yy, half],
                send_sem=box_send.at[step],
                recv_sem=box_recv.at[step],
                **to,
            ),
            pltpu.make_async_remote_copy(
                src_ref=boxm.at[zz, yy, kv],
                dst_ref=r1m.at[zz, yy, kv],
                send_sem=boxm_send.at[step],
                recv_sem=boxm_recv.at[step],
                **to,
            ),
        )

    turn = lambda i: 3 * i - 5 * (i // 2) - 2 * (i // 3)

    def near_place(s):
        kv, d = s % 2, turn(s // 2)
        return kv, (z + kv * d) % 4, (y + (1 - kv) * d) % 4

    def mid_place(s):
        late, way, j = s // 8, (s % 8) // 2, s % 2
        kv, far_way = way % 2, way // 2
        d = 3 - 2 * far_way
        i = 2 * ((1 - far_way) * late + far_way * (1 - late)) + j
        zz = (1 - kv) * ((z + d) % 4) + kv * i
        yy = (1 - kv) * i + kv * ((y + d) % 4)
        return kv, zz, yy

    def far_place(s):
        kv, i = s // 4, s % 4
        zz = (1 - kv) * ((z + 2) % 4) + kv * i
        yy = (1 - kv) * i + kv * ((y + 2) % 4)
        return kv, zz, yy

    def near(s, carry):
        @pl.when(s == 2)
        def _():
            arrive(*over_first[:4])

        @pl.when(s == 6)
        def _():
            arrive(*over_first[4:])
            for i in range(4):
                q["second"][i].wait_recv()
                run(q["second_on"][i], q["over"][i])

        unit(s, *near_place(s))
        return carry

    lax.fori_loop(0, 8, near, 0)

    def mid(s, carry):
        @pl.when(s == 0)
        def _():
            arrive(*q["over"])

        @pl.when(s == 4)
        def _():
            for i in range(4):
                q["second_more"][i].wait_recv()
                run(q["over_more"][i])
            for i in range(2):
                w_first[i].wait_recv()
                run(w_on[i], w_over[i])
            locals_[3].wait()
            locals_[4].wait()
            run(*m["first"])

        @pl.when(s == 8)
        def _():
            arrive(*q["over_more"])

        @pl.when(s == 10)
        def _():
            arrive(*q["second_on"])
            run(*q["over_last"])
            for i in range(4):
                m["first"][i].wait_recv()
                run(m["first_on"][i])

        @pl.when(s == 12)
        def _():
            arrive(*m["first_on"])
            run(*m["second"], *m["second_more"], *m["over_line"])

        unit(8 + s, *mid_place(s))
        return carry

    lax.fori_loop(0, 16, mid, 0)

    def far(s, carry):
        @pl.when(s == 0)
        def _():
            arrive(*q["over_last"])

        @pl.when(s == 3)
        def _():
            for i in range(4):
                m["second"][i].wait_recv()
                run(m["second_on"][i], m["over"][i])

        @pl.when(s == 6)
        def _():
            for i in range(4):
                m["second_more"][i].wait_recv()
                run(m["over_more"][i])
            arrive(*w_on)
            run(w_over[2])

        unit(24 + s, *far_place(s))
        return carry

    lax.fori_loop(0, 8, far, 0)
    run(locals_[5], locals_[6])

    def near_arrived(s, carry):
        for copy in ship(s, *near_place(s)):
            copy.wait_recv()
        return carry

    def mid_arrived(s, carry):
        for copy in ship(8 + s, *mid_place(s)):
            copy.wait_recv()
        return carry

    def far_arrived(s, carry):
        for copy in ship(24 + s, *far_place(s)):
            copy.wait_recv()
        return carry

    lax.fori_loop(0, 8, near_arrived, 0)
    lax.fori_loop(0, 16, mid_arrived, 0)
    lax.fori_loop(0, 8, far_arrived, 0)

    def core_merge(i, carry):
        zz, yy = i // 4, i % 4
        for kv in range(2):
            stat = lambda ref: (ref[zz, yy, kv, 0:4], ref[zz, yy, kv, 4:8])
            weights, top, total = merge_stats([stat(accm), stat(r1m)])
            accm[zz, yy, kv, 0:4] = top
            accm[zz, yy, kv, 4:8] = total
            for g in range(4):
                here = (zz, yy, pl.ds(kv * HD, HD), pl.ds(g * 256, 256))
                acc[here] = blend([acc[here], r1[here]], weights, g).astype(jnp.bfloat16)
        return carry

    lax.fori_loop(0, 16, core_merge, 0)
    run(locals_[7], locals_[8])
    arrive(*m["second_on"])
    run(*m["over_last"])
    arrive(*m["over_line"], *m["over"], *m["over_more"], *m["over_last"], *w_over)
    for copy in plan.made:
        copy.wait_send()

    def near_sent(s, carry):
        for copy in ship(s, *near_place(s)):
            copy.wait_send()
        return carry

    def mid_sent(s, carry):
        for copy in ship(8 + s, *mid_place(s)):
            copy.wait_send()
        return carry

    def far_sent(s, carry):
        for copy in ship(24 + s, *far_place(s)):
            copy.wait_send()
        return carry

    lax.fori_loop(0, 8, near_sent, 0)
    lax.fori_loop(0, 16, mid_sent, 0)
    lax.fori_loop(0, 8, far_sent, 0)
    for copy in locals_[5:]:
        copy.wait()


def front(prefix_len, packed, w_out, mlp_rows, k_cache, v_cache, collective_id):
    bf, f32 = jnp.bfloat16, jnp.float32
    hbm = pl.BlockSpec(memory_space=pl.ANY)
    vmem = pl.BlockSpec(memory_space=pltpu.VMEM)
    reqs, span, width = k_cache.shape
    acc, new, wo_all, mw_all, accm, own_o, own_ml = pl.pallas_call(
        lambda p, x, wo, mw, k, v, o0, o1, o2, o3, o4, *rest: front_kernel(
            p, x, wo, mw, k, v, o0, o4, o1, o2, o3, *rest
        ),
        out_shape=(
            jax.ShapeDtypeStruct((4, 4, 128, 1024), bf),
            jax.ShapeDtypeStruct((4, 4, 2, 64, 1024), bf),
            jax.ShapeDtypeStruct((4,) + w_out.shape, bf),
            jax.ShapeDtypeStruct((4, 4, 2) + mlp_rows.shape, bf),
            jax.ShapeDtypeStruct((4, 4, 2, 8, 256), f32),
            jax.ShapeDtypeStruct((128, 1024), f32),
            jax.ShapeDtypeStruct((2, 8, 256), f32),
        ),
        in_specs=[pl.BlockSpec(memory_space=pltpu.SMEM), vmem, hbm, vmem, hbm, hbm],
        out_specs=(hbm,) * 5 + (vmem,) * 2,
        scratch_shapes=[
            pltpu.VMEM((128, 2048), bf),
            pltpu.VMEM((2, HD + 16, NEW_TOK), bf),
            pltpu.VMEM(w_out.shape, bf),
            pltpu.VMEM((4, 4, 2, 192, 1024), bf),
            pltpu.VMEM(k_cache.shape, bf),
            pltpu.VMEM(k_cache.shape, bf),
            pltpu.VMEM((reqs, 2, HD + 16, span), bf),
            pltpu.VMEM((4, 4, 128, 1024), bf),
            pltpu.VMEM((4, 4, 2, 8, 256), f32),
            pltpu.VMEM((4, 4, 128, 1024), bf),
            pltpu.VMEM((4, 4, 2, 8, 256), f32),
            pltpu.VMEM((4, 4, 128, 1024), bf),
            pltpu.VMEM((4, 4, 2, 8, 256), f32),
            pltpu.VMEM((2, 128, 2048), bf),
            pltpu.SemaphoreType.DMA((10,)),
            pltpu.SemaphoreType.DMA((80,)),
            pltpu.SemaphoreType.DMA((80,)),
            pltpu.SemaphoreType.DMA((32,)),
            pltpu.SemaphoreType.DMA((32,)),
            pltpu.SemaphoreType.DMA((32,)),
            pltpu.SemaphoreType.DMA((32,)),
        ],
        compiler_params=pltpu.CompilerParams(
            collective_id=collective_id, has_side_effects=True, vmem_limit_bytes=60 << 20
        ),
        cost_estimate=pl.CostEstimate(
            flops=20 << 30, bytes_accessed=60 << 20, transcendentals=reqs * 2048 * span
        ),
    )(prefix_len, packed, w_out, mlp_rows, k_cache, v_cache)
    wo_all = wo_all.reshape(-1, w_out.shape[1])
    mw_all = mw_all.reshape((reqs,) + mlp_rows.shape)
    return (acc, accm, own_o, own_ml), new.reshape(reqs, 64, 1024), wo_all, mw_all


def tokens_kernel(
    x_ref, w_ref, gain_ref, cos_ref, sin_ref, wq_hbm, wk_hbm, wv_hbm, whole_out, packed_ref, w_all,
    out_ref, normed, wq_ref, wk_ref, wv_ref, local_sems, send_sems, recv_sems,
):
    me, z, y, c = grid_place()
    dev = lambda zz, yy: zz * 8 + yy * 2 + c
    t = lax.axis_index("tp")
    right, left = (t + 1) % 4, (t + 3) % 4
    rows, width = x_ref.shape
    plan = Planner(send_sems, recv_sems)
    cols = lambda i: pl.ds(pl.multiple_of(i * width, width), width)
    top, low = pl.ds(0, rows // 2), pl.ds(rows // 2, rows // 2)
    p = plan(x_ref, out_ref.at[:, cols(t)], right, "tp")
    m = plan(x_ref, out_ref.at[:, cols(t)], left, "tp")
    ref = out_ref.at[top, cols(left)]
    fp = plan(ref, ref, right, "tp")
    ref = out_ref.at[low, cols(right)]
    fm = plan(ref, ref, left, "tp")
    w = ring(plan, w_ref, w_all)
    locals_ = [
        pltpu.make_async_copy(x_ref, out_ref.at[:, cols(t)], local_sems.at[0]),
        pltpu.make_async_copy(w_ref, w_all.at[z, y, c], local_sems.at[1]),
        pltpu.make_async_copy(wq_hbm, wq_ref, local_sems.at[3]),
        pltpu.make_async_copy(wk_hbm, wk_ref, local_sems.at[4]),
        pltpu.make_async_copy(wv_hbm, wv_ref, local_sems.at[5]),
    ]
    run(*locals_[:2])
    greet(
        [("grp", dev(z, (y + 1) % 4)), ("grp", dev(z, (y + 3) % 4))]
        + [("grp", dev((z + 1) % 4, y)), ("grp", dev((z + 3) % 4, y)), ("grp", me + 1 - 2 * c)]
        + [("tp", right), ("tp", left)]
    )
    run(p, m, *w["first"], *locals_[2:])
    for i in range(4):
        w["first"][i].wait_recv()
        run(w["first_on"][i])
    locals_[1].wait()
    arrive(*w["first_on"])
    run(*w["second"], *w["second_more"], *w["over_line"])
    arrive(p)
    run(fp)
    arrive(m)
    run(fm)
    arrive(fp, fm)
    locals_[0].wait()
    whole_copy = pltpu.make_async_copy(out_ref, whole_out, local_sems.at[2])
    whole_copy.start()

    def norm(i, carry):
        at = pl.ds(pl.multiple_of(i * 32, 32), 32)
        normed[at] = rms_scale(out_ref[at], gain_ref[...]).astype(jnp.bfloat16)
        return carry

    lax.fori_loop(0, rows // 32, norm, 0)
    for i in range(4):
        w["second"][i].wait_recv()
        run(w["second_on"][i], w["over"][i])
    cosine, sine = cos_ref[...], sin_ref[...]
    for load in locals_[2:]:
        load.wait()

    def heads_of(ref, i):
        both = jnp.transpose(
            jnp.dot(
                normed[...], ref[:, i * 128 : (i + 1) * 128], preferred_element_type=jnp.float32
            )
        )
        return both[:HD], both[HD:]

    def rope(head):
        first, second = head[:32], head[32:]
        return (
            (first * cosine - second * sine).astype(jnp.bfloat16),
            (second * cosine + first * sine).astype(jnp.bfloat16),
        )

    for i in range(4):
        for j, head in enumerate(heads_of(wq_ref, i)):
            kv, g = divmod(2 * i + j, 4)
            for k, part in enumerate(rope(head)):
                at = pl.ds(kv * 96 + k * 32, 32)
                packed_ref[at, g * 256 : (g + 1) * 256] = part * jnp.bfloat16(0.125)
    for i in range(4):
        w["second_more"][i].wait_recv()
        run(w["over_more"][i])
    for j, head in enumerate(heads_of(wk_ref, 0)):
        for k, part in enumerate(rope(head)):
            packed_ref[64 + 96 * k : 96 + 96 * k, j * 256 : (j + 1) * 256] = part
    for j, head in enumerate(heads_of(wv_ref, 0)):
        for k in range(2):
            part = head[k * 32 : (k + 1) * 32].astype(jnp.bfloat16)
            packed_ref[64 + 96 * k : 96 + 96 * k, (2 + j) * 256 : (3 + j) * 256] = part
    arrive(*w["second_on"])
    run(*w["over_last"])
    arrive(*w["over_line"], *w["over"], *w["over_more"], *w["over_last"])
    whole_copy.wait()
    for copy in plan.made:
        copy.wait_send()


def gather_tokens(x, w, gain, cosine, sine, w_query, w_key, w_value, collective_id):
    rows, width = x.shape
    hbm = pl.BlockSpec(memory_space=pl.ANY)
    vmem = pl.BlockSpec(memory_space=pltpu.VMEM)
    out, packed, w_all = pl.pallas_call(
        tokens_kernel,
        out_shape=(
            jax.ShapeDtypeStruct((rows, 4 * width), x.dtype),
            jax.ShapeDtypeStruct((192, 1024), x.dtype),
            jax.ShapeDtypeStruct((4, 4, 2) + w.shape, w.dtype),
        ),
        in_specs=[vmem] * 5 + [hbm] * 3,
        out_specs=(hbm, vmem, hbm),
        scratch_shapes=[
            pltpu.VMEM((rows, 4 * width), x.dtype),
            pltpu.VMEM((rows, 4 * width), x.dtype),
            pltpu.VMEM(w_query.shape, x.dtype),
            pltpu.VMEM(w_key.shape, x.dtype),
            pltpu.VMEM(w_value.shape, x.dtype),
            pltpu.SemaphoreType.DMA((6,)),
            pltpu.SemaphoreType.DMA((40,)),
            pltpu.SemaphoreType.DMA((40,)),
        ],
        compiler_params=pltpu.CompilerParams(
            collective_id=collective_id, has_side_effects=True, vmem_limit_bytes=58 << 20
        ),
        cost_estimate=pl.CostEstimate(flops=1 << 30, bytes_accessed=40 << 20, transcendentals=0),
    )(x, w, gain[None], cosine, sine, w_query, w_key, w_value)
    return out, packed, w_all.reshape((32,) + w.shape)


def merge_stats(parts):
    top = parts[0][0]
    for m, _ in parts[1:]:
        top = jnp.maximum(top, m)
    weights = [jnp.exp2((m - top) * LOG2E) for m, _ in parts]
    total = weights[0] * parts[0][1]
    for w, (_, l) in zip(weights[1:], parts[1:]):
        total = total + w * l
    return weights, top, total


def blend(outs, weights, g):
    acc = outs[0].astype(jnp.float32) * weights[0][g : g + 1]
    for o, w in zip(outs[1:], weights[1:]):
        acc = acc + o.astype(jnp.float32) * w[g : g + 1]
    return acc


def merge_into(acc, accm, others, index, kv, picks):
    stat = lambda ref, i: (ref[i + (pl.ds(0, 4),)], ref[i + (pl.ds(4, 4),)])
    mine = index + (kv,)
    weights, top, total = merge_stats(
        [stat(accm, mine)] + [stat(m, pick) for (_, m), pick in zip(others, picks)]
    )
    accm[mine + (pl.ds(0, 4),)] = top
    accm[mine + (pl.ds(4, 4),)] = total
    for g in range(4):
        lanes = pl.ds(g * 256, 256)
        here = index + (pl.ds(kv * HD, HD), lanes)
        outs = [acc[here]] + [o[pick + (pl.ds(0, HD), lanes)] for (o, _), pick in zip(others, picks)]
        acc[here] = blend(outs, weights, g).astype(jnp.bfloat16)


def grp_merge_kernel(
    sent, o_ref, ml_ref, own_o_ref, own_ml_ref, out_ref,
    acc, accm, ra, ram, rb, rbm, r3, r3m, att, local_sems, send_sems, recv_sems,
):
    me, z, y, c = grid_place()
    yp, ym, yo = (y + 1) % 4, (y + 3) % 4, (y + 2) % 4
    zp, zm, zo = (z + 1) % 4, (z + 3) % 4, (z + 2) % 4
    dev = lambda zz, yy: zz * 8 + yy * 2 + c
    east, west, north, south = dev(z, yp), dev(z, ym), dev(zp, y), dev(zm, y)
    far_y, far_z = dev(z, yo), dev(zo, y)
    send = Sender("grp", send_sems, recv_sems)
    loads = [
        pltpu.make_async_copy(o_ref, acc, local_sems.at[0]),
        pltpu.make_async_copy(ml_ref, accm, local_sems.at[1]),
    ]
    for load in loads:
        load.start()
    x = lax.axis_index("tp")
    right, left = (x + 1) % 4, (x + 3) % 4
    greet(
        [("grp", i) for i in (east, west, north, south, far_y, far_z)]
        + [("tp", right), ("tp", left), ("tp", (x + 2) % 4)]
    )
    for load in loads:
        load.wait()
    lo, hi = pl.ds(0, 2), pl.ds(2, 2)
    ka, kb = pl.ds(0, HD), pl.ds(HD, HD)

    def ship_a(zs, yy, slot, device):
        return (
            send(acc.at[zs, yy, ka], ra.at[slot], device),
            send(accm.at[zs, yy, 0], ram.at[slot], device),
        )

    def ship_b(zz, ys, slot, device):
        return (
            send(acc.at[zz, ys, kb], rb.at[slot], device),
            send(accm.at[zz, ys, 1], rbm.at[slot], device),
        )

    def arrived(pair):
        pair[0].wait_recv()
        pair[1].wait_recv()

    axp = ship_a(lo, yo, 0, east)
    bxp = ship_b(zo, lo, 0, north)
    axm = ship_a(hi, yo, 1, west)
    bxm = ship_b(zo, hi, 1, south)
    app = ship_a(hi, yp, 2, east)
    bpp = ship_b(zp, hi, 2, north)
    apm = ship_a(lo, ym, 3, west)
    bpm = ship_b(zm, lo, 3, south)
    sent()

    def fold_a(base, yy, slots):
        def body(i, carry):
            merge_into(acc, accm, [(ra, ram)] * len(slots), (base + i, yy), 0, [(s, i) for s in slots])
            return carry

        lax.fori_loop(0, 2, body, 0)

    def fold_b(zz, base, slots):
        def body(i, carry):
            merge_into(acc, accm, [(rb, rbm)] * len(slots), (zz, base + i), 1, [(s, i) for s in slots])
            return carry

        lax.fori_loop(0, 2, body, 0)

    arrived(axp)
    fold_a(0, yp, [0])
    amp = ship_a(lo, yp, 4, east)
    arrived(bxp)
    fold_b(zp, 0, [0])
    bmp = ship_b(zp, lo, 4, north)
    arrived(axm)
    fold_a(2, ym, [1])
    amm = ship_a(hi, ym, 5, west)
    arrived(bxm)
    fold_b(zm, 2, [1])
    bmm = ship_b(zm, hi, 5, south)
    arrived(app)
    arrived(apm)
    arrived(bpp)
    arrived(bpm)
    arrived(amp)
    fold_a(0, y, [3, 4])
    arrived(amm)
    fold_a(2, y, [2, 5])
    arrived(bmp)
    fold_b(z, 0, [3, 4])
    arrived(bmm)
    fold_b(z, 2, [2, 5])

    last = []
    for slot, (zz, device) in enumerate(((zo, far_z), (zp, north), (zm, south))):
        last.append(send(acc.at[zz, y, ka], r3.at[0, slot], device))
        last.append(send(accm.at[zz, y, 0], r3m.at[0, slot], device))
    for slot, (yy, device) in enumerate(((yo, far_y), (yp, east), (ym, west))):
        last.append(send(acc.at[z, yy, kb], r3.at[1, slot], device))
        last.append(send(accm.at[z, yy, 1], r3m.at[1, slot], device))
    for copy in last:
        copy.wait_recv()
    for kv in range(2):
        stat = lambda ref, i: (ref[i + (pl.ds(0, 4),)], ref[i + (pl.ds(4, 4),)])
        parts = [stat(own_ml_ref, (kv,)), stat(accm, (z, y, kv))]
        parts += [stat(r3m, (kv, s)) for s in range(3)]
        weights, _, total = merge_stats(parts)
        scale = 1.0 / total
        weights = [w * scale for w in weights]
        rows = pl.ds(kv * HD, HD)
        for pair in range(2):
            heads = []
            for g in (2 * pair, 2 * pair + 1):
                lanes = pl.ds(g * 256, 256)
                outs = [own_o_ref[rows, lanes], acc[z, y, rows, lanes]]
                outs += [r3[kv, s, :, lanes] for s in range(3)]
                heads.append(blend(outs, weights, g))
            block = jnp.transpose(jnp.concatenate(heads, axis=0)).astype(jnp.bfloat16)
            att[:, pl.ds((kv * 2 + pair) * 128, 128)] = block
    rows, width = att.shape
    cols = lambda i: pl.ds(pl.multiple_of(i * width, width), width)
    upper, lower = pl.ds(0, rows // 2), pl.ds(rows // 2, rows // 2)
    own = pltpu.make_async_copy(att, out_ref.at[:, cols(x)], local_sems.at[5])
    own.start()
    p = send(att, out_ref.at[:, cols(x)], right, "tp")
    m = send(att, out_ref.at[:, cols(x)], left, "tp")
    p.wait_recv()
    ref = out_ref.at[upper, cols(left)]
    fp = send(ref, ref, right, "tp")
    m.wait_recv()
    ref = out_ref.at[lower, cols(right)]
    fm = send(ref, ref, left, "tp")
    fp.wait_recv()
    fm.wait_recv()
    own.wait()
    send.finish()


def tail_kernel(
    make_attended, att_ref, tok_ref, gain_ref, wo_ref, w_ref, wd_ref, out_ref,
    wo, wb, wd, acc, firsts, n2, gate, up, hid, mine, outbox, inbox, load_sems, send_sems, recv_sems,
):
    me = lax.axis_index("tp")
    right, left, facing = (me + 1) % 4, (me + 3) % 4, (me + 2) % 4
    send = Sender("tp", send_sems, recv_sems)
    wo_part = lambda i: pltpu.make_async_copy(
        wo_ref.at[pl.ds(i * 512, 512)], wo.at[pl.ds(i * 512, 512)], load_sems.at[i]
    )
    w_part = lambda i: pltpu.make_async_copy(
        w_ref.at[pl.ds(i * 4, 4)], wb.at[pl.ds(i * 4, 4)], load_sems.at[4 + i]
    )
    down = pltpu.make_async_copy(wd_ref, wd, load_sems.at[12])

    def start_loads():
        for i in range(4):
            wo_part(i).start()
        for i in range(8):
            w_part(i).start()
        down.start()

    make_attended(start_loads)
    f32, bf = jnp.float32, jnp.bfloat16
    acc[...] = tok_ref[...].astype(f32)
    for i in range(4):
        wo_part(i).wait()

        def project(n, carry, i=i):
            lanes = pl.ds(pl.multiple_of(n * 512, 512), 512)
            acc[:, lanes] += jnp.dot(
                att_ref[:, i * 512 : (i + 1) * 512],
                wo[i * 512 : (i + 1) * 512, lanes],
                preferred_element_type=f32,
            )
            return carry

        lax.fori_loop(0, 4, project, 0)

    def norm(i, carry):
        rows = pl.ds(pl.multiple_of(i * 32, 32), 32)
        first = acc[rows].astype(bf)
        firsts[rows] = first
        n2[rows] = rms_scale(first, gain_ref[...]).astype(bf)
        return carry

    lax.fori_loop(0, NEW_TOK // 32, norm, 0)
    gate[...] = jnp.zeros_like(gate)
    up[...] = jnp.zeros_like(up)
    for i in range(8):
        w_part(i).wait()

        def widen(n, carry, i=i):
            lanes = pl.ds(pl.multiple_of(n * 512, 512), 512)
            x = n2[:, i * 256 : (i + 1) * 256]
            for total, at in ((gate, 0), (up, 64)):
                w = wb[4 * i : 4 * i + 4, at : at + 64, lanes].reshape(256, 512)
                total[:, lanes] += jnp.dot(x, w, preferred_element_type=f32)
            return carry

        lax.fori_loop(0, 2, widen, 0)

    def squash(i, carry):
        rows = pl.ds(pl.multiple_of(i * 32, 32), 32)
        v = gate[rows]
        hid[rows] = (v / (1.0 + jnp.exp(-v)) * up[rows]).astype(bf)
        return carry

    lax.fori_loop(0, NEW_TOK // 32, squash, 0)

    down.wait()

    def terms(target):
        w = wd[pl.ds(target * 8, 8)].reshape(512, 1024)
        return lax.dot_general(
            hid[...], w, (((1,), (1,)), ((), ())), preferred_element_type=f32
        )

    for slot, target in enumerate((facing, right, left)):
        outbox[slot] = terms(target).astype(bf)
        send(outbox.at[slot], inbox.at[slot], target)
    cols = pl.ds(pl.multiple_of(me * 512, 512), 512)
    mine[...] = firsts[:, cols].astype(f32) + terms(me)
    for copy in send.started:
        copy.wait_recv()
    for slot in range(3):
        mine[...] += inbox[slot].astype(f32)
    out_ref[...] = mine[...]
    send.finish()


MERGE_SCRATCH = 12


def back_kernel(o_ref, ml_ref, own_o_ref, own_ml_ref, tok_ref, gain_ref, wo_ref, w_ref, wd_ref, out_ref, att, *rest):
    merge = lambda sent: grp_merge_kernel(
        sent, o_ref, ml_ref, own_o_ref, own_ml_ref, att, *rest[:MERGE_SCRATCH]
    )
    tail_kernel(
        merge, att, tok_ref, gain_ref, wo_ref, w_ref, wd_ref, out_ref, *rest[MERGE_SCRATCH:]
    )


def back(parts, whole, gain, w_out, weights, down_rows, collective_id):
    bf, f32 = jnp.bfloat16, jnp.float32
    vmem = pl.BlockSpec(memory_space=pltpu.VMEM)
    hbm = pl.BlockSpec(memory_space=pl.ANY)
    rows, width = whole.shape
    copies = 24 + 12 + 4
    merge_scratch = [
        pltpu.VMEM((4, 4, 128, 1024), bf),
        pltpu.VMEM((4, 4, 2, 8, 256), f32),
        pltpu.VMEM((6, 2, HD, 1024), bf),
        pltpu.VMEM((6, 2, 8, 256), f32),
        pltpu.VMEM((6, 2, HD, 1024), bf),
        pltpu.VMEM((6, 2, 8, 256), f32),
        pltpu.VMEM((2, 3, HD, 1024), bf),
        pltpu.VMEM((2, 3, 8, 256), f32),
        pltpu.VMEM((NEW_TOK, 512), bf),
        pltpu.SemaphoreType.DMA((6,)),
        pltpu.SemaphoreType.DMA((copies,)),
        pltpu.SemaphoreType.DMA((copies,)),
    ]
    assert len(merge_scratch) == MERGE_SCRATCH
    return pl.pallas_call(
        back_kernel,
        out_shape=jax.ShapeDtypeStruct((rows, width // 4), f32),
        in_specs=[hbm, hbm, vmem, vmem, vmem, vmem, hbm, hbm, hbm],
        out_specs=vmem,
        scratch_shapes=[
            pltpu.VMEM((rows, width), bf),
            *merge_scratch,
            pltpu.VMEM(w_out.shape, bf),
            pltpu.VMEM(weights.shape, bf),
            pltpu.VMEM(down_rows.shape, bf),
            pltpu.VMEM((rows, width), f32),
            pltpu.VMEM((rows, width), bf),
            pltpu.VMEM((rows, width), bf),
            pltpu.VMEM((rows, 1024), f32),
            pltpu.VMEM((rows, 1024), f32),
            pltpu.VMEM((rows, 1024), bf),
            pltpu.VMEM((rows, 512), f32),
            pltpu.VMEM((3, rows, 512), bf),
            pltpu.VMEM((3, rows, 512), bf),
            pltpu.SemaphoreType.DMA((13,)),
            pltpu.SemaphoreType.DMA((3,)),
            pltpu.SemaphoreType.DMA((3,)),
        ],
        compiler_params=pltpu.CompilerParams(
            collective_id=collective_id, has_side_effects=True, vmem_limit_bytes=60 << 20
        ),
        cost_estimate=pl.CostEstimate(
            flops=5 << 30, bytes_accessed=130 << 20, transcendentals=1 << 18
        ),
    )(*parts, whole, gain[None], w_out, weights, down_rows)


def shards(
    tokens,
    attn_gain,
    w_query,
    w_key,
    w_value,
    w_out,
    mlp_gain,
    w_gate,
    w_up,
    w_down,
    k_cache,
    v_cache,
    prefix_len,
):
    group = lax.axis_index("grp")
    slice_len = k_cache.shape[1]
    start = group * slice_len
    own_len = lax.dynamic_slice_in_dim(prefix_len, group, 1)[0]
    positions = (own_len + jnp.arange(NEW_TOK, dtype=jnp.int32)).astype(jnp.float32)
    inverse = ROPE_BASE ** (-2.0 * jnp.arange(HD // 2, dtype=jnp.float32) / HD)
    angles = positions[None, :] * inverse[:, None]
    cosine, sine = jnp.cos(angles), jnp.sin(angles)
    whole, packed, down_rows = gather_tokens(
        tokens, w_down.T, attn_gain, cosine, sine, w_query, w_key, w_value, 0
    )
    mlp_rows = jnp.concatenate([w_gate, w_up], axis=0)
    parts, new_rows, whole_out, weights = front(
        prefix_len, packed, w_out, mlp_rows, k_cache, v_cache, 1
    )
    k_next, v_next = place_new(start[None], prefix_len, new_rows, k_cache, v_cache)
    result = back(parts, whole, mlp_gain, whole_out, weights, down_rows, 2)
    return (result, k_next, v_next)


def solution(mesh):
    placed = (
        P("grp", "tp"),
        P(),
        P(None, "tp"),
        P(None, "tp"),
        P(None, "tp"),
        P("tp", None),
        P(),
        P("grp", "tp"),
        P("grp", "tp"),
        P("tp", "grp"),
        P(None, "grp", "tp"),
        P(None, "grp", "tp"),
        P(),
    )
    return jax.shard_map(
        shards,
        mesh=mesh,
        in_specs=placed,
        out_specs=(P("grp", "tp"), P(None, "grp", "tp"), P(None, "grp", "tp")),
        check_vma=False,
    )
```

```python
import math

import jax
import jax.numpy as jnp
from jax import lax
from jax.experimental import pallas as pl
from jax.experimental.pallas import tpu as pltpu
from jax.sharding import PartitionSpec as P

HD = 64
NEW_TOK = 256
EPS = 1e-05
ROPE_BASE = 500000.0
NEG = -1e30
LOG2E = math.log2(math.e)


def rms_scale(rows, gain):
    rows = rows.astype(jnp.float32)
    return rows * lax.rsqrt(jnp.mean(rows * rows, axis=-1, keepdims=True) + EPS) * gain


def attend(keys, qbd, vta, mask, o_store, ml_ref, width=512):
    blocks = 2048 // width

    def scores(i):
        return jnp.dot(
            keys, qbd[:, i * width : (i + 1) * width], preferred_element_type=jnp.float32
        )

    def soften(s):
        s = jnp.where(mask, s, NEG)
        top = jnp.max(s, axis=0, keepdims=True)
        return top, jnp.exp2((s - top) * LOG2E).astype(jnp.bfloat16)

    def finish(i, top, p):
        kv, first = divmod(i * width, 1024)
        o = jnp.dot(vta[kv], p, preferred_element_type=jnp.float32)
        o_store(kv, pl.ds(first, width), o[:HD])
        for j in range(0, width, 256):
            g = (first + j) // 256
            ml_ref[kv, g : g + 1] = top[:, j : j + 256]
            ml_ref[kv, 4 + g : 5 + g] = o[HD : HD + 1, j : j + 256]

    s, before = scores(0), None
    for i in range(blocks):
        ahead = scores(i + 1) if i + 1 < blocks else None
        now = soften(s)
        if before is not None:
            finish(i - 1, *before)
        before, s = now, ahead
    finish(blocks - 1, *before)


def fill_scratch(q, vt, qbd, vta):
    zero = jnp.zeros((HD, 1024), jnp.bfloat16)
    qbd[0:HD, 0:1024] = q[0:HD]
    qbd[HD : 2 * HD, 0:1024] = zero
    qbd[0:HD, 1024:2048] = zero
    qbd[HD : 2 * HD, 1024:2048] = q[HD : 2 * HD]
    ones = jnp.ones((16, vt.shape[1]), jnp.bfloat16)
    for kv in range(2):
        vta[kv, 0:HD] = vt[kv * HD : (kv + 1) * HD]
        vta[kv, HD : HD + 16] = ones


def flip(x):
    return jnp.transpose(x.astype(jnp.float32)).astype(jnp.bfloat16)


def place_kernel(start_ref, plen_ref, new_ref, k_ref, v_ref, ko_ref, vo_ref, kbuf, vbuf, nbuf, sems):
    reqs, span, _ = k_ref.shape
    each = 4
    pieces = reqs // each
    at = lambda i: pl.ds(i * each, each)
    news = pltpu.make_async_copy(new_ref, nbuf, sems.at[4, 0])
    sets = []
    for row, (src, dst) in enumerate(((k_ref, kbuf), (v_ref, vbuf), (kbuf, ko_ref), (vbuf, vo_ref))):
        sets.append(
            [
                pltpu.make_async_copy(src.at[at(i)], dst.at[at(i)], sems.at[row, i])
                for i in range(pieces)
            ]
        )
    news.start()
    for i in range(pieces):
        sets[0][i].start()
        sets[1][i].start()
    news.wait()

    for i in range(pieces):
        sets[0][i].wait()
        sets[1][i].wait()

        def patch(r, carry):
            off = plen_ref[r] - start_ref[0]

            @pl.when((off > -NEW_TOK) & (off < span))
            def _():
                rows = lax.broadcasted_iota(jnp.int32, (span, NEW_TOK), 0)
                cols = lax.broadcasted_iota(jnp.int32, (span, NEW_TOK), 1)
                pick = (rows - off == cols).astype(jnp.float32).astype(jnp.bfloat16)
                rel = lax.broadcasted_iota(jnp.int32, (span, 128), 0) - off
                inside = (rel >= 0) & (rel < NEW_TOK)
                for first, buf in ((0, kbuf), (512, vbuf)):
                    new = jnp.concatenate(
                        [nbuf[r, :, first : first + 256], nbuf[r, :, first + 256 : first + 512]],
                        axis=0,
                    )
                    placed = jnp.dot(pick, flip(new), preferred_element_type=jnp.float32)
                    old = buf[r].astype(jnp.float32)
                    buf[r] = jnp.where(inside, placed, old).astype(jnp.bfloat16)

            return carry

        lax.fori_loop(i * each, (i + 1) * each, patch, 0)
        sets[2][i].start()
        sets[3][i].start()
    for i in range(pieces):
        sets[2][i].wait()
        sets[3][i].wait()


def place_new(start, prefix_len, new, k_cache, v_cache):
    smem = pl.BlockSpec(memory_space=pltpu.SMEM)
    hbm = pl.BlockSpec(memory_space=pl.ANY)
    return pl.pallas_call(
        place_kernel,
        out_shape=(
            jax.ShapeDtypeStruct(k_cache.shape, k_cache.dtype),
            jax.ShapeDtypeStruct(v_cache.shape, v_cache.dtype),
        ),
        in_specs=[smem, smem, hbm, hbm, hbm],
        out_specs=(hbm, hbm),
        scratch_shapes=[
            pltpu.VMEM(k_cache.shape, k_cache.dtype),
            pltpu.VMEM(v_cache.shape, v_cache.dtype),
            pltpu.VMEM(new.shape, new.dtype),
            pltpu.SemaphoreType.DMA((5, 8)),
        ],
        compiler_params=pltpu.CompilerParams(vmem_limit_bytes=58 << 20),
        cost_estimate=pl.CostEstimate(flops=1 << 28, bytes_accessed=20 << 20, transcendentals=0),
    )(start, prefix_len, new, k_cache, v_cache)


def own_kernel(q_ref, o_ref, ml_ref, qbd, vta):
    new = jnp.concatenate([q_ref[64:96], q_ref[160:192]], axis=0)
    part = lambda i: new[:, i * 256 : (i + 1) * 256]
    heads = jnp.concatenate([q_ref[0:64], q_ref[96:160]], axis=0)
    fill_scratch(heads, jnp.concatenate([part(2), part(3)], axis=0), qbd, vta)
    keys = flip(jnp.concatenate([part(0), part(1)], axis=0))
    mask = (
        lax.broadcasted_iota(jnp.int32, (NEW_TOK, 512), 0)
        <= lax.broadcasted_iota(jnp.int32, (NEW_TOK, 512), 1) % NEW_TOK
    )

    def store(kv, lanes, o):
        o_ref[pl.ds(kv * HD, HD), lanes] = o

    attend(keys, qbd, vta, mask, store, ml_ref)


MESH = pl.DeviceIdType.MESH


def grid_place():
    me = lax.axis_index("grp")
    z, y, core = me // 8, (me // 2) % 4, me % 2
    return me, z, y, core


class Sender:
    def __init__(self, axis, send_sems, recv_sems):
        self.axis, self.send_sems, self.recv_sems, self.started = axis, send_sems, recv_sems, []

    def __call__(self, src, dst, device, axis=None):
        i = len(self.started)
        copy = pltpu.make_async_remote_copy(
            src_ref=src,
            dst_ref=dst,
            send_sem=self.send_sems.at[i],
            recv_sem=self.recv_sems.at[i],
            device_id={axis or self.axis: device},
            device_id_type=MESH,
        )
        copy.start()
        self.started.append(copy)
        return copy

    def finish(self):
        for copy in self.started:
            copy.wait_send()


def greet(devices):
    barrier = pltpu.get_barrier_semaphore()
    for axis, device in devices:
        pl.semaphore_signal(barrier, inc=1, device_id={axis: device}, device_id_type=MESH)
    pl.semaphore_wait(barrier, len(devices))


class Planner:
    def __init__(self, send_sems, recv_sems):
        self.send_sems, self.recv_sems, self.made = send_sems, recv_sems, []

    def __call__(self, src, dst, device, axis="grp"):
        i = len(self.made)
        self.made.append(
            pltpu.make_async_remote_copy(
                src_ref=src,
                dst_ref=dst,
                send_sem=self.send_sems.at[i],
                recv_sem=self.recv_sems.at[i],
                device_id={axis: device},
                device_id_type=MESH,
            )
        )
        return self.made[-1]


def run(*copies):
    for copy in copies:
        copy.start()


def arrive(*copies):
    for copy in copies:
        copy.wait_recv()


def ring(plan, src, whole, full=True):
    me, z, y, c = grid_place()
    sib = me + 1 - 2 * c
    yp, ym, yo = (y + 1) % 4, (y + 3) % 4, (y + 2) % 4
    zp, zm, zo = (z + 1) % 4, (z + 3) % 4, (z + 2) % 4
    dev = lambda zz, yy: zz * 8 + yy * 2 + c
    east, west, north, south = dev(z, yp), dev(z, ym), dev(zp, y), dev(zm, y)
    n = src.shape[0] // 4
    a, b = pl.ds(0, 2 * n), pl.ds(2 * n, 2 * n)
    a0, a1, b0, b1 = (pl.ds(i * n, n) for i in range(4))
    lo, hi, every = pl.ds(0, 2), pl.ds(2, 2), pl.ds(0, 4)
    same = lambda device, *index: plan(whole.at[index], whole.at[index], device)
    own = lambda rows, device: plan(src.at[rows], whole.at[z, y, c, rows], device)
    out = dict(
        first=[own(a, east), own(b, north), own(a, west), own(b, south)],
        first_on=[
            same(east, z, ym, c, a0),
            same(north, zm, y, c, b0),
            same(west, z, yp, c, a1),
            same(south, zp, y, c, b1),
        ],
        second=[
            same(north, z, lo, c, a),
            same(east, lo, y, c, b),
            same(south, z, hi, c, a),
            same(west, hi, y, c, b),
        ],
        second_more=[
            same(north, z, hi, c, a),
            same(east, hi, y, c, b),
            same(south, z, lo, c, a),
            same(west, lo, y, c, b),
        ],
        second_on=[
            same(north, zm, lo, c, a),
            same(east, lo, ym, c, b),
            same(south, zp, hi, c, a),
            same(west, hi, yp, c, b),
        ],
        over=[
            same(sib, zm, lo, c, a),
            same(sib, lo, ym, c, b),
            same(sib, zp, hi, c, a),
            same(sib, hi, yp, c, b),
        ],
        over_more=[
            same(sib, zm, hi, c, a),
            same(sib, hi, ym, c, b),
            same(sib, zp, lo, c, a),
            same(sib, lo, yp, c, b),
        ],
        over_last=[same(sib, zo, every, c, a), same(sib, every, yo, c, b)],
    )
    if full:
        out["over_line"] = [same(sib, z, every, c, a), same(sib, every, y, c, b)]
    return out


def attend_pair(keys, limits, q, vts, stores):
    masks = [lax.broadcasted_iota(jnp.int32, (keys[0].shape[0], 512), 0) < n for n in limits]

    def scores(i):
        return jnp.dot(
            keys[i // 2], q[:, i * 512 : (i + 1) * 512], preferred_element_type=jnp.float32
        )

    def soften(i, s):
        s = jnp.where(masks[i // 2], s, NEG)
        top = jnp.max(s, axis=0, keepdims=True)
        return top, jnp.exp2((s - top) * LOG2E).astype(jnp.bfloat16)

    def finish(i, top, p):
        o = jnp.dot(vts[i // 2], p, preferred_element_type=jnp.float32)
        stores[i // 2](i % 2, o, top)

    s, before = scores(0), None
    for i in range(4):
        ahead = scores(i + 1) if i < 3 else None
        now = soften(i, s)
        if before is not None:
            finish(i - 1, *before)
        before, s = now, ahead
    finish(3, *before)


def front_kernel(
    plen_ref, x_ref, wo_hbm, wg_hbm, wu_hbm, k_ref, v_ref,
    acc_out, accm_out, new_out, wo_all, mw_all, own_o, own_ml,
    own_q, own_v, mw_ref, wo_ref, qg, kbuf, vbuf, vta, acc, accm, box, boxm, r1, r1m, qbd,
    local_sems, send_sems, recv_sems, box_send, box_recv, boxm_send, boxm_recv,
):
    me, z, y, c = grid_place()
    x = lax.axis_index("tp")
    sib = me + 1 - 2 * c
    yp, ym, yo = (y + 1) % 4, (y + 3) % 4, (y + 2) % 4
    zp, zm, zo = (z + 1) % 4, (z + 3) % 4, (z + 2) % 4
    right, left, facing = (x + 1) % 4, (x + 3) % 4, (x + 2) % 4
    dev = lambda zz, yy: zz * 8 + yy * 2 + c
    east, west, north, south = dev(z, yp), dev(z, ym), dev(zp, y), dev(zm, y)
    span = k_ref.shape[1]
    start = me * span
    plan = Planner(send_sems, recv_sems)
    a, b = pl.ds(0, 96), pl.ds(96, 96)
    q = ring(plan, x_ref, qg, full=False)
    same_q = lambda *index: plan(qg.at[index], qg.at[index], sib)
    over_own = plan(x_ref, qg.at[z, y, c], sib)
    over_first = [
        same_q(z, ym, c, a),
        same_q(zm, y, c, b),
        same_q(z, yp, c, a),
        same_q(zp, y, c, b),
        same_q(z, yo, c, a),
        same_q(zo, y, c, b),
    ]
    m = ring(plan, mw_ref, mw_all)
    share = wo_ref.shape[0] // 2
    mine = pl.ds(pl.multiple_of(c * share, share), share)
    mine0 = pl.ds(pl.multiple_of(c * share, share // 2), share // 2)
    mine1 = pl.ds(pl.multiple_of(c * share + share // 2, share // 2), share // 2)
    same_w = lambda device, axis, *index: plan(wo_all.at[index], wo_all.at[index], device, axis)
    w_first = [
        plan(wo_ref.at[mine], wo_all.at[x, mine], right, "tp"),
        plan(wo_ref.at[mine], wo_all.at[x, mine], left, "tp"),
    ]
    w_on = [same_w(right, "tp", left, mine0), same_w(left, "tp", right, mine1)]
    w_over = [
        same_w(sib, "grp", left, mine),
        same_w(sib, "grp", right, mine),
        same_w(sib, "grp", facing, mine),
    ]
    locals_ = [
        pltpu.make_async_copy(src, dst, local_sems.at[i])
        for i, (src, dst) in enumerate(
            (
                (k_ref, kbuf),
                (v_ref, vbuf),
                (x_ref, qg.at[z, y, c]),
                (mw_ref, mw_all.at[z, y, c]),
                (wo_ref, wo_all.at[x]),
                (qg.at[:, :, :, pl.ds(64, 32)], new_out.at[:, :, :, pl.ds(0, 32)]),
                (qg.at[:, :, :, pl.ds(160, 32)], new_out.at[:, :, :, pl.ds(32, 32)]),
                (acc, acc_out),
                (accm, accm_out),
            )
        )
    ]
    wo_load = pltpu.make_async_copy(wo_hbm, wo_ref, local_sems.at[9])
    part = wg_hbm.shape[0]
    mw_loads = [
        pltpu.make_async_copy(src, mw_ref.at[pl.ds(i * part, part)], local_sems.at[10 + i])
        for i, src in enumerate((wg_hbm, wu_hbm))
    ]
    run(locals_[1], locals_[2])
    greet(
        [("grp", i) for i in (east, west, north, south, sib)] + [("tp", right), ("tp", left)]
    )
    run(*q["first"], over_own)
    wo_load.start()
    run(locals_[0], *mw_loads)
    wo_load.wait()
    run(*w_first, locals_[4])
    own_kernel(x_ref, own_o, own_ml, own_q, own_v)
    locals_[1].wait()
    qbd[...] = jnp.zeros_like(qbd)

    def prepare(r, carry):
        vt = flip(vbuf[r])
        ones = jnp.ones((16, span), jnp.bfloat16)
        for kv in range(2):
            vta[r, kv, 0:HD] = vt[kv * HD : (kv + 1) * HD]
            vta[r, kv, HD : HD + 16] = ones
        return carry

    lax.fori_loop(0, 16, prepare, 0)
    for i in range(4):
        q["first"][i].wait_recv()
        run(q["first_on"][i], over_first[i])
    lax.fori_loop(16, 32, prepare, 0)
    locals_[2].wait()
    arrive(*q["first_on"])
    run(*q["second"], over_first[4], over_first[5], *q["second_more"])
    locals_[0].wait()
    over_own.wait_recv()

    def unit(step, kv, zz, yy):
        cores = (c, 1 - c)
        reqs = [(zz * 4 + yy) * 2 + cc for cc in cores]
        half = pl.ds(pl.multiple_of(kv * HD, HD), HD)
        q_rows = pl.ds(pl.multiple_of(kv * 96, 96), HD)
        for role in range(2):
            qbd[kv, half, role * 1024 : (role + 1) * 1024] = qg[zz, yy, cores[role], q_rows]

        def keep(o_ref, m_ref):
            def store(block, o, top):
                o_ref[zz, yy, half, pl.ds(block * 512, 512)] = o[:HD].astype(jnp.bfloat16)
                for j in range(2):
                    g = block * 2 + j
                    m_ref[zz, yy, kv, g : g + 1] = top[:, j * 256 : (j + 1) * 256]
                    m_ref[zz, yy, kv, 4 + g : 5 + g] = o[HD : HD + 1, j * 256 : (j + 1) * 256]

            return store

        attend_pair(
            [kbuf[r] for r in reqs],
            [plen_ref[r] - start for r in reqs],
            qbd.at[kv],
            [vta[r, kv] for r in reqs],
            [keep(acc, accm), keep(box, boxm)],
        )
        run(*ship(step, kv, zz, yy))

    def ship(step, kv, zz, yy):
        half = pl.ds(pl.multiple_of(kv * HD, HD), HD)
        to = dict(device_id={"grp": sib}, device_id_type=MESH)
        return (
            pltpu.make_async_remote_copy(
                src_ref=box.at[zz, yy, half],
                dst_ref=r1.at[zz, yy, half],
                send_sem=box_send.at[step],
                recv_sem=box_recv.at[step],
                **to,
            ),
            pltpu.make_async_remote_copy(
                src_ref=boxm.at[zz, yy, kv],
                dst_ref=r1m.at[zz, yy, kv],
                send_sem=boxm_send.at[step],
                recv_sem=boxm_recv.at[step],
                **to,
            ),
        )

    turn = lambda i: 3 * i - 5 * (i // 2) - 2 * (i // 3)

    def near_place(s):
        kv, d = s % 2, turn(s // 2)
        return kv, (z + kv * d) % 4, (y + (1 - kv) * d) % 4

    def mid_place(s):
        late, way, j = s // 8, (s % 8) // 2, s % 2
        kv, far_way = way % 2, way // 2
        d = 3 - 2 * far_way
        i = 2 * ((1 - far_way) * late + far_way * (1 - late)) + j
        zz = (1 - kv) * ((z + d) % 4) + kv * i
        yy = (1 - kv) * i + kv * ((y + d) % 4)
        return kv, zz, yy

    def far_place(s):
        kv, i = s // 4, s % 4
        zz = (1 - kv) * ((z + 2) % 4) + kv * i
        yy = (1 - kv) * i + kv * ((y + 2) % 4)
        return kv, zz, yy

    def near(s, carry):
        @pl.when(s == 2)
        def _():
            arrive(*over_first[:4])

        @pl.when(s == 6)
        def _():
            arrive(*over_first[4:])
            for i in range(4):
                q["second"][i].wait_recv()
                run(q["second_on"][i], q["over"][i])

        unit(s, *near_place(s))
        return carry

    lax.fori_loop(0, 8, near, 0)

    def mid(s, carry):
        @pl.when(s == 0)
        def _():
            arrive(*q["over"])

        @pl.when(s == 4)
        def _():
            for i in range(4):
                q["second_more"][i].wait_recv()
                run(q["over_more"][i])
            for i in range(2):
                w_first[i].wait_recv()
                run(w_on[i], w_over[i])
            for load in mw_loads:
                load.wait()
            locals_[3].start()
            locals_[4].wait()
            run(*m["first"])

        @pl.when(s == 8)
        def _():
            arrive(*q["over_more"])

        @pl.when(s == 10)
        def _():
            arrive(*q["second_on"])
            run(*q["over_last"])
            for i in range(4):
                m["first"][i].wait_recv()
                run(m["first_on"][i])

        @pl.when(s == 12)
        def _():
            arrive(*m["first_on"])
            locals_[3].wait()
            run(*m["second"], *m["second_more"], *m["over_line"])

        unit(8 + s, *mid_place(s))
        return carry

    lax.fori_loop(0, 16, mid, 0)

    def far(s, carry):
        @pl.when(s == 0)
        def _():
            arrive(*q["over_last"])

        @pl.when(s == 3)
        def _():
            for i in range(4):
                m["second"][i].wait_recv()
                run(m["second_on"][i], m["over"][i])

        @pl.when(s == 6)
        def _():
            for i in range(4):
                m["second_more"][i].wait_recv()
                run(m["over_more"][i])
            arrive(*w_on)
            run(w_over[2])

        unit(24 + s, *far_place(s))
        return carry

    lax.fori_loop(0, 8, far, 0)
    run(locals_[5], locals_[6])

    def near_arrived(s, carry):
        for copy in ship(s, *near_place(s)):
            copy.wait_recv()
        return carry

    def mid_arrived(s, carry):
        for copy in ship(8 + s, *mid_place(s)):
            copy.wait_recv()
        return carry

    def far_arrived(s, carry):
        for copy in ship(24 + s, *far_place(s)):
            copy.wait_recv()
        return carry

    lax.fori_loop(0, 8, near_arrived, 0)
    lax.fori_loop(0, 16, mid_arrived, 0)
    lax.fori_loop(0, 8, far_arrived, 0)

    def core_merge(i, carry):
        zz, yy = i // 4, i % 4
        for kv in range(2):
            stat = lambda ref: (ref[zz, yy, kv, 0:4], ref[zz, yy, kv, 4:8])
            weights, top, total = merge_stats([stat(accm), stat(r1m)])
            accm[zz, yy, kv, 0:4] = top
            accm[zz, yy, kv, 4:8] = total
            for g in range(4):
                here = (zz, yy, pl.ds(kv * HD, HD), pl.ds(g * 256, 256))
                acc[here] = blend([acc[here], r1[here]], weights, g).astype(jnp.bfloat16)
        return carry

    lax.fori_loop(0, 16, core_merge, 0)
    run(locals_[7], locals_[8])
    arrive(*m["second_on"])
    run(*m["over_last"])
    arrive(*m["over_line"], *m["over"], *m["over_more"], *m["over_last"], *w_over)
    for copy in plan.made:
        copy.wait_send()

    def near_sent(s, carry):
        for copy in ship(s, *near_place(s)):
            copy.wait_send()
        return carry

    def mid_sent(s, carry):
        for copy in ship(8 + s, *mid_place(s)):
            copy.wait_send()
        return carry

    def far_sent(s, carry):
        for copy in ship(24 + s, *far_place(s)):
            copy.wait_send()
        return carry

    lax.fori_loop(0, 8, near_sent, 0)
    lax.fori_loop(0, 16, mid_sent, 0)
    lax.fori_loop(0, 8, far_sent, 0)
    for copy in locals_[5:]:
        copy.wait()


def front(prefix_len, packed, w_out, w_gate, w_up, k_cache, v_cache, collective_id):
    bf, f32 = jnp.bfloat16, jnp.float32
    hbm = pl.BlockSpec(memory_space=pl.ANY)
    vmem = pl.BlockSpec(memory_space=pltpu.VMEM)
    reqs, span, width = k_cache.shape
    mlp_shape = (2 * w_gate.shape[0], w_gate.shape[1])
    acc, new, wo_all, mw_all, accm, own_o, own_ml = pl.pallas_call(
        lambda p, x, wo, wg, wu, k, v, o0, o1, o2, o3, o4, *rest: front_kernel(
            p, x, wo, wg, wu, k, v, o0, o4, o1, o2, o3, *rest
        ),
        out_shape=(
            jax.ShapeDtypeStruct((4, 4, 128, 1024), bf),
            jax.ShapeDtypeStruct((4, 4, 2, 64, 1024), bf),
            jax.ShapeDtypeStruct((4,) + w_out.shape, bf),
            jax.ShapeDtypeStruct((4, 4, 2) + mlp_shape, bf),
            jax.ShapeDtypeStruct((4, 4, 2, 8, 256), f32),
            jax.ShapeDtypeStruct((128, 1024), f32),
            jax.ShapeDtypeStruct((2, 8, 256), f32),
        ),
        in_specs=[pl.BlockSpec(memory_space=pltpu.SMEM), vmem] + [hbm] * 5,
        out_specs=(hbm,) * 5 + (vmem,) * 2,
        scratch_shapes=[
            pltpu.VMEM((128, 2048), bf),
            pltpu.VMEM((2, HD + 16, NEW_TOK), bf),
            pltpu.VMEM(mlp_shape, bf),
            pltpu.VMEM(w_out.shape, bf),
            pltpu.VMEM((4, 4, 2, 192, 1024), bf),
            pltpu.VMEM(k_cache.shape, bf),
            pltpu.VMEM(k_cache.shape, bf),
            pltpu.VMEM((reqs, 2, HD + 16, span), bf),
            pltpu.VMEM((4, 4, 128, 1024), bf),
            pltpu.VMEM((4, 4, 2, 8, 256), f32),
            pltpu.VMEM((4, 4, 128, 1024), bf),
            pltpu.VMEM((4, 4, 2, 8, 256), f32),
            pltpu.VMEM((4, 4, 128, 1024), bf),
            pltpu.VMEM((4, 4, 2, 8, 256), f32),
            pltpu.VMEM((2, 128, 2048), bf),
            pltpu.SemaphoreType.DMA((12,)),
            pltpu.SemaphoreType.DMA((80,)),
            pltpu.SemaphoreType.DMA((80,)),
            pltpu.SemaphoreType.DMA((32,)),
            pltpu.SemaphoreType.DMA((32,)),
            pltpu.SemaphoreType.DMA((32,)),
            pltpu.SemaphoreType.DMA((32,)),
        ],
        compiler_params=pltpu.CompilerParams(
            collective_id=collective_id, has_side_effects=True, vmem_limit_bytes=60 << 20
        ),
        cost_estimate=pl.CostEstimate(
            flops=20 << 30, bytes_accessed=60 << 20, transcendentals=reqs * 2048 * span
        ),
    )(prefix_len, packed, w_out, w_gate, w_up, k_cache, v_cache)
    wo_all = wo_all.reshape(-1, w_out.shape[1])
    mw_all = mw_all.reshape((reqs,) + mlp_shape)
    return (acc, accm, own_o, own_ml), new.reshape(reqs, 64, 1024), wo_all, mw_all


def tokens_kernel(
    x_ref, w_ref, gain_ref, cos_ref, sin_ref, wq_hbm, wk_hbm, wv_hbm, whole_out, packed_ref, w_all,
    out_ref, normed, wq_ref, wk_ref, wv_ref, local_sems, send_sems, recv_sems,
):
    me, z, y, c = grid_place()
    dev = lambda zz, yy: zz * 8 + yy * 2 + c
    t = lax.axis_index("tp")
    right, left = (t + 1) % 4, (t + 3) % 4
    rows, width = x_ref.shape
    plan = Planner(send_sems, recv_sems)
    cols = lambda i: pl.ds(pl.multiple_of(i * width, width), width)
    top, low = pl.ds(0, rows // 2), pl.ds(rows // 2, rows // 2)
    p = plan(x_ref, out_ref.at[:, cols(t)], right, "tp")
    m = plan(x_ref, out_ref.at[:, cols(t)], left, "tp")
    ref = out_ref.at[top, cols(left)]
    fp = plan(ref, ref, right, "tp")
    ref = out_ref.at[low, cols(right)]
    fm = plan(ref, ref, left, "tp")
    w = ring(plan, w_ref, w_all)
    locals_ = [
        pltpu.make_async_copy(x_ref, out_ref.at[:, cols(t)], local_sems.at[0]),
        pltpu.make_async_copy(w_ref, w_all.at[z, y, c], local_sems.at[1]),
        pltpu.make_async_copy(wq_hbm, wq_ref, local_sems.at[3]),
        pltpu.make_async_copy(wk_hbm, wk_ref, local_sems.at[4]),
        pltpu.make_async_copy(wv_hbm, wv_ref, local_sems.at[5]),
    ]
    run(*locals_[:2])
    greet(
        [("grp", dev(z, (y + 1) % 4)), ("grp", dev(z, (y + 3) % 4))]
        + [("grp", dev((z + 1) % 4, y)), ("grp", dev((z + 3) % 4, y)), ("grp", me + 1 - 2 * c)]
        + [("tp", right), ("tp", left)]
    )
    run(p, m, *w["first"], *locals_[2:])
    for i in range(4):
        w["first"][i].wait_recv()
        run(w["first_on"][i])
    locals_[1].wait()
    arrive(*w["first_on"])
    run(*w["second"], *w["second_more"], *w["over_line"])
    arrive(p)
    run(fp)
    arrive(m)
    run(fm)
    arrive(fp, fm)
    locals_[0].wait()
    whole_copy = pltpu.make_async_copy(out_ref, whole_out, local_sems.at[2])
    whole_copy.start()

    def norm(i, carry):
        at = pl.ds(pl.multiple_of(i * 32, 32), 32)
        normed[at] = rms_scale(out_ref[at], gain_ref[...]).astype(jnp.bfloat16)
        return carry

    lax.fori_loop(0, rows // 32, norm, 0)
    for i in range(4):
        w["second"][i].wait_recv()
        run(w["second_on"][i], w["over"][i])
    cosine, sine = cos_ref[...], sin_ref[...]
    for load in locals_[2:]:
        load.wait()

    def heads_of(ref, i):
        both = jnp.transpose(
            jnp.dot(
                normed[...], ref[:, i * 128 : (i + 1) * 128], preferred_element_type=jnp.float32
            )
        )
        return both[:HD], both[HD:]

    def rope(head):
        first, second = head[:32], head[32:]
        return (
            (first * cosine - second * sine).astype(jnp.bfloat16),
            (second * cosine + first * sine).astype(jnp.bfloat16),
        )

    for i in range(4):
        for j, head in enumerate(heads_of(wq_ref, i)):
            kv, g = divmod(2 * i + j, 4)
            for k, part in enumerate(rope(head)):
                at = pl.ds(kv * 96 + k * 32, 32)
                packed_ref[at, g * 256 : (g + 1) * 256] = part * jnp.bfloat16(0.125)
    for i in range(4):
        w["second_more"][i].wait_recv()
        run(w["over_more"][i])
    for j, head in enumerate(heads_of(wk_ref, 0)):
        for k, part in enumerate(rope(head)):
            packed_ref[64 + 96 * k : 96 + 96 * k, j * 256 : (j + 1) * 256] = part
    for j, head in enumerate(heads_of(wv_ref, 0)):
        for k in range(2):
            part = head[k * 32 : (k + 1) * 32].astype(jnp.bfloat16)
            packed_ref[64 + 96 * k : 96 + 96 * k, (2 + j) * 256 : (3 + j) * 256] = part
    arrive(*w["second_on"])
    run(*w["over_last"])
    arrive(*w["over_line"], *w["over"], *w["over_more"], *w["over_last"])
    whole_copy.wait()
    for copy in plan.made:
        copy.wait_send()


def gather_tokens(x, w, gain, cosine, sine, w_query, w_key, w_value, collective_id):
    rows, width = x.shape
    hbm = pl.BlockSpec(memory_space=pl.ANY)
    vmem = pl.BlockSpec(memory_space=pltpu.VMEM)
    out, packed, w_all = pl.pallas_call(
        tokens_kernel,
        out_shape=(
            jax.ShapeDtypeStruct((rows, 4 * width), x.dtype),
            jax.ShapeDtypeStruct((192, 1024), x.dtype),
            jax.ShapeDtypeStruct((4, 4, 2) + w.shape, w.dtype),
        ),
        in_specs=[vmem] * 5 + [hbm] * 3,
        out_specs=(hbm, vmem, hbm),
        scratch_shapes=[
            pltpu.VMEM((rows, 4 * width), x.dtype),
            pltpu.VMEM((rows, 4 * width), x.dtype),
            pltpu.VMEM(w_query.shape, x.dtype),
            pltpu.VMEM(w_key.shape, x.dtype),
            pltpu.VMEM(w_value.shape, x.dtype),
            pltpu.SemaphoreType.DMA((6,)),
            pltpu.SemaphoreType.DMA((40,)),
            pltpu.SemaphoreType.DMA((40,)),
        ],
        compiler_params=pltpu.CompilerParams(
            collective_id=collective_id, has_side_effects=True, vmem_limit_bytes=58 << 20
        ),
        cost_estimate=pl.CostEstimate(flops=1 << 30, bytes_accessed=40 << 20, transcendentals=0),
    )(x, w, gain[None], cosine, sine, w_query, w_key, w_value)
    return out, packed, w_all.reshape((32,) + w.shape)


def merge_stats(parts):
    top = parts[0][0]
    for m, _ in parts[1:]:
        top = jnp.maximum(top, m)
    weights = [jnp.exp2((m - top) * LOG2E) for m, _ in parts]
    total = weights[0] * parts[0][1]
    for w, (_, l) in zip(weights[1:], parts[1:]):
        total = total + w * l
    return weights, top, total


def blend(outs, weights, g):
    acc = outs[0].astype(jnp.float32) * weights[0][g : g + 1]
    for o, w in zip(outs[1:], weights[1:]):
        acc = acc + o.astype(jnp.float32) * w[g : g + 1]
    return acc


def merge_into(acc, accm, others, index, kv, picks):
    stat = lambda ref, i: (ref[i + (pl.ds(0, 4),)], ref[i + (pl.ds(4, 4),)])
    mine = index + (kv,)
    weights, top, total = merge_stats(
        [stat(accm, mine)] + [stat(m, pick) for (_, m), pick in zip(others, picks)]
    )
    accm[mine + (pl.ds(0, 4),)] = top
    accm[mine + (pl.ds(4, 4),)] = total
    for g in range(4):
        lanes = pl.ds(g * 256, 256)
        here = index + (pl.ds(kv * HD, HD), lanes)
        outs = [acc[here]] + [o[pick + (pl.ds(0, HD), lanes)] for (o, _), pick in zip(others, picks)]
        acc[here] = blend(outs, weights, g).astype(jnp.bfloat16)


def grp_merge_kernel(
    sent, o_ref, ml_ref, own_o_ref, own_ml_ref, out_ref,
    acc, accm, ra, ram, rb, rbm, r3, r3m, att, local_sems, send_sems, recv_sems,
):
    me, z, y, c = grid_place()
    yp, ym, yo = (y + 1) % 4, (y + 3) % 4, (y + 2) % 4
    zp, zm, zo = (z + 1) % 4, (z + 3) % 4, (z + 2) % 4
    dev = lambda zz, yy: zz * 8 + yy * 2 + c
    east, west, north, south = dev(z, yp), dev(z, ym), dev(zp, y), dev(zm, y)
    far_y, far_z = dev(z, yo), dev(zo, y)
    send = Sender("grp", send_sems, recv_sems)
    loads = [
        pltpu.make_async_copy(o_ref, acc, local_sems.at[0]),
        pltpu.make_async_copy(ml_ref, accm, local_sems.at[1]),
    ]
    for load in loads:
        load.start()
    x = lax.axis_index("tp")
    right, left = (x + 1) % 4, (x + 3) % 4
    greet(
        [("grp", i) for i in (east, west, north, south, far_y, far_z)]
        + [("tp", right), ("tp", left), ("tp", (x + 2) % 4)]
    )
    for load in loads:
        load.wait()
    lo, hi = pl.ds(0, 2), pl.ds(2, 2)
    ka, kb = pl.ds(0, HD), pl.ds(HD, HD)

    def ship_a(zs, yy, slot, device):
        return (
            send(acc.at[zs, yy, ka], ra.at[slot], device),
            send(accm.at[zs, yy, 0], ram.at[slot], device),
        )

    def ship_b(zz, ys, slot, device):
        return (
            send(acc.at[zz, ys, kb], rb.at[slot], device),
            send(accm.at[zz, ys, 1], rbm.at[slot], device),
        )

    def arrived(pair):
        pair[0].wait_recv()
        pair[1].wait_recv()

    axp = ship_a(lo, yo, 0, east)
    bxp = ship_b(zo, lo, 0, north)
    axm = ship_a(hi, yo, 1, west)
    bxm = ship_b(zo, hi, 1, south)
    app = ship_a(hi, yp, 2, east)
    bpp = ship_b(zp, hi, 2, north)
    apm = ship_a(lo, ym, 3, west)
    bpm = ship_b(zm, lo, 3, south)
    sent()

    def fold_a(base, yy, slots):
        def body(i, carry):
            merge_into(acc, accm, [(ra, ram)] * len(slots), (base + i, yy), 0, [(s, i) for s in slots])
            return carry

        lax.fori_loop(0, 2, body, 0)

    def fold_b(zz, base, slots):
        def body(i, carry):
            merge_into(acc, accm, [(rb, rbm)] * len(slots), (zz, base + i), 1, [(s, i) for s in slots])
            return carry

        lax.fori_loop(0, 2, body, 0)

    arrived(axp)
    fold_a(0, yp, [0])
    amp = ship_a(lo, yp, 4, east)
    arrived(bxp)
    fold_b(zp, 0, [0])
    bmp = ship_b(zp, lo, 4, north)
    arrived(axm)
    fold_a(2, ym, [1])
    amm = ship_a(hi, ym, 5, west)
    arrived(bxm)
    fold_b(zm, 2, [1])
    bmm = ship_b(zm, hi, 5, south)
    arrived(app)
    arrived(apm)
    arrived(bpp)
    arrived(bpm)
    arrived(amp)
    fold_a(0, y, [3, 4])
    arrived(amm)
    fold_a(2, y, [2, 5])
    arrived(bmp)
    fold_b(z, 0, [3, 4])
    arrived(bmm)
    fold_b(z, 2, [2, 5])

    last = []
    for slot, (zz, device) in enumerate(((zo, far_z), (zp, north), (zm, south))):
        last.append(send(acc.at[zz, y, ka], r3.at[0, slot], device))
        last.append(send(accm.at[zz, y, 0], r3m.at[0, slot], device))
    for slot, (yy, device) in enumerate(((yo, far_y), (yp, east), (ym, west))):
        last.append(send(acc.at[z, yy, kb], r3.at[1, slot], device))
        last.append(send(accm.at[z, yy, 1], r3m.at[1, slot], device))
    for copy in last:
        copy.wait_recv()
    for kv in range(2):
        stat = lambda ref, i: (ref[i + (pl.ds(0, 4),)], ref[i + (pl.ds(4, 4),)])
        parts = [stat(own_ml_ref, (kv,)), stat(accm, (z, y, kv))]
        parts += [stat(r3m, (kv, s)) for s in range(3)]
        weights, _, total = merge_stats(parts)
        scale = 1.0 / total
        weights = [w * scale for w in weights]
        rows = pl.ds(kv * HD, HD)
        for pair in range(2):
            heads = []
            for g in (2 * pair, 2 * pair + 1):
                lanes = pl.ds(g * 256, 256)
                outs = [own_o_ref[rows, lanes], acc[z, y, rows, lanes]]
                outs += [r3[kv, s, :, lanes] for s in range(3)]
                heads.append(blend(outs, weights, g))
            block = jnp.transpose(jnp.concatenate(heads, axis=0)).astype(jnp.bfloat16)
            att[:, pl.ds((kv * 2 + pair) * 128, 128)] = block
    rows, width = att.shape
    cols = lambda i: pl.ds(pl.multiple_of(i * width, width), width)
    upper, lower = pl.ds(0, rows // 2), pl.ds(rows // 2, rows // 2)
    own = pltpu.make_async_copy(att, out_ref.at[:, cols(x)], local_sems.at[5])
    own.start()
    p = send(att, out_ref.at[:, cols(x)], right, "tp")
    m = send(att, out_ref.at[:, cols(x)], left, "tp")
    p.wait_recv()
    ref = out_ref.at[upper, cols(left)]
    fp = send(ref, ref, right, "tp")
    m.wait_recv()
    ref = out_ref.at[lower, cols(right)]
    fm = send(ref, ref, left, "tp")
    fp.wait_recv()
    fm.wait_recv()
    own.wait()
    send.finish()


def tail_kernel(
    make_attended, att_ref, tok_ref, gain_ref, wo_ref, w_ref, wd_ref, out_ref,
    wo, wb, wd, acc, firsts, n2, gate, up, hid, mine, outbox, inbox, load_sems, send_sems, recv_sems,
):
    me = lax.axis_index("tp")
    right, left, facing = (me + 1) % 4, (me + 3) % 4, (me + 2) % 4
    send = Sender("tp", send_sems, recv_sems)
    wo_part = lambda i: pltpu.make_async_copy(
        wo_ref.at[pl.ds(i * 512, 512)], wo.at[pl.ds(i * 512, 512)], load_sems.at[i]
    )
    w_part = lambda i: pltpu.make_async_copy(
        w_ref.at[pl.ds(i * 4, 4)], wb.at[pl.ds(i * 4, 4)], load_sems.at[4 + i]
    )
    down = pltpu.make_async_copy(wd_ref, wd, load_sems.at[12])

    def start_loads():
        for i in range(4):
            wo_part(i).start()
        for i in range(8):
            w_part(i).start()
        down.start()

    make_attended(start_loads)
    f32, bf = jnp.float32, jnp.bfloat16
    acc[...] = tok_ref[...].astype(f32)
    for i in range(4):
        wo_part(i).wait()

        def project(n, carry, i=i):
            lanes = pl.ds(pl.multiple_of(n * 512, 512), 512)
            acc[:, lanes] += jnp.dot(
                att_ref[:, i * 512 : (i + 1) * 512],
                wo[i * 512 : (i + 1) * 512, lanes],
                preferred_element_type=f32,
            )
            return carry

        lax.fori_loop(0, 4, project, 0)

    def norm(i, carry):
        rows = pl.ds(pl.multiple_of(i * 32, 32), 32)
        first = acc[rows].astype(bf)
        firsts[rows] = first
        n2[rows] = rms_scale(first, gain_ref[...]).astype(bf)
        return carry

    lax.fori_loop(0, NEW_TOK // 32, norm, 0)
    gate[...] = jnp.zeros_like(gate)
    up[...] = jnp.zeros_like(up)
    for i in range(8):
        w_part(i).wait()

        def widen(n, carry, i=i):
            lanes = pl.ds(pl.multiple_of(n * 512, 512), 512)
            x = n2[:, i * 256 : (i + 1) * 256]
            for total, at in ((gate, 0), (up, 64)):
                w = wb[4 * i : 4 * i + 4, at : at + 64, lanes].reshape(256, 512)
                total[:, lanes] += jnp.dot(x, w, preferred_element_type=f32)
            return carry

        lax.fori_loop(0, 2, widen, 0)

    def squash(i, carry):
        rows = pl.ds(pl.multiple_of(i * 32, 32), 32)
        v = gate[rows]
        hid[rows] = (v / (1.0 + jnp.exp(-v)) * up[rows]).astype(bf)
        return carry

    lax.fori_loop(0, NEW_TOK // 32, squash, 0)

    down.wait()

    def terms(target):
        w = wd[pl.ds(target * 8, 8)].reshape(512, 1024)
        return lax.dot_general(
            hid[...], w, (((1,), (1,)), ((), ())), preferred_element_type=f32
        )

    for slot, target in enumerate((facing, right, left)):
        outbox[slot] = terms(target).astype(bf)
        send(outbox.at[slot], inbox.at[slot], target)
    cols = pl.ds(pl.multiple_of(me * 512, 512), 512)
    mine[...] = firsts[:, cols].astype(f32) + terms(me)
    for copy in send.started:
        copy.wait_recv()
    for slot in range(3):
        mine[...] += inbox[slot].astype(f32)
    out_ref[...] = mine[...]
    send.finish()


MERGE_SCRATCH = 12


def back_kernel(o_ref, ml_ref, own_o_ref, own_ml_ref, tok_ref, gain_ref, wo_ref, w_ref, wd_ref, out_ref, att, *rest):
    merge = lambda sent: grp_merge_kernel(
        sent, o_ref, ml_ref, own_o_ref, own_ml_ref, att, *rest[:MERGE_SCRATCH]
    )
    tail_kernel(
        merge, att, tok_ref, gain_ref, wo_ref, w_ref, wd_ref, out_ref, *rest[MERGE_SCRATCH:]
    )


def back(parts, whole, gain, w_out, weights, down_rows, collective_id):
    bf, f32 = jnp.bfloat16, jnp.float32
    vmem = pl.BlockSpec(memory_space=pltpu.VMEM)
    hbm = pl.BlockSpec(memory_space=pl.ANY)
    rows, width = whole.shape
    copies = 24 + 12 + 4
    merge_scratch = [
        pltpu.VMEM((4, 4, 128, 1024), bf),
        pltpu.VMEM((4, 4, 2, 8, 256), f32),
        pltpu.VMEM((6, 2, HD, 1024), bf),
        pltpu.VMEM((6, 2, 8, 256), f32),
        pltpu.VMEM((6, 2, HD, 1024), bf),
        pltpu.VMEM((6, 2, 8, 256), f32),
        pltpu.VMEM((2, 3, HD, 1024), bf),
        pltpu.VMEM((2, 3, 8, 256), f32),
        pltpu.VMEM((NEW_TOK, 512), bf),
        pltpu.SemaphoreType.DMA((6,)),
        pltpu.SemaphoreType.DMA((copies,)),
        pltpu.SemaphoreType.DMA((copies,)),
    ]
    assert len(merge_scratch) == MERGE_SCRATCH
    return pl.pallas_call(
        back_kernel,
        out_shape=jax.ShapeDtypeStruct((rows, width // 4), f32),
        in_specs=[hbm, hbm, vmem, vmem, vmem, vmem, hbm, hbm, hbm],
        out_specs=vmem,
        scratch_shapes=[
            pltpu.VMEM((rows, width), bf),
            *merge_scratch,
            pltpu.VMEM(w_out.shape, bf),
            pltpu.VMEM(weights.shape, bf),
            pltpu.VMEM(down_rows.shape, bf),
            pltpu.VMEM((rows, width), f32),
            pltpu.VMEM((rows, width), bf),
            pltpu.VMEM((rows, width), bf),
            pltpu.VMEM((rows, 1024), f32),
            pltpu.VMEM((rows, 1024), f32),
            pltpu.VMEM((rows, 1024), bf),
            pltpu.VMEM((rows, 512), f32),
            pltpu.VMEM((3, rows, 512), bf),
            pltpu.VMEM((3, rows, 512), bf),
            pltpu.SemaphoreType.DMA((13,)),
            pltpu.SemaphoreType.DMA((3,)),
            pltpu.SemaphoreType.DMA((3,)),
        ],
        compiler_params=pltpu.CompilerParams(
            collective_id=collective_id, has_side_effects=True, vmem_limit_bytes=60 << 20
        ),
        cost_estimate=pl.CostEstimate(
            flops=5 << 30, bytes_accessed=130 << 20, transcendentals=1 << 18
        ),
    )(*parts, whole, gain[None], w_out, weights, down_rows)


def shards(
    tokens,
    attn_gain,
    w_query,
    w_key,
    w_value,
    w_out,
    mlp_gain,
    w_gate,
    w_up,
    w_down,
    k_cache,
    v_cache,
    prefix_len,
):
    group = lax.axis_index("grp")
    slice_len = k_cache.shape[1]
    start = group * slice_len
    own_len = lax.dynamic_slice_in_dim(prefix_len, group, 1)[0]
    positions = (own_len + jnp.arange(NEW_TOK, dtype=jnp.int32)).astype(jnp.float32)
    inverse = ROPE_BASE ** (-2.0 * jnp.arange(HD // 2, dtype=jnp.float32) / HD)
    angles = positions[None, :] * inverse[:, None]
    cosine, sine = jnp.cos(angles), jnp.sin(angles)
    whole, packed, down_rows = gather_tokens(
        tokens, w_down.T, attn_gain, cosine, sine, w_query, w_key, w_value, 0
    )
    parts, new_rows, whole_out, weights = front(
        prefix_len, packed, w_out, w_gate, w_up, k_cache, v_cache, 1
    )
    k_next, v_next = place_new(start[None], prefix_len, new_rows, k_cache, v_cache)
    result = back(parts, whole, mlp_gain, whole_out, weights, down_rows, 2)
    return (result, k_next, v_next)


def solution(mesh):
    placed = (
        P("grp", "tp"),
        P(),
        P(None, "tp"),
        P(None, "tp"),
        P(None, "tp"),
        P("tp", None),
        P(),
        P("grp", "tp"),
        P("grp", "tp"),
        P("tp", "grp"),
        P(None, "grp", "tp"),
        P(None, "grp", "tp"),
        P(),
    )
    return jax.shard_map(
        shards,
        mesh=mesh,
        in_specs=placed,
        out_specs=(P("grp", "tp"), P(None, "grp", "tp"), P(None, "grp", "tp")),
        check_vma=False,
    )
```
